32 devices in a mesh: dp: 16 (over z, x, core), tensor: 2 (over y).
Axes of the slice: x: 2, y: 2, z: 4, core: 2. Of those that a mesh axis runs over, the one named last changes fastest.
Arguments:
- hidden_in: bfloat16 [12288, 2048], P(('dp', 'tensor')), may hold values from -6 to 6
- per_layer_input: bfloat16 [12288, 256], P(('dp', 'tensor')), may hold values from -6 to 6
- out_grad: bfloat16 [12288, 2048], P(('dp', 'tensor')), may hold values from -6 to 6
- adapter_ids: int32 [16], P('dp'), may hold values from 0 to 7
- weight_qkv: bfloat16 [2048, 2, 1536], P('dp', 'tensor'), may hold values from -0.125 to 0.125
- weight_attn_out: bfloat16 [2048, 2048], P('tensor', 'dp'), may hold values from -0.125 to 0.125
- weight_gate_up: bfloat16 [2048, 2, 8192], P('dp', None, 'tensor'), may hold values from -0.125 to 0.125
- weight_down: bfloat16 [8192, 2048], P('tensor', 'dp'), may hold values from -0.0625 to 0.0625
- laurel_left: bfloat16 [2048, 64], P('dp'), may hold values from -0.125 to 0.125
- laurel_right: bfloat16 [64, 2048], P(None, 'dp'), may hold values from -0.75 to 0.75
- per_layer_gate: bfloat16 [2048, 256], P('dp'), may hold values from -0.125 to 0.125
- per_layer_proj: bfloat16 [256, 2048], P(None, 'dp'), may hold values from -0.375 to 0.375
- norm_gains: float32 [6, 2048], replicated, may hold values from 0.1 to 1.9
- head_gains: float32 [2, 256], replicated, may hold values from 0.1 to 1.9
- adapter_qkv_in: bfloat16 [8, 2048, 48], replicated, may hold values from -0.125 to 0.125
- adapter_qkv_out: bfloat16 [8, 16, 2, 1536], P(None, None, 'tensor'), may hold values from -0.75 to 0.75
- adapter_attn_in: bfloat16 [8, 2048, 16], P(None, 'tensor'), may hold values from -0.125 to 0.125
- adapter_attn_out: bfloat16 [8, 16, 2048], replicated, may hold values from -0.75 to 0.75
- adapter_ffn_in: bfloat16 [8, 2048, 32], replicated, may hold values from -0.125 to 0.125
- adapter_ffn_out: bfloat16 [8, 16, 2, 8192], P(None, None, None, 'tensor'), may hold values from -0.75 to 0.75
- adapter_down_in: bfloat16 [8, 8192, 16], P(None, 'tensor'), may hold values from -0.0625 to 0.0625
- adapter_down_out: bfloat16 [8, 16, 2048], replicated, may hold values from -0.75 to 0.75
Outputs:
- layer_out: bfloat16 [12288, 2048], P(('dp', 'tensor'))
- input_grad: float32 [12288, 2048], P(('dp', 'tensor'))
- grad_qkv_in: float32 [8, 2048, 48], P(None, ('dp', 'tensor'))
- grad_qkv_out: float32 [8, 16, 2, 1536], P(None, None, 'tensor')
- grad_attn_in: float32 [8, 2048, 16], P(None, 'tensor')
- grad_attn_out: float32 [8, 16, 2048], P(None, None, ('dp', 'tensor'))
- grad_ffn_in: float32 [8, 2048, 32], P(None, ('dp', 'tensor'))
- grad_ffn_out: float32 [8, 16, 2, 8192], P(None, None, None, 'tensor')
- grad_down_in: float32 [8, 8192, 16], P(None, 'tensor')
- grad_down_out: float32 [8, 16, 2048], P(None, None, ('dp', 'tensor'))
The draws below stay inside these ranges and needn't reach their ends.
Inputs may be any that keep to these rules, and one draw needn't show every extreme that they name: `adapter_ids`: the adapter that each sequence uses.
All inputs are finite; a program needn't handle non-finite values.
Results may differ from the reference program's by a relative error of at most 0.018.
Values may be sent and summed in bfloat16 or wider, within the bound.
A program may use at most 320 MiB of HBM per device.

```python
import jax
import jax.numpy as jnp
from jax import lax

D = 2048
HEADS = 8
KV = 2
HD = 256
FEED_UNITS = 8192
LR = 64
PD = 256
WIN = 512
BLK = 256
ADAPTERS = 8
ADAPTER_RANK = 16
SEQ_LEN = 768
SEQS = 16
TOKENS = 12288


def touch_ends(entries, rng, low, top_value):
    shape = entries.shape
    spot = [jax.random.randint(jax.random.fold_in(rng, axis), (), 0, shape[axis]) for axis in range(len(shape))]
    entries = entries.at[tuple(spot)].set(low)
    longest = shape.index(max(shape))
    spot[longest] = (spot[longest] + 1) % shape[longest]
    return entries.at[tuple(spot)].set(top_value)


def block_levels(own_key, shape, split, smallest, top_value):
    level = 1.0
    for dim, shards_of in split:
        steps = jax.random.uniform(jax.random.fold_in(jax.random.fold_in(own_key, 6), dim), (shards_of,), jnp.float32, smallest / len(split), top_value / len(split))
        level = level * jnp.repeat(jnp.exp(steps), shape[dim] // shards_of).reshape((-1,) + (1,) * (len(shape) - 1 - dim))
    return level


def centred(rng, shape, deviation, limit, split=(), kind=jnp.bfloat16):
    level = block_levels(rng, shape, split, -0.22, 0.18) if split else 1.0
    values = jax.random.normal(rng, shape, jnp.float32) * deviation * level
    return jnp.minimum(jnp.maximum(values, -limit), limit).astype(kind)


def setup_inputs(seed: int = 0) -> dict:
    streams_of = jax.random.split(jax.random.key(seed), 23)
    hidden_in = centred(streams_of[0], (TOKENS, D), 1.0, 6.0, ((0, 32),))
    per_layer_input = centred(streams_of[1], (TOKENS, PD), 1.0, 6.0, ((0, 32),))
    out_grad = centred(streams_of[2], (TOKENS, D), 1.0, 6.0, ((0, 32),))
    adapter_ids = touch_ends(jax.random.randint(streams_of[3], (SEQS,), 0, ADAPTERS), jax.random.fold_in(streams_of[3], 1), 0, ADAPTERS - 1).astype(jnp.int32)
    weight_qkv = centred(streams_of[4], (D, KV, (HEADS // KV + 2) * HD), D ** -0.5, 0.125, ((0, 16), (1, 2)))
    weight_attn_out = centred(streams_of[5], (HEADS * HD, D), (HEADS * HD) ** -0.5, 0.125, ((0, 2), (1, 16)))
    weight_gate_up = centred(streams_of[6], (D, 2, FEED_UNITS), D ** -0.5, 0.125, ((0, 16), (2, 2)))
    weight_down = centred(streams_of[7], (FEED_UNITS, D), FEED_UNITS ** -0.5, 0.0625, ((0, 2), (1, 16)))
    laurel_left = centred(streams_of[8], (D, LR), D ** -0.5, 0.125, ((0, 16),))
    laurel_right = centred(streams_of[9], (LR, D), LR ** -0.5, 0.75, ((1, 16),))
    per_layer_gate = centred(streams_of[10], (D, PD), D ** -0.5, 0.125, ((0, 16),))
    per_layer_proj = centred(streams_of[11], (PD, D), PD ** -0.5, 0.375, ((1, 16),))
    norm_gains = jnp.clip(1.0 + 0.18 * jax.random.normal(streams_of[12], (6, D), jnp.float32), 0.1, 1.9)
    head_gains = jnp.clip(1.0 + 0.18 * jax.random.normal(streams_of[13], (2, HD), jnp.float32), 0.1, 1.9)
    adapter_qkv_in = centred(streams_of[14], (ADAPTERS, D, 3 * ADAPTER_RANK), D ** -0.5, 0.125)
    adapter_qkv_out = centred(streams_of[15], (ADAPTERS, ADAPTER_RANK, KV, (HEADS // KV + 2) * HD), (4 * ADAPTER_RANK) ** -0.5, 0.75, ((2, 2),))
    adapter_attn_in = centred(streams_of[16], (ADAPTERS, HEADS * HD, ADAPTER_RANK), (HEADS * HD) ** -0.5, 0.125, ((1, 2),))
    adapter_attn_out = centred(streams_of[17], (ADAPTERS, ADAPTER_RANK, D), (4 * ADAPTER_RANK) ** -0.5, 0.75)
    adapter_ffn_in = centred(streams_of[18], (ADAPTERS, D, 2 * ADAPTER_RANK), D ** -0.5, 0.125)
    adapter_ffn_out = centred(streams_of[19], (ADAPTERS, ADAPTER_RANK, 2, FEED_UNITS), (4 * ADAPTER_RANK) ** -0.5, 0.75, ((3, 2),))
    adapter_down_in = centred(streams_of[20], (ADAPTERS, FEED_UNITS, ADAPTER_RANK), FEED_UNITS ** -0.5, 0.0625, ((1, 2),))
    adapter_down_out = centred(streams_of[21], (ADAPTERS, ADAPTER_RANK, D), (4 * ADAPTER_RANK) ** -0.5, 0.75)
    return {"hidden_in": hidden_in, "per_layer_input": per_layer_input, "out_grad": out_grad, "adapter_ids": adapter_ids, "weight_qkv": weight_qkv, "weight_attn_out": weight_attn_out, "weight_gate_up": weight_gate_up, "weight_down": weight_down, "laurel_left": laurel_left, "laurel_right": laurel_right, "per_layer_gate": per_layer_gate, "per_layer_proj": per_layer_proj, "norm_gains": norm_gains, "head_gains": head_gains, "adapter_qkv_in": adapter_qkv_in, "adapter_qkv_out": adapter_qkv_out, "adapter_attn_in": adapter_attn_in, "adapter_attn_out": adapter_attn_out, "adapter_ffn_in": adapter_ffn_in, "adapter_ffn_out": adapter_ffn_out, "adapter_down_in": adapter_down_in, "adapter_down_out": adapter_down_out}


NORM_EPSILON = 1e-06
ADAPTER_SCALE = 2.0
RSQRT_TWO = 0.7071067811865476
ROPE_BASE = 10000.0
NEG_BIG = -1e+30

@jax.custom_vjp
def low(v):
    return lax.optimization_barrier(v.astype(jnp.bfloat16)).astype(jnp.float32)

@jax.custom_vjp
def adapter_backward(v):
    return v

def low_keep(v):
    return (low(v), None)

def low_pass(kept, grad):
    return (grad,)

def back_keep(v):
    return (v, None)

def back_low(kept, grad):
    return (low(grad),)
low.defvjp(low_keep, low_pass)
adapter_backward.defvjp(back_keep, back_low)

def normed(values, gains):
    return values * lax.rsqrt(lax.optimization_barrier(jnp.mean(values * values, axis=-1, keepdims=True)) + NORM_EPSILON) * gains

def product_result(left_side, right_side):
    return jnp.dot(left_side, right_side, precision=lax.Precision.HIGHEST)

def rotary(values, positions):
    half_dim = values.shape[-1] // 2
    inverse = ROPE_BASE ** (-jnp.arange(half_dim, dtype=jnp.float32) / half_dim)
    angles = positions[:, None] * inverse[None, :]
    angles = angles.reshape((positions.shape[0],) + (1,) * (values.ndim - 2) + (half_dim,))
    cosines = jnp.cos(angles)
    sinusoid = jnp.sin(angles)
    leading = values[..., :half_dim]
    trailing = values[..., half_dim:]
    return jnp.concatenate([leading * cosines - trailing * sinusoid, trailing * cosines + leading * sinusoid], axis=-1)

def window_mask(length):
    blocks = jnp.arange(length) // BLK
    distance = blocks[:, None] - blocks[None, :]
    return (distance >= 0) & (distance < WIN // BLK)

def attend(queries, keys, values):
    length = queries.shape[0]
    scores = jnp.einsum('lgqd,mgd->gqlm', queries, keys, precision=lax.Precision.HIGHEST) * HD ** (-0.5)
    scores = adapter_backward(scores)
    scores = jnp.where(window_mask(length)[None, None], scores, NEG_BIG)
    attn_probs = low(jax.nn.softmax(scores, axis=-1))
    return jnp.einsum('gqlm,mgd->lgqd', attn_probs, values, precision=lax.Precision.HIGHEST)

def layer_forward(x_seq, ple_seq, weights, adapters, selected_adapter):
    w_qkv, attention_weight, w_gate_up, down_weight, l_left, l_right, p_gate, p_proj, gains_model, gains_head = weights
    a_qkv_in, a_qkv_out, attention_down_factor, attention_up_factor, a_ffn_in, a_ffn_out, down_input_factor, down_output_factor = adapters
    length = x_seq.shape[0]
    per_group = HEADS // KV
    q_cols = per_group * HD
    x_norm = normed(x_seq, gains_model[0])
    h_low = low(x_norm)
    query_key_value_unrotated = product_result(h_low, w_qkv.reshape(D, KV * (per_group + 2) * HD)).reshape(length, KV, (per_group + 2) * HD)
    u_qkv = product_result(h_low, a_qkv_in[selected_adapter])
    b_qkv = a_qkv_out[selected_adapter]
    query_adapter_delta = product_result(u_qkv[:, :ADAPTER_RANK], b_qkv[:, :, :q_cols].reshape(ADAPTER_RANK, -1)).reshape(length, KV, q_cols)
    key_adapter_delta = product_result(u_qkv[:, ADAPTER_RANK:2 * ADAPTER_RANK], b_qkv[:, :, q_cols:q_cols + HD].reshape(ADAPTER_RANK, -1)).reshape(length, KV, HD)
    value_adapter_delta = product_result(u_qkv[:, 2 * ADAPTER_RANK:], b_qkv[:, :, q_cols + HD:].reshape(ADAPTER_RANK, -1)).reshape(length, KV, HD)
    query_key_value_unrotated = adapter_backward(query_key_value_unrotated + ADAPTER_SCALE * jnp.concatenate([query_adapter_delta, key_adapter_delta, value_adapter_delta], axis=2))
    positions = jnp.arange(length, dtype=jnp.float32)
    queries = query_key_value_unrotated[:, :, :q_cols].reshape(length, KV, per_group, HD)
    queries = low(rotary(normed(queries, gains_head[0]), positions))
    keys = low(rotary(normed(query_key_value_unrotated[:, :, q_cols:q_cols + HD], gains_head[1]), positions))
    values = low(query_key_value_unrotated[:, :, q_cols + HD:])
    context_rows = jax.checkpoint(attend)(queries, keys, values)
    context_rows = low(adapter_backward(context_rows.reshape(length, HEADS * HD)))
    attention_projected = product_result(context_rows, attention_weight) + ADAPTER_SCALE * product_result(product_result(context_rows, attention_down_factor[selected_adapter]), attention_up_factor[selected_adapter])
    attention_projected = adapter_backward(attention_projected)
    laurel_low = low(adapter_backward(product_result(h_low, l_left)))
    laurel_wide = adapter_backward(product_result(laurel_low, l_right))
    laurel_out = x_norm + normed(laurel_wide, gains_model[2])
    combined = (x_seq + normed(attention_projected, gains_model[1]) + laurel_out) * RSQRT_TWO
    h_second = low(normed(combined, gains_model[3]))
    gate_up_matrix = product_result(h_second, w_gate_up.reshape(D, 2 * FEED_UNITS))
    feed_update = product_result(h_second, a_ffn_in[selected_adapter])
    feed_bias_factor = a_ffn_out[selected_adapter]
    gate_preactivation = adapter_backward(gate_up_matrix[:, :FEED_UNITS] + ADAPTER_SCALE * product_result(feed_update[:, :ADAPTER_RANK], feed_bias_factor[:, 0]))
    up_preactivation = adapter_backward(gate_up_matrix[:, FEED_UNITS:] + ADAPTER_SCALE * product_result(feed_update[:, ADAPTER_RANK:], feed_bias_factor[:, 1]))
    hidden_state = low(jax.nn.gelu(gate_preactivation, approximate=True) * up_preactivation)
    feed_projected = product_result(hidden_state, down_weight) + ADAPTER_SCALE * product_result(product_result(hidden_state, down_input_factor[selected_adapter]), down_output_factor[selected_adapter])
    feed_projected = adapter_backward(feed_projected)
    y_first = combined + normed(feed_projected, gains_model[4])
    ple_pre = adapter_backward(product_result(low(y_first), p_gate))
    ple_hidden = low(jax.nn.gelu(ple_pre, approximate=True) * ple_seq)
    ple_wide = adapter_backward(product_result(ple_hidden, p_proj))
    return y_first + normed(ple_wide, gains_model[5])

def reference(hidden_in, per_layer_input, out_grad, adapter_ids, weight_qkv, weight_attn_out, weight_gate_up, weight_down, laurel_left, laurel_right, per_layer_gate, per_layer_proj, norm_gains, head_gains, adapter_qkv_in, adapter_qkv_out, adapter_attn_in, adapter_attn_out, adapter_ffn_in, adapter_ffn_out, adapter_down_in, adapter_down_out):
    weights = tuple((item.astype(jnp.float32) for item in (weight_qkv, weight_attn_out, weight_gate_up, weight_down, laurel_left, laurel_right, per_layer_gate, per_layer_proj, norm_gains, head_gains)))
    adapters = tuple((item.astype(jnp.float32) for item in (adapter_qkv_in, adapter_qkv_out, adapter_attn_in, adapter_attn_out, adapter_ffn_in, adapter_ffn_out, adapter_down_in, adapter_down_out)))
    x_all = hidden_in.astype(jnp.float32).reshape(SEQS, SEQ_LEN, D)
    ple_all = per_layer_input.astype(jnp.float32).reshape(SEQS, SEQ_LEN, PD)
    grad_all = out_grad.astype(jnp.float32).reshape(SEQS, SEQ_LEN, D)

    def per_sequence(totals, sequence_data):
        x_seq, ple_seq, grad_seq, selected_adapter = sequence_data

        def forward(x_value, adapter_values):
            return layer_forward(x_value, ple_seq, weights, adapter_values, selected_adapter)
        result, pullback = jax.vjp(forward, x_seq, adapters)
        x_grad, adapter_grads = pullback(grad_seq)
        totals = jax.tree.map(jnp.add, totals, adapter_grads)
        return (totals, (result.astype(jnp.bfloat16), x_grad))
    initial = jax.tree.map(jnp.zeros_like, adapters)
    totals, (results, x_grads) = lax.scan(per_sequence, initial, (x_all, ple_all, grad_all, adapter_ids))
    return (results.reshape(TOKENS, D), x_grads.reshape(TOKENS, D), totals[0], totals[1], totals[2], totals[3], totals[4], totals[5], totals[6], totals[7])
```

```python
import functools

import jax
import jax.numpy as jnp
from jax import lax
from jax.experimental import pallas as pl
from jax.experimental.pallas import tpu as pltpu
from jax.sharding import PartitionSpec as P

HEADS = 8
KV = 2
HD = 256
WIN = 512
BLK = 256
RANK = 16
UB = 512
FB = 3 * UB

NORM_EPSILON = 1e-06
RSQRT_TWO = 0.7071067811865476
ROPE_BASE = 10000.0
NEG_BIG = -1e30
GELU_A = 0.7978845608028654
GELU_B = 0.044715

F32 = jnp.float32
BF16 = jnp.bfloat16
VMEM_LIMIT = 58 * 1024 * 1024


def dot(a, b):
    return lax.dot_general(a, b, (((1,), (0,)), ((), ())), preferred_element_type=F32)


def dot_nt(a, b):
    return lax.dot_general(a, b, (((1,), (1,)), ((), ())), preferred_element_type=F32)


def dot_tn(a, b):
    return lax.dot_general(a, b, (((0,), (0,)), ((), ())), preferred_element_type=F32)


def inv_rms(v):
    return lax.rsqrt(jnp.mean(v * v, axis=-1, keepdims=True) + NORM_EPSILON)


def normed(v, gains):
    return v * inv_rms(v) * gains


def norm_back(v, gains, cotangent):
    r = inv_rms(v)
    gc = gains * cotangent
    return r * gc - v * (r * r * r * jnp.mean(v * gc, axis=-1, keepdims=True))


def gelu_tanh(v):
    return 0.5 * v * (1.0 + jnp.tanh(GELU_A * (v + GELU_B * v * v * v)))


def gelu_both(v):
    v2 = v * v
    th = jnp.tanh(GELU_A * v * (1.0 + GELU_B * v2))
    half = 0.5 * (1.0 + th)
    slope = half + 0.5 * v * (1.0 - th * th) * (GELU_A * (1.0 + 3.0 * GELU_B * v2))
    return v * half, slope


def const_spec(shape):
    return pl.BlockSpec(shape, lambda *_: (0,) * len(shape), pipeline_mode=pl.Buffered(1))


def any_spec():
    return pl.BlockSpec(memory_space=pl.ANY)


def params():
    return pltpu.CompilerParams(vmem_limit_bytes=VMEM_LIMIT)


def pack_blocks(gate_up, down, first, count, rest, cols, name):
    rows = gate_up.shape[0]
    widths = [n for _, n in rest]

    def body(gu_ref, down_ref, *refs):
        out = refs[-1]
        for b in range(count):
            cs = slice(b * UB, (b + 1) * UB)
            out[:, b * FB : b * FB + UB] = gu_ref[:, 0, cs]
            out[:, b * FB + UB : b * FB + 2 * UB] = gu_ref[:, 1, cs]
            out[:, b * FB + 2 * UB : (b + 1) * FB] = down_ref[cs, :].T
        at = count * FB
        for ref, (value, n) in zip(refs[:-1], rest):
            if value.ndim == 3:
                out[:, at : at + n] = ref[:, 0, :]
            elif value.shape[0] == rows and value.shape[1] == n:
                out[:, at : at + n] = ref[...]
            else:
                out[:, at : at + n] = ref[...].T
            at += n

    lo = first * UB
    return pl.pallas_call(
        body,
        grid=(1,),
        in_specs=[
            pl.BlockSpec((pl.Element(rows), pl.Element(2), pl.Element(count * UB)), lambda i: (0, 0, lo)),
            pl.BlockSpec((pl.Element(count * UB), pl.Element(rows)), lambda i: (lo, 0)),
        ]
        + [const_spec(v.shape) for v, _ in rest],
        out_specs=const_spec((rows, count * FB + sum(widths))),
        out_shape=jax.ShapeDtypeStruct((rows, count * FB + sum(widths)), BF16),
        compiler_params=params(),
        name=name,
    )(gate_up, down, *[v for v, _ in rest])


def ffn_fwd(h2, packed, blocks, first, u_low, bgu, ad_t, bd, prev, last):
    rows, width = h2.shape
    units = ad_t.shape[1]
    stream = last is not None
    r = rows // 2 if stream else rows
    rb = last if stream else 0
    half = r // 2
    tile = rows // 2
    sub = 256

    def body(*refs):
        h_ref, w_ref, ul_ref, bgu_ref, ad_ref, bd_ref = refs[:6]
        at = 6
        if prev is not None:
            acc_in, ud_in = refs[6:8]
            at = 10
        outs = refs[at:]
        if stream:
            g_out, u_out, own_out, peer_out, ud_out, acc, ud, hs = outs
        else:
            g_out, u_out, acc_out, ud_out, acc, ud, hs = outs
        j = pl.program_id(0)

        @pl.when(j == 0)
        def _():
            if prev is None:
                acc[...] = jnp.zeros_like(acc)
                ud[...] = jnp.zeros_like(ud)
            else:
                acc[...] = acc_in[...]
                ud[...] = ud_in[...]

        for k in range(r // tile):
            at_rows = slice(k * tile, (k + 1) * tile)
            h = h_ref[at_rows, :]
            ul = ul_ref[at_rows, :]
            for n in range(UB // sub):
                cs = slice(n * sub, (n + 1) * sub)
                us = slice(UB + n * sub, UB + (n + 1) * sub)
                g = dot(h, w_ref[:, cs]) + dot(ul, bgu_ref[:, cs])
                u = dot(h, w_ref[:, us]) + dot(ul, bgu_ref[:, us])
                g_out[at_rows, cs] = g.astype(BF16)
                u_out[at_rows, cs] = u.astype(BF16)
                hs[at_rows, cs] = (gelu_tanh(g) * u).astype(BF16)
            hidden = hs[at_rows, :]
            for c in range(width // 512):
                cc = slice(c * 512, (c + 1) * 512)
                acc[at_rows, cc] += dot_nt(hidden, w_ref[cc, 2 * UB : 3 * UB])
            ud[at_rows, :] += dot_nt(hidden, ad_ref[...])

        @pl.when(j == blocks - 1)
        def _():
            ud_out[...] = ud[...]
            if stream:
                total = acc[...] + dot(ud[...].astype(BF16), bd_ref[...])
                own_out[...] = total[:half]
                peer_out[...] = total[half:].astype(BF16)
            else:
                acc_out[...] = acc[...]

    row_const = lambda n: pl.BlockSpec((r, n), lambda j: (rb, 0), pipeline_mode=pl.Buffered(1))
    in_specs = [
        row_const(width),
        pl.BlockSpec((width, FB), lambda j: (0, j)),
        row_const(2 * RANK),
        pl.BlockSpec((2 * RANK, 2 * UB), lambda j: (0, first + j)),
        pl.BlockSpec((RANK, UB), lambda j: (0, first + j)),
        const_spec((RANK, width)),
    ]
    args = [h2, packed, u_low, bgu, ad_t, bd]
    aliases = {}
    if prev is not None:
        acc_prev, ud_prev, g_prev, u_prev = prev
        in_specs += [row_const(width), row_const(RANK), any_spec(), any_spec()]
        args += [acc_prev, ud_prev, g_prev, u_prev]
        aliases = {8: 0, 9: 1}
    pre_spec = pl.BlockSpec((r, UB), lambda j: (rb, first + j))
    out_specs = [pre_spec, pre_spec]
    shape = jax.ShapeDtypeStruct
    out_shape = [shape((rows, units), BF16)] * 2
    if stream:
        out_specs += [const_spec((half, width)), const_spec((half, width)), const_spec((r, RANK))]
        out_shape += [
            shape((half, width), F32),
            shape((half, width), BF16),
            shape((r, RANK), F32),
        ]
    else:
        out_specs += [const_spec((r, width)), const_spec((r, RANK))]
        out_shape += [shape((r, width), F32), shape((r, RANK), F32)]
    return pl.pallas_call(
        body,
        grid=(blocks,),
        in_specs=in_specs,
        out_specs=out_specs,
        out_shape=out_shape,
        scratch_shapes=[
            pltpu.VMEM((r, width), F32),
            pltpu.VMEM((r, RANK), F32),
            pltpu.VMEM((r, UB), BF16),
        ],
        input_output_aliases=aliases,
        compiler_params=params(),
        cost_estimate=pl.CostEstimate(
            flops=6 * r * width * UB * blocks,
            bytes_accessed=2 * width * FB * blocks + 8 * r * width,
            transcendentals=r * UB * blocks,
        ),
        name="ffn_fwd",
    )(*args)


def ffn_bwd(own, peer, packs, counts, g_pre, u_pre, bgu, ad_t, bd, u_t, a_in_t, rb):
    half, width = own.shape
    r = 2 * half
    units = ad_t.shape[1]
    blocks = units // UB

    def body(
        own_ref, peer_ref, p0, p1, p2, g_ref, u_ref, bgu_ref, ad_ref, bd_ref, ut_ref,
        ain_ref, own_out, peer_out, dbg_out, dbu_out, gad_out, du_out,
        df, acc, wbuf, dd, du, dgu, hs, sem,
    ):
        j = pl.program_id(0)
        slot = lax.rem(j, 2)

        def fetch(step, where):
            base = 0
            for ref, count in zip((p0, p1, p2), counts):
                low = base

                @pl.when((step >= low) & (step < low + count))
                def _(ref=ref, low=low):
                    column = pl.multiple_of((step - low) * FB, FB)
                    pltpu.make_async_copy(
                        ref.at[:, pl.ds(column, FB)], wbuf.at[where], sem.at[where]
                    ).start()

                base += count

        @pl.when(j == 0)
        def _():
            fetch(j, 0)
            df[0:half, :] = own_ref[...]
            df[half:r, :] = peer_ref[...]
            acc[...] = jnp.zeros_like(acc)
            du[...] = jnp.zeros_like(du)
            dd[...] = dot_nt(df[...], bd_ref[...]).astype(BF16)

        @pl.when(j + 1 < blocks)
        def _():
            fetch(j + 1, 1 - slot)

        pltpu.make_async_copy(p0.at[:, pl.ds(0, FB)], wbuf.at[slot], sem.at[slot]).wait()

        sub = 256
        for n in range(UB // sub):
            cs = slice(n * sub, (n + 1) * sub)
            dh = dot(df[...], wbuf[slot, :, 2 * UB + n * sub : 2 * UB + (n + 1) * sub])
            dh += dot(dd[...], ad_ref[:, cs])
            g = g_ref[:, cs].astype(F32)
            u = u_ref[:, cs].astype(F32)
            act, slope = gelu_both(g)
            dgu[:, cs] = (dh * u * slope).astype(BF16)
            dgu[:, UB + n * sub : UB + (n + 1) * sub] = (dh * act).astype(BF16)
            hs[:, cs] = (act * u).astype(BF16)
        d_both = dgu[...]
        for c in range(width // 512):
            cc = slice(c * 512, (c + 1) * 512)
            acc[:, cc] += dot_nt(d_both, wbuf[slot, cc, 0 : 2 * UB])
        du[...] += dot_nt(d_both, bgu_ref[...])
        both = dot(ut_ref[...], d_both)
        dbg_out[...] = both[:RANK, :UB]
        dbu_out[...] = both[RANK:, UB:]
        gad_out[...] = dot_tn(dd[...], hs[...])

        @pl.when(j == blocks - 1)
        def _():
            total = acc[...] + dot(du[...].astype(BF16), ain_ref[...])
            own_out[...] = total[:half]
            peer_out[...] = total[half:].astype(BF16)
            du_out[...] = du[...]

    rows_block = lambda: pl.BlockSpec((r, UB), lambda j: (rb, j))
    unit_block = lambda: pl.BlockSpec((RANK, UB), lambda j: (0, j))
    row_const = lambda n: pl.BlockSpec((r, n), lambda j: (rb, 0), pipeline_mode=pl.Buffered(1))
    shape = jax.ShapeDtypeStruct
    return pl.pallas_call(
        body,
        grid=(blocks,),
        in_specs=[
            const_spec((half, width)),
            const_spec((half, width)),
            any_spec(),
            any_spec(),
            any_spec(),
            rows_block(),
            rows_block(),
            pl.BlockSpec((2 * RANK, 2 * UB), lambda j: (0, j)),
            unit_block(),
            const_spec((RANK, width)),
            pl.BlockSpec((2 * RANK, r), lambda j: (0, rb), pipeline_mode=pl.Buffered(1)),
            const_spec((2 * RANK, width)),
        ],
        out_specs=[
            const_spec((half, width)),
            const_spec((half, width)),
            unit_block(),
            unit_block(),
            unit_block(),
            const_spec((r, 2 * RANK)),
        ],
        out_shape=[
            shape((half, width), F32),
            shape((half, width), BF16),
            shape((RANK, units), F32),
            shape((RANK, units), F32),
            shape((RANK, units), F32),
            shape((r, 2 * RANK), F32),
        ],
        scratch_shapes=[
            pltpu.VMEM((r, width), BF16),
            pltpu.VMEM((r, width), F32),
            pltpu.VMEM((2, width, FB), BF16),
            pltpu.VMEM((r, RANK), BF16),
            pltpu.VMEM((r, 2 * RANK), F32),
            pltpu.VMEM((r, 2 * UB), BF16),
            pltpu.VMEM((r, UB), BF16),
            pltpu.SemaphoreType.DMA((2,)),
        ],
        compiler_params=params(),
        cost_estimate=pl.CostEstimate(
            flops=6 * r * width * units,
            bytes_accessed=6 * width * units,
            transcendentals=r * units,
        ),
        name="ffn_bwd",
    )(own, peer, *packs, g_pre, u_pre, bgu, ad_t, bd, u_t, a_in_t)


def ple_both(combined, ffn_own, ffn_recv, out_grad, ple_in, packed, column, gains, prev, rb):
    half, width = ffn_own.shape
    rows = combined.shape[0]
    pd = ple_in.shape[1]
    tile = half // 2

    def body(c_ref, fo_ref, fr_ref, og_ref, pi_ref, w_ref, gain_ref, *refs):
        out_ref, dffn_ref, dfirst_ref = refs[-3:]
        ffn = fo_ref[...] + fr_ref[...].astype(F32)
        y = c_ref[...] + normed(ffn, gain_ref[4:5, :])
        pre = dot(y.astype(BF16), w_ref[:, 0:pd])
        side = pi_ref[...].astype(F32)
        act, slope = gelu_both(pre)
        wide = dot_nt((act * side).astype(BF16), w_ref[:, pd : 2 * pd])
        out_ref[...] = (y + normed(wide, gain_ref[5:6, :])).astype(BF16)
        cot = og_ref[...].astype(F32)
        d_wide = norm_back(wide, gain_ref[5:6, :], cot).astype(BF16)
        d_pre = (dot(d_wide, w_ref[:, pd : 2 * pd]) * side * slope).astype(BF16)
        d_first = cot + dot_nt(d_pre, w_ref[:, 0:pd])
        dfirst_ref[...] = d_first
        dffn_ref[...] = norm_back(ffn, gain_ref[4:5, :], d_first).astype(BF16)

    n = half // tile
    here = lambda w: pl.BlockSpec((tile, w), lambda i: (i, 0))
    there = lambda w: pl.BlockSpec((tile, w), lambda i: (rb * n + i, 0))
    shape = jax.ShapeDtypeStruct
    return pl.pallas_call(
        body,
        grid=(n,),
        in_specs=[
            there(width),
            here(width),
            here(width),
            there(width),
            there(pd),
            pl.BlockSpec((width, 2 * pd), lambda i: (0, column), pipeline_mode=pl.Buffered(1)),
            const_spec(gains.shape),
        ]
        + [any_spec() for _ in prev],
        out_specs=[there(width), here(width), here(width)],
        out_shape=[
            shape((rows, width), BF16),
            shape((half, width), BF16),
            shape((half, width), F32),
        ],
        input_output_aliases={7: 0} if prev else {},
        compiler_params=params(),
        cost_estimate=pl.CostEstimate(
            flops=8 * half * width * pd, bytes_accessed=20 * half * width, transcendentals=0
        ),
        name="ple_both",
    )(combined, ffn_own, ffn_recv, out_grad, ple_in, packed, gains, *prev)


def between_bwd(d_first, combined, dh_own, dh_recv, attn_proj, low, packed, column, gains, prev, rb):
    half, width = d_first.shape
    rows = combined.shape[0]
    lr = low.shape[1]
    tile = half // 2

    def body(df_ref, c_ref, ho_ref, hr_ref, ap_ref, low_ref, w_ref, gain_ref, *refs):
        da_ref, db_ref, dn_ref = refs[-3:]
        d_h2 = ho_ref[...] + hr_ref[...].astype(F32)
        d_comb = df_ref[...] + norm_back(c_ref[...], gain_ref[3:4, :], d_h2)
        d_branch = d_comb * RSQRT_TWO
        db_ref[...] = d_branch
        da_ref[...] = norm_back(ap_ref[...], gain_ref[1:2, :], d_branch).astype(BF16)
        wide = dot_nt(low_ref[...], w_ref[:, lr : 2 * lr])
        d_wide = norm_back(wide, gain_ref[2:3, :], d_branch).astype(BF16)
        d_low = dot(d_wide, w_ref[:, lr : 2 * lr]).astype(BF16)
        dn_ref[...] = d_branch + dot_nt(d_low, w_ref[:, 0:lr])

    n = half // tile
    here = lambda w: pl.BlockSpec((tile, w), lambda i: (i, 0))
    there = lambda w: pl.BlockSpec((tile, w), lambda i: (rb * n + i, 0))
    shape = jax.ShapeDtypeStruct
    return pl.pallas_call(
        body,
        grid=(n,),
        in_specs=[
            here(width),
            there(width),
            here(width),
            here(width),
            there(width),
            there(lr),
            pl.BlockSpec((width, 2 * lr), lambda i: (0, column), pipeline_mode=pl.Buffered(1)),
            const_spec(gains.shape),
        ]
        + [any_spec() for _ in prev],
        out_specs=[here(width), there(width), there(width)],
        out_shape=[
            shape((half, width), BF16),
            shape((rows, width), F32),
            shape((rows, width), F32),
        ],
        input_output_aliases={8: 1, 9: 2} if prev else {},
        compiler_params=params(),
        cost_estimate=pl.CostEstimate(
            flops=6 * half * width * lr, bytes_accessed=26 * half * width, transcendentals=0
        ),
        name="between_bwd",
    )(d_first, combined, dh_own, dh_recv, attn_proj, low, packed, gains, *prev)


def attention_bwd(pieces, turn, packed, wo_column, bo, ao_t, q, k, v, probs, raw, gains, cos, sin):
    length, q_width = q.shape
    width = packed.shape[0]
    heads = q_width // HD
    half_hd = HD // 2
    scale = HD ** (-0.5)
    n_blocks = length // BLK
    span = WIN // BLK
    quarter = pieces[0].shape[0]
    count = len(pieces)

    def unrotate(d, cos_v, sin_v):
        d1, d2 = d[:, :half_hd], d[:, half_hd:]
        return jnp.concatenate([d1 * cos_v + d2 * sin_v, d2 * cos_v - d1 * sin_v], axis=1)

    def body(turn_ref, *refs):
        piece_refs = refs[:count]
        (wo_ref, bo_ref, ao_ref, q_ref, k_ref, v_ref, p_ref, rq_ref, rk_ref, gain_ref, cos_ref,
         sin_ref, out_ref, du_ref, da, du, dk, dv) = refs[count:]
        hh = pl.program_id(0)

        @pl.when(hh == 0)
        def _():
            shift = turn_ref[0] * (length // 2)
            for i, ref in enumerate(piece_refs):
                place = lax.rem(shift + i * quarter, length)
                da[pl.ds(pl.multiple_of(place, quarter), quarter), :] = ref[...]
            got = dot_nt(da[...], bo_ref[...])
            du_ref[...] = got
            du[...] = got.astype(BF16)
            dk[...] = jnp.zeros_like(dk)
            dv[...] = jnp.zeros_like(dv)

        dctx = (dot(da[...], wo_ref[...]) + dot(du[...], ao_ref[...])).astype(BF16)
        cos_v, sin_v = cos_ref[...], sin_ref[...]
        for i in range(n_blocks):
            low, high = max(0, i - span + 1) * BLK, (i + 1) * BLK
            rows = slice(i * BLK, (i + 1) * BLK)
            d_i = dctx[rows]
            p_i = p_ref[0, rows, low:high]
            p_f = p_i.astype(F32)
            dp = dot_nt(d_i, v_ref[low:high, :])
            ds = p_f * (dp - jnp.sum(p_f * dp, axis=-1, keepdims=True))
            ds = ds.astype(BF16)
            dq = dot(ds, k_ref[low:high, :]) * scale
            dk[low:high, :] += dot_tn(ds, q_ref[rows, :])
            dv[low:high, :] += dot_tn(p_i, d_i)
            back = norm_back(rq_ref[rows, :], gain_ref[0:1, :], unrotate(dq, cos_v[rows], sin_v[rows]))
            out_ref[rows, pl.ds(pl.multiple_of(hh * HD, HD), HD)] = back.astype(BF16)

        @pl.when(hh == heads - 1)
        def _():
            back = norm_back(rk_ref[...], gain_ref[1:2, :], unrotate(dk[...] * scale, cos_v, sin_v))
            out_ref[:, q_width : q_width + HD] = back.astype(BF16)
            out_ref[:, q_width + HD : q_width + 2 * HD] = dv[...].astype(BF16)

    shape = jax.ShapeDtypeStruct
    head_block = pl.BlockSpec((length, HD), lambda h: (0, h))
    total = q_width + 2 * HD
    return pl.pallas_call(
        body,
        grid=(heads,),
        in_specs=[pl.BlockSpec(memory_space=pltpu.SMEM)]
        + [const_spec(piece.shape) for piece in pieces]
        + [
            pl.BlockSpec((width, HD), lambda h: (0, wo_column + h)),
            const_spec(bo.shape),
            pl.BlockSpec((RANK, HD), lambda h: (0, h)),
            head_block,
            const_spec(k.shape),
            const_spec(v.shape),
            pl.BlockSpec((1, length, length), lambda h: (h, 0, 0)),
            head_block,
            pl.BlockSpec((length, HD), lambda h: (0, heads), pipeline_mode=pl.Buffered(1)),
            const_spec(gains.shape),
            const_spec(cos.shape),
            const_spec(sin.shape),
        ],
        out_specs=[const_spec((length, total)), const_spec((length, RANK))],
        out_shape=[shape((length, total), BF16), shape((length, RANK), F32)],
        scratch_shapes=[
            pltpu.VMEM((length, width), BF16),
            pltpu.VMEM((length, RANK), BF16),
            pltpu.VMEM((length, HD), F32),
            pltpu.VMEM((length, HD), F32),
        ],
        compiler_params=params(),
        cost_estimate=pl.CostEstimate(
            flops=2 * length * width * q_width + 8 * heads * length * WIN * HD,
            bytes_accessed=24 * 1024 * 1024,
            transcendentals=0,
        ),
        name="attention_bwd",
    )(turn, *pieces, packed, bo, ao_t, q, k, v, probs, raw, raw, gains, cos, sin)


def final_bwd(x, d_norm, d_branch, dh_own, dh_recv, gains):
    rows, width = x.shape
    tile = rows // 4

    def body(x_ref, dn_ref, db_ref, ho_ref, hr_ref, gain_ref, out_ref):
        total = dn_ref[...] + ho_ref[...] + hr_ref[...].astype(F32)
        out_ref[...] = db_ref[...] + norm_back(x_ref[...].astype(F32), gain_ref[0:1, :], total)

    block = pl.BlockSpec((tile, width), lambda i: (i, 0))
    return pl.pallas_call(
        body,
        grid=(rows // tile,),
        in_specs=[block] * 5 + [const_spec(gains.shape)],
        out_specs=block,
        out_shape=jax.ShapeDtypeStruct((rows, width), F32),
        compiler_params=params(),
        cost_estimate=pl.CostEstimate(
            flops=20 * rows * width, bytes_accessed=20 * rows * width, transcendentals=0
        ),
        name="final_bwd",
    )(x, d_norm, d_branch, dh_own, dh_recv, gains)


def rope_tables(length):
    half_dim = HD // 2
    inverse = ROPE_BASE ** (-jnp.arange(half_dim, dtype=F32) / half_dim)
    angles = jnp.arange(length, dtype=F32)[:, None] * inverse[None, :]
    return jnp.cos(angles), jnp.sin(angles)


def rotate(values, cos, sin):
    half_dim = HD // 2
    a, b = values[..., :half_dim], values[..., half_dim:]
    return jnp.concatenate([a * cos - b * sin, b * cos + a * sin], axis=-1)


def on_device(
    hidden_in,
    per_layer_input,
    out_grad,
    adapter_ids,
    weight_qkv,
    weight_attn_out,
    weight_gate_up,
    weight_down,
    laurel_left,
    laurel_right,
    per_layer_gate,
    per_layer_proj,
    norm_gains,
    head_gains,
    adapter_qkv_in,
    adapter_qkv_out,
    adapter_attn_in,
    adapter_attn_out,
    adapter_ffn_in,
    adapter_ffn_out,
    adapter_down_in,
    adapter_down_out,
):
    rows_here, width = hidden_in.shape
    dp = lax.axis_size("dp")
    length = rows_here * 2
    half = rows_here // 2
    per_group = HEADS // KV
    q_width = per_group * HD
    qkv_width = q_width + 2 * HD
    units = weight_down.shape[0]
    blocks = units // UB
    adapters = adapter_qkv_in.shape[0]
    a = adapter_ids[0]
    t = lax.axis_index("tensor")

    def swap(v):
        return lax.ppermute(v, "tensor", [(0, 1), (1, 0)])

    def in_order(own, other):
        first = jnp.where(t == 0, own, other)
        second = jnp.where(t == 0, other, own)
        return jnp.concatenate([first, second], axis=0)

    def mine(v):
        return lax.dynamic_slice_in_dim(v, t * rows_here, rows_here, axis=0)

    def theirs(v):
        return lax.dynamic_slice_in_dim(v, (1 - t) * rows_here, rows_here, axis=0)

    counts = (1, blocks // 2, blocks - 1 - blocks // 2)
    lr = laurel_left.shape[1]
    pd = per_layer_gate.shape[1]
    pack_1 = pack_blocks(
        weight_gate_up, weight_down, 0, counts[0],
        [(weight_qkv, qkv_width), (weight_attn_out, q_width), (laurel_left, lr), (laurel_right, lr)],
        width, "pack_1",
    )
    gather = lambda v: lax.all_gather(v, "dp", axis=0, tiled=True)
    full_1 = gather(pack_1)
    x_peer = swap(hidden_in)
    pack_2 = pack_blocks(
        weight_gate_up, weight_down, counts[0], counts[1],
        [(per_layer_gate, pd), (per_layer_proj, pd)], width, "pack_2",
    )
    pack_3 = pack_blocks(
        weight_gate_up, weight_down, counts[0] + counts[1], counts[2], [], width, "pack_3"
    )
    pack_2, _ = lax.optimization_barrier((pack_2, full_1))
    full_2 = gather(pack_2)
    w_qkv = full_1[:, FB : FB + qkv_width]
    wo_at = FB + qkv_width
    w_o_t = full_1[:, wo_at : wo_at + q_width]
    lau_at = wo_at + q_width
    left = full_1[:, lau_at : lau_at + lr]
    right_t = full_1[:, lau_at + lr : lau_at + 2 * lr]
    ple_column = counts[1] * FB // (2 * pd)

    two = jnp.asarray(2.0, BF16)
    qkv_in = adapter_qkv_in[a]
    raw_out = adapter_qkv_out[a].reshape(RANK, qkv_width) * two
    column = jnp.arange(qkv_width)
    member = (column >= q_width).astype(jnp.int32) + (column >= q_width + HD).astype(jnp.int32)
    pick = (jnp.arange(3)[:, None] == member[None, :]).astype(BF16)
    b_qkv = (pick[:, None, :] * raw_out[None]).reshape(3 * RANK, qkv_width)
    a_o = adapter_attn_in[a]
    b_o = adapter_attn_out[a] * two
    a_ffn = adapter_ffn_in[a]
    b_ffn = adapter_ffn_out[a] * two
    b_unit = jnp.swapaxes(b_ffn.reshape(RANK, 2, blocks, UB), 1, 2)
    side = (jnp.arange(2)[:, None] == jnp.arange(2)[None, :]).astype(BF16)
    bgu = (side[:, None, None, :, None] * b_unit[None]).reshape(2 * RANK, 2 * units)
    ad_t = adapter_down_in[a].T
    b_d = adapter_down_out[a] * two

    cos, sin = rope_tables(length)
    x_float = hidden_in.astype(F32)
    x_norm = normed(x_float, norm_gains[0])
    h_own = x_norm.astype(BF16)
    x_all = in_order(hidden_in, x_peer)
    h_all = normed(x_all.astype(F32), norm_gains[0]).astype(BF16)
    u_qkv = dot(h_all, qkv_in).astype(BF16)
    raw = dot(h_all, w_qkv) + dot(u_qkv, b_qkv)
    q_raw = raw[:, :q_width].reshape(length, per_group, HD)
    k_raw = raw[:, q_width : q_width + HD]
    queries = rotate(normed(q_raw, head_gains[0]), cos[:, None], sin[:, None]).astype(BF16)
    keys = rotate(normed(k_raw, head_gains[1]), cos, sin).astype(BF16)
    values = raw[:, q_width + HD :].astype(BF16)
    index = jnp.arange(length) // BLK
    distance = index[:, None] - index[None, :]
    allowed = ((distance >= 0) & (distance < WIN // BLK))[None]
    scores = jnp.einsum("lqd,md->qlm", queries, keys, preferred_element_type=F32) * HD ** (-0.5)
    scores = jnp.where(allowed, scores, NEG_BIG)
    shifted = jnp.exp(scores - jnp.max(scores, axis=-1, keepdims=True))
    probs = (shifted / jnp.sum(shifted, axis=-1, keepdims=True)).astype(BF16)
    context = (
        jnp.einsum("qlm,md->lqd", probs, values, preferred_element_type=F32)
        .reshape(length, q_width)
        .astype(BF16)
    )
    queries = queries.reshape(length, q_width)
    u_attn_f = dot(context, a_o)
    u_attn = u_attn_f.astype(BF16)
    attn_part = dot_nt(context, w_o_t) + dot(u_attn, b_o)
    attn_recv = swap(theirs(attn_part).astype(BF16))
    attn_proj = mine(attn_part) + attn_recv.astype(F32)
    laurel_low = dot(h_own, left).astype(BF16)
    laurel_wide = dot_nt(laurel_low, right_t)
    combined = (
        x_float + normed(attn_proj, norm_gains[1]) + x_norm + normed(laurel_wide, norm_gains[2])
    ) * RSQRT_TWO
    h2_own = normed(combined, norm_gains[3]).astype(BF16)

    h2_peer = swap(h2_own)
    h2 = jnp.concatenate([h2_own[:half], h2_peer[:half], h2_own[half:], h2_peer[half:]], axis=0)
    u_ffn = dot(h2, a_ffn).astype(BF16)
    pack_3, _, _ = lax.optimization_barrier((pack_3, full_2, h2_own))
    full_3 = gather(pack_3)
    g_pre, u_pre, acc, ud = ffn_fwd(
        h2, full_1, counts[0], 0, u_ffn, bgu, ad_t, b_d, None, None
    )
    g_pre, u_pre, acc, ud = ffn_fwd(
        h2, full_2, counts[1], counts[0], u_ffn, bgu, ad_t, b_d, (acc, ud, g_pre, u_pre), None
    )
    at = counts[0] + counts[1]
    fwd_parts, ud_parts, ple_parts, bwd_parts = [], [], [], []
    d_ffn_parts, d_attn_own, d_attn_peer = [], [], []
    for s in range(2):
        g_pre, u_pre, own, peer, ud_s = ffn_fwd(
            h2, full_3, counts[2], at, u_ffn, bgu, ad_t, b_d, (acc, ud, g_pre, u_pre), s
        )
        fwd_parts.append((own, swap(peer)))
        ud_parts.append(ud_s)
    layer_out = []
    for s in range(2):
        own, recv = fwd_parts[s]
        whole, d_ffn_s, d_first_s = ple_both(
            combined, own, recv, out_grad, per_layer_input, full_2, ple_column, norm_gains,
            layer_out, s,
        )
        layer_out = [whole]
        ple_parts.append((d_ffn_s, swap(d_ffn_s), d_first_s))
    packs = (full_1, full_2, full_3)
    branch = []
    for s in range(2):
        d_ffn_s, d_ffn_recv, d_first_s = ple_parts[s]
        got = ffn_bwd(
            d_ffn_s, d_ffn_recv, packs, counts, g_pre, u_pre, bgu, ad_t, b_d, u_ffn.T, a_ffn.T, s
        )
        bwd_parts.append(got[2:])
        d_ffn_parts += [d_ffn_s, d_ffn_recv]
        d_h2_recv = swap(got[1])
        d_attn_s, *branch = between_bwd(
            d_first_s, combined, got[0], d_h2_recv, attn_proj, laurel_low, full_1,
            lau_at // (2 * lr), norm_gains, branch, s,
        )
        d_attn_own.append(d_attn_s)
        d_attn_peer.append(swap(d_attn_s))
    d_branch, d_norm = branch

    tag = jnp.full((1, 128), a, BF16)

    def onehot_of(ids):
        return (ids[None, :] == jnp.arange(adapters, dtype=F32)[:, None]).astype(BF16)

    def over_sequences(grad):
        n, m = grad.shape
        send = jnp.concatenate([grad.astype(BF16), jnp.broadcast_to(tag, (n, 128))], axis=1)
        return send

    def summed(send):
        got = lax.all_gather(send, "dp", axis=0, tiled=False)
        onehot = onehot_of(got[:, 0, send.shape[1] - 1].astype(F32))
        got = got[:, :, : send.shape[1] - 128]
        return jnp.einsum("as,snm->anm", onehot, got, preferred_element_type=F32)

    send_ffn = over_sequences(
        jnp.concatenate(
            [
                2.0 * (bwd_parts[0][0] + bwd_parts[1][0]),
                2.0 * (bwd_parts[0][1] + bwd_parts[1][1]),
                bwd_parts[0][2] + bwd_parts[1][2],
            ],
            axis=0,
        )
    )

    pieces = d_attn_own + d_attn_peer
    pieces, send_ffn = lax.optimization_barrier((pieces, send_ffn))
    sum_ffn = summed(send_ffn)
    d_raw, du_attn = attention_bwd(
        pieces, t.astype(jnp.int32).reshape(1), full_1, wo_at // HD, b_o, a_o.T, queries, keys,
        values, probs, raw, head_gains, cos, sin,
    )
    d_u = dot_nt(d_raw, b_qkv).astype(BF16)
    d_h_peer = (dot_nt(theirs(d_raw), w_qkv) + dot_nt(theirs(d_u), qkv_in)).astype(BF16)
    d_h_recv = swap(d_h_peer)
    d_raw, d_u, _ = lax.optimization_barrier((d_raw, d_u, d_h_peer))
    grad_b = 2.0 * dot_tn(u_qkv, d_raw)
    grad_qkv_out = jnp.concatenate(
        [
            grad_b[:RANK, :q_width],
            grad_b[RANK : 2 * RANK, q_width : q_width + HD],
            grad_b[2 * RANK :, q_width + HD :],
        ],
        axis=1,
    )
    sum_qkv_out = summed(over_sequences(grad_qkv_out))
    sum_attn_in = summed(over_sequences(dot_tn(du_attn.astype(BF16), context)))

    d_attn_all = in_order(
        jnp.concatenate(d_attn_own, axis=0), jnp.concatenate(d_attn_peer, axis=0)
    )
    d_ffn_all = jnp.concatenate(d_ffn_parts, axis=0)
    du_ffn = jnp.concatenate([bwd_parts[0][3], bwd_parts[1][3]], axis=0).astype(BF16)
    ud_low = jnp.concatenate(ud_parts, axis=0).astype(BF16)
    send = jnp.concatenate(
        [
            dot_tn(h2, du_ffn).astype(BF16),
            (2.0 * dot_tn(d_ffn_all, ud_low)).astype(BF16),
            (2.0 * dot_tn(d_attn_all, u_attn)).astype(BF16),
            dot_tn(h_all, d_u).astype(BF16),
            jnp.broadcast_to(tag[:, :1], (width, 1)),
        ],
        axis=1,
    )
    got = lax.all_to_all(send, ("dp", "tensor"), 0, 0, tiled=True).reshape(2 * dp, -1, send.shape[1])
    onehot = onehot_of(got[:, 0, send.shape[1] - 1].astype(F32))
    shared = jnp.einsum("as,snm->anm", onehot, got, preferred_element_type=F32)
    d_h_own = dot_nt(mine(d_raw), w_qkv) + dot_nt(mine(d_u), qkv_in)
    input_grad = final_bwd(hidden_in, d_norm, d_branch, d_h_own, d_h_recv, norm_gains)
    return (
        layer_out[0],
        input_grad,
        shared[:, :, 4 * RANK : 7 * RANK],
        sum_qkv_out.reshape(adapters, RANK, 1, qkv_width),
        jnp.swapaxes(sum_attn_in, 1, 2),
        jnp.swapaxes(shared[:, :, 3 * RANK : 4 * RANK], 1, 2),
        shared[:, :, : 2 * RANK],
        jnp.stack([sum_ffn[:, :RANK], sum_ffn[:, RANK : 2 * RANK]], axis=2),
        jnp.swapaxes(sum_ffn[:, 2 * RANK :], 1, 2),
        jnp.swapaxes(shared[:, :, 2 * RANK : 3 * RANK], 1, 2),
    )


def solution(mesh):
    in_specs = (
        P(("dp", "tensor"), None),
        P(("dp", "tensor"), None),
        P(("dp", "tensor"), None),
        P("dp"),
        P("dp", "tensor", None),
        P("tensor", "dp"),
        P("dp", None, "tensor"),
        P("tensor", "dp"),
        P("dp", None),
        P(None, "dp"),
        P("dp", None),
        P(None, "dp"),
        P(),
        P(),
        P(),
        P(None, None, "tensor", None),
        P(None, "tensor", None),
        P(),
        P(),
        P(None, None, None, "tensor"),
        P(None, "tensor", None),
        P(),
    )
    out_specs = (
        P(("dp", "tensor"), None),
        P(("dp", "tensor"), None),
        P(None, ("dp", "tensor"), None),
        P(None, None, "tensor", None),
        P(None, "tensor", None),
        P(None, None, ("dp", "tensor")),
        P(None, ("dp", "tensor"), None),
        P(None, None, None, "tensor"),
        P(None, "tensor", None),
        P(None, None, ("dp", "tensor")),
    )
    return jax.shard_map(
        on_device, mesh=mesh, in_specs=in_specs, out_specs=out_specs, check_vma=False
    )
```

```python
import functools

import jax
import jax.numpy as jnp
from jax import lax
from jax.experimental import pallas as pl
from jax.experimental.pallas import tpu as pltpu
from jax.sharding import PartitionSpec as P

HEADS = 8
KV = 2
HD = 256
WIN = 512
BLK = 256
RANK = 16
UB = 512
FB = 3 * UB

NORM_EPSILON = 1e-06
RSQRT_TWO = 0.7071067811865476
ROPE_BASE = 10000.0
NEG_BIG = -1e30
GELU_A = 0.7978845608028654
GELU_B = 0.044715

F32 = jnp.float32
BF16 = jnp.bfloat16
VMEM_LIMIT = 58 * 1024 * 1024


def dot(a, b):
    return lax.dot_general(a, b, (((1,), (0,)), ((), ())), preferred_element_type=F32)


def dot_nt(a, b):
    return lax.dot_general(a, b, (((1,), (1,)), ((), ())), preferred_element_type=F32)


def dot_tn(a, b):
    return lax.dot_general(a, b, (((0,), (0,)), ((), ())), preferred_element_type=F32)


def inv_rms(v):
    return lax.rsqrt(jnp.mean(v * v, axis=-1, keepdims=True) + NORM_EPSILON)


def normed(v, gains):
    return v * inv_rms(v) * gains


def norm_back(v, gains, cotangent):
    r = inv_rms(v)
    gc = gains * cotangent
    return r * gc - v * (r * r * r * jnp.mean(v * gc, axis=-1, keepdims=True))


def gelu_tanh(v):
    return 0.5 * v * (1.0 + jnp.tanh(GELU_A * (v + GELU_B * v * v * v)))


def gelu_both(v):
    v2 = v * v
    th = jnp.tanh(GELU_A * v * (1.0 + GELU_B * v2))
    half = 0.5 * (1.0 + th)
    slope = half + 0.5 * v * (1.0 - th * th) * (GELU_A * (1.0 + 3.0 * GELU_B * v2))
    return v * half, slope


def const_spec(shape):
    return pl.BlockSpec(shape, lambda *_: (0,) * len(shape), pipeline_mode=pl.Buffered(1))


def any_spec():
    return pl.BlockSpec(memory_space=pl.ANY)


def params():
    return pltpu.CompilerParams(vmem_limit_bytes=VMEM_LIMIT)


def pack_blocks(gate_up, down, first, count, rest, cols, name):
    rows = gate_up.shape[0]
    widths = [n for _, n in rest]

    def body(gu_ref, down_ref, *refs):
        out = refs[-1]
        for b in range(count):
            cs = slice(b * UB, (b + 1) * UB)
            out[:, b * FB : b * FB + UB] = gu_ref[:, 0, cs]
            out[:, b * FB + UB : b * FB + 2 * UB] = gu_ref[:, 1, cs]
            out[:, b * FB + 2 * UB : (b + 1) * FB] = down_ref[cs, :].T
        at = count * FB
        for ref, (value, n) in zip(refs[:-1], rest):
            if value.shape == (rows, n):
                out[:, at : at + n] = ref[...]
            else:
                out[:, at : at + n] = ref[...].T
            at += n

    lo = first * UB
    return pl.pallas_call(
        body,
        grid=(1,),
        in_specs=[
            pl.BlockSpec((pl.Element(rows), pl.Element(2), pl.Element(count * UB)), lambda i: (0, 0, lo)),
            pl.BlockSpec((pl.Element(count * UB), pl.Element(rows)), lambda i: (lo, 0)),
        ]
        + [const_spec(v.shape) for v, _ in rest],
        out_specs=const_spec((rows, count * FB + sum(widths))),
        out_shape=jax.ShapeDtypeStruct((rows, count * FB + sum(widths)), BF16),
        compiler_params=params(),
        name=name,
    )(gate_up, down, *[v for v, _ in rest])


def ffn_fwd(h2, packed, blocks, first, u_low, bgu, ad_t, bd, prev, last):
    rows, width = h2.shape
    units = ad_t.shape[1]
    stream = last is not None
    r = rows // 2 if stream else rows
    rb = last if stream else 0
    half = r // 2
    tile = rows // 2
    sub = 256

    def body(*refs):
        h_ref, w_ref, ul_ref, bgu_ref, ad_ref, bd_ref = refs[:6]
        at = 6
        if prev is not None:
            acc_in, ud_in = refs[6:8]
            at = 10
        outs = refs[at:]
        if stream:
            g_out, u_out, own_out, peer_out, ud_out, acc, ud, hs = outs
        else:
            g_out, u_out, acc_out, ud_out, acc, ud, hs = outs
        j = pl.program_id(0)

        @pl.when(j == 0)
        def _():
            if prev is None:
                acc[...] = jnp.zeros_like(acc)
                ud[...] = jnp.zeros_like(ud)
            else:
                acc[...] = acc_in[...]
                ud[...] = ud_in[...]

        for k in range(r // tile):
            at_rows = slice(k * tile, (k + 1) * tile)
            h = h_ref[at_rows, :]
            ul = ul_ref[at_rows, :]
            for n in range(UB // sub):
                cs = slice(n * sub, (n + 1) * sub)
                us = slice(UB + n * sub, UB + (n + 1) * sub)
                g = dot(h, w_ref[:, cs]) + dot(ul, bgu_ref[:, cs])
                u = dot(h, w_ref[:, us]) + dot(ul, bgu_ref[:, us])
                g_out[at_rows, cs] = g.astype(BF16)
                u_out[at_rows, cs] = u.astype(BF16)
                hs[at_rows, cs] = (gelu_tanh(g) * u).astype(BF16)
            hidden = hs[at_rows, :]
            for c in range(width // 512):
                cc = slice(c * 512, (c + 1) * 512)
                acc[at_rows, cc] += dot_nt(hidden, w_ref[cc, 2 * UB : 3 * UB])
            ud[at_rows, :] += dot_nt(hidden, ad_ref[...])

        @pl.when(j == blocks - 1)
        def _():
            ud_out[...] = ud[...]
            if stream:
                total = acc[...] + dot(ud[...].astype(BF16), bd_ref[...])
                own_out[...] = total[:half]
                peer_out[...] = total[half:].astype(BF16)
            else:
                acc_out[...] = acc[...]

    row_const = lambda n: pl.BlockSpec((r, n), lambda j: (rb, 0), pipeline_mode=pl.Buffered(1))
    in_specs = [
        row_const(width),
        pl.BlockSpec((width, FB), lambda j: (0, j)),
        row_const(2 * RANK),
        pl.BlockSpec((2 * RANK, 2 * UB), lambda j: (0, first + j)),
        pl.BlockSpec((RANK, UB), lambda j: (0, first + j)),
        const_spec((RANK, width)),
    ]
    args = [h2, packed, u_low, bgu, ad_t, bd]
    aliases = {}
    if prev is not None:
        acc_prev, ud_prev, g_prev, u_prev = prev
        in_specs += [row_const(width), row_const(RANK), any_spec(), any_spec()]
        args += [acc_prev, ud_prev, g_prev, u_prev]
        aliases = {8: 0, 9: 1}
    pre_spec = pl.BlockSpec((r, UB), lambda j: (rb, first + j))
    out_specs = [pre_spec, pre_spec]
    shape = jax.ShapeDtypeStruct
    out_shape = [shape((rows, units), BF16)] * 2
    if stream:
        out_specs += [const_spec((half, width)), const_spec((half, width)), const_spec((r, RANK))]
        out_shape += [
            shape((half, width), F32),
            shape((half, width), BF16),
            shape((r, RANK), F32),
        ]
    else:
        out_specs += [const_spec((r, width)), const_spec((r, RANK))]
        out_shape += [shape((r, width), F32), shape((r, RANK), F32)]
    return pl.pallas_call(
        body,
        grid=(blocks,),
        in_specs=in_specs,
        out_specs=out_specs,
        out_shape=out_shape,
        scratch_shapes=[
            pltpu.VMEM((r, width), F32),
            pltpu.VMEM((r, RANK), F32),
            pltpu.VMEM((r, UB), BF16),
        ],
        input_output_aliases=aliases,
        compiler_params=params(),
        cost_estimate=pl.CostEstimate(
            flops=6 * r * width * UB * blocks,
            bytes_accessed=2 * width * FB * blocks + 8 * r * width,
            transcendentals=r * UB * blocks,
        ),
        name="ffn_fwd",
    )(*args)


def ffn_bwd(own, peer, packs, counts, first, g_pre, u_pre, bgu, ad_t, bd, u_t, a_in_t, rb, prev, last):
    half, width = own.shape
    r = 2 * half
    units = ad_t.shape[1]
    blocks = sum(counts)
    sub = 256

    def body(*refs):
        own_ref, peer_ref, g_ref, u_ref, bgu_ref, ad_ref, bd_ref, ut_ref, ain_ref = refs[:9]
        pack_refs = refs[9 : 9 + len(packs)]
        at = 9 + len(packs)
        if prev is not None:
            acc_in, du_in = refs[at : at + 2]
            at += 5
        if last:
            dbg_out, dbu_out, gad_out, du_out, own_out, peer_out = refs[at : at + 6]
            at += 6
        else:
            dbg_out, dbu_out, gad_out, du_out, acc_out = refs[at : at + 5]
            at += 5
        df, acc, wbuf, dd, du, dgu, hs, sem = refs[at:]
        j = pl.program_id(0)
        slot = lax.rem(j, 2)

        def fetch(step, where):
            base = 0
            for ref, count in zip(pack_refs, counts):
                low = base

                @pl.when((step >= low) & (step < low + count))
                def _(ref=ref, low=low):
                    column = pl.multiple_of((step - low) * FB, FB)
                    pltpu.make_async_copy(
                        ref.at[:, pl.ds(column, FB)], wbuf.at[where], sem.at[where]
                    ).start()

                base += count

        @pl.when(j == 0)
        def _():
            fetch(j, 0)
            df[0:half, :] = own_ref[...]
            df[half:r, :] = peer_ref[...]
            if prev is None:
                acc[...] = jnp.zeros_like(acc)
                du[...] = jnp.zeros_like(du)
            else:
                acc[...] = acc_in[...]
                du[...] = du_in[...]
            dd[...] = dot_nt(df[...], bd_ref[...]).astype(BF16)

        @pl.when(j + 1 < blocks)
        def _():
            fetch(j + 1, 1 - slot)

        pltpu.make_async_copy(
            pack_refs[0].at[:, pl.ds(0, FB)], wbuf.at[slot], sem.at[slot]
        ).wait()

        for n in range(UB // sub):
            cs = slice(n * sub, (n + 1) * sub)
            dh = dot(df[...], wbuf[slot, :, 2 * UB + n * sub : 2 * UB + (n + 1) * sub])
            dh += dot(dd[...], ad_ref[:, cs])
            g = g_ref[:, cs].astype(F32)
            u = u_ref[:, cs].astype(F32)
            act, slope = gelu_both(g)
            dgu[:, cs] = (dh * u * slope).astype(BF16)
            dgu[:, UB + n * sub : UB + (n + 1) * sub] = (dh * act).astype(BF16)
            hs[:, cs] = (act * u).astype(BF16)
        d_both = dgu[...]
        for c in range(width // 512):
            cc = slice(c * 512, (c + 1) * 512)
            acc[:, cc] += dot_nt(d_both, wbuf[slot, cc, 0 : 2 * UB])
        du[...] += dot_nt(d_both, bgu_ref[...])
        both = dot(ut_ref[...], d_both)
        dbg_out[...] = both[:RANK, :UB]
        dbu_out[...] = both[RANK:, UB:]
        gad_out[...] = dot_tn(dd[...], hs[...])

        @pl.when(j == blocks - 1)
        def _():
            du_out[...] = du[...]
            if last:
                total = acc[...] + dot(du[...].astype(BF16), ain_ref[...])
                own_out[...] = total[:half]
                peer_out[...] = total[half:].astype(BF16)
            else:
                acc_out[...] = acc[...]

    rows_block = lambda: pl.BlockSpec((r, UB), lambda j: (rb, first + j))
    unit_block = lambda: pl.BlockSpec((RANK, UB), lambda j: (0, first + j))
    shape = jax.ShapeDtypeStruct
    in_specs = [
        const_spec((half, width)),
        const_spec((half, width)),
        rows_block(),
        rows_block(),
        pl.BlockSpec((2 * RANK, 2 * UB), lambda j: (0, first + j)),
        unit_block(),
        const_spec((RANK, width)),
        pl.BlockSpec((2 * RANK, r), lambda j: (0, rb), pipeline_mode=pl.Buffered(1)),
        const_spec((2 * RANK, width)),
    ] + [any_spec() for _ in packs]
    args = [own, peer, g_pre, u_pre, bgu, ad_t, bd, u_t, a_in_t, *packs]
    aliases = {}
    if prev is not None:
        at = len(args)
        in_specs += [const_spec((r, width)), const_spec((r, 2 * RANK))] + [any_spec()] * 3
        args += list(prev)
        aliases = {at + 2: 0, at + 3: 1, at + 4: 2}
    out_specs = [unit_block(), unit_block(), unit_block(), const_spec((r, 2 * RANK))]
    out_shape = [shape((RANK, units), F32)] * 3 + [shape((r, 2 * RANK), F32)]
    if last:
        out_specs += [const_spec((half, width)), const_spec((half, width))]
        out_shape += [shape((half, width), F32), shape((half, width), BF16)]
    else:
        out_specs += [const_spec((r, width))]
        out_shape += [shape((r, width), F32)]
    return pl.pallas_call(
        body,
        grid=(blocks,),
        in_specs=in_specs,
        out_specs=out_specs,
        out_shape=out_shape,
        scratch_shapes=[
            pltpu.VMEM((r, width), BF16),
            pltpu.VMEM((r, width), F32),
            pltpu.VMEM((2, width, FB), BF16),
            pltpu.VMEM((r, RANK), BF16),
            pltpu.VMEM((r, 2 * RANK), F32),
            pltpu.VMEM((r, 2 * UB), BF16),
            pltpu.VMEM((r, UB), BF16),
            pltpu.SemaphoreType.DMA((2,)),
        ],
        input_output_aliases=aliases,
        compiler_params=params(),
        cost_estimate=pl.CostEstimate(
            flops=6 * r * width * UB * blocks,
            bytes_accessed=6 * width * UB * blocks,
            transcendentals=r * UB * blocks,
        ),
        name="ffn_bwd",
    )(*args)


def ple_both(combined, ffn_own, ffn_recv, out_grad, ple_in, packed, column, gains, prev, rb):
    half, width = ffn_own.shape
    rows = combined.shape[0]
    pd = ple_in.shape[1]
    tile = half // 2

    def body(c_ref, fo_ref, fr_ref, og_ref, pi_ref, w_ref, gain_ref, *refs):
        out_ref, dffn_ref, dfirst_ref = refs[-3:]
        ffn = fo_ref[...] + fr_ref[...].astype(F32)
        y = c_ref[...] + normed(ffn, gain_ref[4:5, :])
        pre = dot(y.astype(BF16), w_ref[:, 0:pd])
        side = pi_ref[...].astype(F32)
        act, slope = gelu_both(pre)
        wide = dot_nt((act * side).astype(BF16), w_ref[:, pd : 2 * pd])
        out_ref[...] = (y + normed(wide, gain_ref[5:6, :])).astype(BF16)
        cot = og_ref[...].astype(F32)
        d_wide = norm_back(wide, gain_ref[5:6, :], cot).astype(BF16)
        d_pre = (dot(d_wide, w_ref[:, pd : 2 * pd]) * side * slope).astype(BF16)
        d_first = cot + dot_nt(d_pre, w_ref[:, 0:pd])
        dfirst_ref[...] = d_first
        dffn_ref[...] = norm_back(ffn, gain_ref[4:5, :], d_first).astype(BF16)

    n = half // tile
    here = lambda w: pl.BlockSpec((tile, w), lambda i: (i, 0))
    there = lambda w: pl.BlockSpec((tile, w), lambda i: (rb * n + i, 0))
    shape = jax.ShapeDtypeStruct
    return pl.pallas_call(
        body,
        grid=(n,),
        in_specs=[
            there(width),
            here(width),
            here(width),
            there(width),
            there(pd),
            pl.BlockSpec((width, 2 * pd), lambda i: (0, column), pipeline_mode=pl.Buffered(1)),
            const_spec(gains.shape),
        ]
        + [any_spec() for _ in prev],
        out_specs=[there(width), here(width), here(width)],
        out_shape=[
            shape((rows, width), BF16),
            shape((half, width), BF16),
            shape((half, width), F32),
        ],
        input_output_aliases={7: 0} if prev else {},
        compiler_params=params(),
        cost_estimate=pl.CostEstimate(
            flops=8 * half * width * pd, bytes_accessed=20 * half * width, transcendentals=0
        ),
        name="ple_both",
    )(combined, ffn_own, ffn_recv, out_grad, ple_in, packed, gains, *prev)


def between_bwd(d_first, combined, dh_own, dh_recv, attn_proj, low, packed, column, gains, prev, rb):
    half, width = d_first.shape
    rows = combined.shape[0]
    lr = low.shape[1]
    tile = half // 2

    def body(df_ref, c_ref, ho_ref, hr_ref, ap_ref, low_ref, w_ref, gain_ref, *refs):
        da_ref, db_ref, dn_ref = refs[-3:]
        d_h2 = ho_ref[...] + hr_ref[...].astype(F32)
        d_comb = df_ref[...] + norm_back(c_ref[...], gain_ref[3:4, :], d_h2)
        d_branch = d_comb * RSQRT_TWO
        db_ref[...] = d_branch
        da_ref[...] = norm_back(ap_ref[...], gain_ref[1:2, :], d_branch).astype(BF16)
        wide = dot_nt(low_ref[...], w_ref[:, lr : 2 * lr])
        d_wide = norm_back(wide, gain_ref[2:3, :], d_branch).astype(BF16)
        d_low = dot(d_wide, w_ref[:, lr : 2 * lr]).astype(BF16)
        dn_ref[...] = d_branch + dot_nt(d_low, w_ref[:, 0:lr])

    n = half // tile
    here = lambda w: pl.BlockSpec((tile, w), lambda i: (i, 0))
    there = lambda w: pl.BlockSpec((tile, w), lambda i: (rb * n + i, 0))
    shape = jax.ShapeDtypeStruct
    return pl.pallas_call(
        body,
        grid=(n,),
        in_specs=[
            here(width),
            there(width),
            here(width),
            here(width),
            there(width),
            there(lr),
            pl.BlockSpec((width, 2 * lr), lambda i: (0, column), pipeline_mode=pl.Buffered(1)),
            const_spec(gains.shape),
        ]
        + [any_spec() for _ in prev],
        out_specs=[here(width), there(width), there(width)],
        out_shape=[
            shape((half, width), BF16),
            shape((rows, width), F32),
            shape((rows, width), F32),
        ],
        input_output_aliases={8: 1, 9: 2} if prev else {},
        compiler_params=params(),
        cost_estimate=pl.CostEstimate(
            flops=6 * half * width * lr, bytes_accessed=26 * half * width, transcendentals=0
        ),
        name="between_bwd",
    )(d_first, combined, dh_own, dh_recv, attn_proj, low, packed, gains, *prev)


def attention_bwd(pieces, turn, packed, wo_column, bo, ao_t, q, k, v, probs, raw, gains, cos, sin):
    length, q_width = q.shape
    width = packed.shape[0]
    heads = q_width // HD
    half_hd = HD // 2
    scale = HD ** (-0.5)
    n_blocks = length // BLK
    span = WIN // BLK
    quarter = pieces[0].shape[0]
    count = len(pieces)

    def unrotate(d, cos_v, sin_v):
        d1, d2 = d[:, :half_hd], d[:, half_hd:]
        return jnp.concatenate([d1 * cos_v + d2 * sin_v, d2 * cos_v - d1 * sin_v], axis=1)

    def body(turn_ref, *refs):
        piece_refs = refs[:count]
        (wo_ref, bo_ref, ao_ref, q_ref, k_ref, v_ref, p_ref, rq_ref, rk_ref, gain_ref, cos_ref,
         sin_ref, out_ref, du_ref, da, du, dk, dv) = refs[count:]
        hh = pl.program_id(0)

        @pl.when(hh == 0)
        def _():
            shift = turn_ref[0] * (length // 2)
            for i, ref in enumerate(piece_refs):
                place = lax.rem(shift + i * quarter, length)
                da[pl.ds(pl.multiple_of(place, quarter), quarter), :] = ref[...]
            got = dot_nt(da[...], bo_ref[...])
            du_ref[...] = got
            du[...] = got.astype(BF16)
            dk[...] = jnp.zeros_like(dk)
            dv[...] = jnp.zeros_like(dv)

        dctx = (dot(da[...], wo_ref[...]) + dot(du[...], ao_ref[...])).astype(BF16)
        cos_v, sin_v = cos_ref[...], sin_ref[...]
        for i in range(n_blocks):
            low, high = max(0, i - span + 1) * BLK, (i + 1) * BLK
            rows = slice(i * BLK, (i + 1) * BLK)
            d_i = dctx[rows]
            p_i = p_ref[0, rows, low:high]
            p_f = p_i.astype(F32)
            dp = dot_nt(d_i, v_ref[low:high, :])
            ds = p_f * (dp - jnp.sum(p_f * dp, axis=-1, keepdims=True))
            ds = ds.astype(BF16)
            dq = dot(ds, k_ref[low:high, :]) * scale
            dk[low:high, :] += dot_tn(ds, q_ref[rows, :])
            dv[low:high, :] += dot_tn(p_i, d_i)
            back = norm_back(rq_ref[rows, :], gain_ref[0:1, :], unrotate(dq, cos_v[rows], sin_v[rows]))
            out_ref[rows, pl.ds(pl.multiple_of(hh * HD, HD), HD)] = back.astype(BF16)

        @pl.when(hh == heads - 1)
        def _():
            back = norm_back(rk_ref[...], gain_ref[1:2, :], unrotate(dk[...] * scale, cos_v, sin_v))
            out_ref[:, q_width : q_width + HD] = back.astype(BF16)
            out_ref[:, q_width + HD : q_width + 2 * HD] = dv[...].astype(BF16)

    shape = jax.ShapeDtypeStruct
    head_block = pl.BlockSpec((length, HD), lambda h: (0, h))
    total = q_width + 2 * HD
    return pl.pallas_call(
        body,
        grid=(heads,),
        in_specs=[pl.BlockSpec(memory_space=pltpu.SMEM)]
        + [const_spec(piece.shape) for piece in pieces]
        + [
            pl.BlockSpec((width, HD), lambda h: (0, wo_column + h)),
            const_spec(bo.shape),
            pl.BlockSpec((RANK, HD), lambda h: (0, h)),
            head_block,
            const_spec(k.shape),
            const_spec(v.shape),
            pl.BlockSpec((1, length, length), lambda h: (h, 0, 0)),
            head_block,
            pl.BlockSpec((length, HD), lambda h: (0, heads), pipeline_mode=pl.Buffered(1)),
            const_spec(gains.shape),
            const_spec(cos.shape),
            const_spec(sin.shape),
        ],
        out_specs=[const_spec((length, total)), const_spec((length, RANK))],
        out_shape=[shape((length, total), BF16), shape((length, RANK), F32)],
        scratch_shapes=[
            pltpu.VMEM((length, width), BF16),
            pltpu.VMEM((length, RANK), BF16),
            pltpu.VMEM((length, HD), F32),
            pltpu.VMEM((length, HD), F32),
        ],
        compiler_params=params(),
        cost_estimate=pl.CostEstimate(
            flops=1024 * 1024,
            bytes_accessed=1024 * 1024,
            transcendentals=0,
        ),
        name="attention_bwd",
    )(turn, *pieces, packed, bo, ao_t, q, k, v, probs, raw, raw, gains, cos, sin)


def final_bwd(x, d_norm, d_branch, dh_own, dh_recv, gains):
    rows, width = x.shape
    tile = rows // 4

    def body(x_ref, dn_ref, db_ref, ho_ref, hr_ref, gain_ref, out_ref):
        total = dn_ref[...] + ho_ref[...] + hr_ref[...].astype(F32)
        out_ref[...] = db_ref[...] + norm_back(x_ref[...].astype(F32), gain_ref[0:1, :], total)

    block = pl.BlockSpec((tile, width), lambda i: (i, 0))
    return pl.pallas_call(
        body,
        grid=(rows // tile,),
        in_specs=[block] * 5 + [const_spec(gains.shape)],
        out_specs=block,
        out_shape=jax.ShapeDtypeStruct((rows, width), F32),
        compiler_params=params(),
        cost_estimate=pl.CostEstimate(
            flops=20 * rows * width, bytes_accessed=20 * rows * width, transcendentals=0
        ),
        name="final_bwd",
    )(x, d_norm, d_branch, dh_own, dh_recv, gains)


def ffn_adapter_sums(got, onehot, units):
    seqs = got.shape[0]
    adapters = onehot.shape[0]
    tile = 512

    def body(hot_ref, got_ref, out_ref, down_ref):
        for a in range(adapters):
            total = hot_ref[a, 0] * got_ref[0].astype(F32)
            for s in range(1, seqs):
                total += hot_ref[a, s] * got_ref[s].astype(F32)
            out_ref[a, :, 0, :] = total[:RANK]
            out_ref[a, :, 1, :] = total[RANK : 2 * RANK]
            down_ref[a] = total[2 * RANK :]

    return pl.pallas_call(
        body,
        grid=(units // tile,),
        in_specs=[
            pl.BlockSpec(memory_space=pltpu.SMEM),
            pl.BlockSpec((seqs, 3 * RANK, tile), lambda i: (0, 0, i)),
        ],
        out_specs=[
            pl.BlockSpec((adapters, RANK, 2, tile), lambda i: (0, 0, 0, i)),
            pl.BlockSpec((adapters, RANK, tile), lambda i: (0, 0, i)),
        ],
        out_shape=[
            jax.ShapeDtypeStruct((adapters, RANK, 2, units), F32),
            jax.ShapeDtypeStruct((adapters, RANK, units), F32),
        ],
        compiler_params=params(),
        cost_estimate=pl.CostEstimate(
            flops=6 * adapters * seqs * RANK * units,
            bytes_accessed=6 * seqs * RANK * units,
            transcendentals=0,
        ),
        name="adapter_sums",
    )(onehot, got)


def rope_tables(length):
    half_dim = HD // 2
    inverse = ROPE_BASE ** (-jnp.arange(half_dim, dtype=F32) / half_dim)
    angles = jnp.arange(length, dtype=F32)[:, None] * inverse[None, :]
    return jnp.cos(angles), jnp.sin(angles)


def rotate(values, cos, sin):
    half_dim = HD // 2
    a, b = values[..., :half_dim], values[..., half_dim:]
    return jnp.concatenate([a * cos - b * sin, b * cos + a * sin], axis=-1)


def on_device(
    hidden_in,
    per_layer_input,
    out_grad,
    adapter_ids,
    weight_qkv,
    weight_attn_out,
    weight_gate_up,
    weight_down,
    laurel_left,
    laurel_right,
    per_layer_gate,
    per_layer_proj,
    norm_gains,
    head_gains,
    adapter_qkv_in,
    adapter_qkv_out,
    adapter_attn_in,
    adapter_attn_out,
    adapter_ffn_in,
    adapter_ffn_out,
    adapter_down_in,
    adapter_down_out,
):
    rows_here, width = hidden_in.shape
    dp = lax.axis_size("dp")
    length = rows_here * 2
    half = rows_here // 2
    per_group = HEADS // KV
    q_width = per_group * HD
    qkv_width = q_width + 2 * HD
    units = weight_down.shape[0]
    blocks = units // UB
    adapters = adapter_qkv_in.shape[0]
    a = adapter_ids[0]
    t = lax.axis_index("tensor")

    def swap(v):
        return lax.ppermute(v, "tensor", [(0, 1), (1, 0)])

    def in_order(own, other):
        first = jnp.where(t == 0, own, other)
        second = jnp.where(t == 0, other, own)
        return jnp.concatenate([first, second], axis=0)

    def mine(v):
        return lax.dynamic_slice_in_dim(v, t * rows_here, rows_here, axis=0)

    def theirs(v):
        return lax.dynamic_slice_in_dim(v, (1 - t) * rows_here, rows_here, axis=0)

    counts = (1, blocks // 2, blocks - 1 - blocks // 2)
    lr = laurel_left.shape[1]
    pd = per_layer_gate.shape[1]
    pack_1 = pack_blocks(
        weight_gate_up, weight_down, 0, counts[0],
        [(weight_qkv[:, 0, :], qkv_width), (weight_attn_out, q_width), (laurel_left.T, lr), (laurel_right, lr)],
        width, "pack_1",
    )
    gather = lambda v: lax.all_gather(v, "dp", axis=0, tiled=True)
    full_1 = gather(pack_1)
    x_peer = swap(hidden_in)
    pack_2 = pack_blocks(
        weight_gate_up, weight_down, counts[0], counts[1],
        [(per_layer_gate, pd), (per_layer_proj, pd)], width, "pack_2",
    )
    pack_3 = pack_blocks(
        weight_gate_up, weight_down, counts[0] + counts[1], counts[2], [], width, "pack_3"
    )
    w_qkv = full_1[:, FB : FB + qkv_width]
    wo_at = FB + qkv_width
    w_o_t = full_1[:, wo_at : wo_at + q_width]
    lau_at = wo_at + q_width
    left = full_1[:, lau_at : lau_at + lr]
    right_t = full_1[:, lau_at + lr : lau_at + 2 * lr]
    ple_column = counts[1] * FB // (2 * pd)

    two = jnp.asarray(2.0, BF16)
    qkv_in = adapter_qkv_in[a]
    raw_out = adapter_qkv_out[a].reshape(RANK, qkv_width) * two
    column = jnp.arange(qkv_width)
    member = (column >= q_width).astype(jnp.int32) + (column >= q_width + HD).astype(jnp.int32)
    pick = (jnp.arange(3)[:, None] == member[None, :]).astype(BF16)
    b_qkv = (pick[:, None, :] * raw_out[None]).reshape(3 * RANK, qkv_width)
    a_o = adapter_attn_in[a]
    b_o = adapter_attn_out[a] * two
    a_ffn = adapter_ffn_in[a]
    b_ffn = adapter_ffn_out[a] * two
    b_unit = jnp.swapaxes(b_ffn.reshape(RANK, 2, blocks, UB), 1, 2)
    side = (jnp.arange(2)[:, None] == jnp.arange(2)[None, :]).astype(BF16)
    bgu = (side[:, None, None, :, None] * b_unit[None]).reshape(2 * RANK, 2 * units)
    ad_t = adapter_down_in[a].T
    b_d = adapter_down_out[a] * two

    cos, sin = rope_tables(length)
    x_float = hidden_in.astype(F32)
    x_norm = normed(x_float, norm_gains[0])
    h_own = x_norm.astype(BF16)
    x_all = in_order(hidden_in, x_peer)
    h_all = normed(x_all.astype(F32), norm_gains[0]).astype(BF16)
    u_qkv = dot(h_all, qkv_in).astype(BF16)
    pack_2, _, h_all, u_qkv, bgu = lax.optimization_barrier((pack_2, full_1, h_all, u_qkv, bgu))
    full_2 = gather(pack_2)
    raw = dot(h_all, w_qkv) + dot(u_qkv, b_qkv)
    q_raw = raw[:, :q_width].reshape(length, per_group, HD)
    k_raw = raw[:, q_width : q_width + HD]
    queries = rotate(normed(q_raw, head_gains[0]), cos[:, None], sin[:, None]).astype(BF16)
    keys = rotate(normed(k_raw, head_gains[1]), cos, sin).astype(BF16)
    values = raw[:, q_width + HD :].astype(BF16)
    index = jnp.arange(length) // BLK
    distance = index[:, None] - index[None, :]
    allowed = ((distance >= 0) & (distance < WIN // BLK))[None]
    scores = jnp.einsum("lqd,md->qlm", queries, keys, preferred_element_type=F32) * HD ** (-0.5)
    scores = jnp.where(allowed, scores, NEG_BIG)
    shifted = jnp.exp(scores - jnp.max(scores, axis=-1, keepdims=True))
    probs = (shifted / jnp.sum(shifted, axis=-1, keepdims=True)).astype(BF16)
    context = (
        jnp.einsum("qlm,md->lqd", probs, values, preferred_element_type=F32)
        .reshape(length, q_width)
        .astype(BF16)
    )
    queries = queries.reshape(length, q_width)
    u_attn_f = dot(context, a_o)
    u_attn = u_attn_f.astype(BF16)
    attn_part = dot_nt(context, w_o_t) + dot(u_attn, b_o)
    attn_recv = swap(theirs(attn_part).astype(BF16))
    attn_proj = mine(attn_part) + attn_recv.astype(F32)
    laurel_low = dot(h_own, left).astype(BF16)
    laurel_wide = dot_nt(laurel_low, right_t)
    combined = (
        x_float + normed(attn_proj, norm_gains[1]) + x_norm + normed(laurel_wide, norm_gains[2])
    ) * RSQRT_TWO
    h2_own = normed(combined, norm_gains[3]).astype(BF16)

    h2_peer = swap(h2_own)
    h2 = jnp.concatenate([h2_own[:half], h2_peer[:half], h2_own[half:], h2_peer[half:]], axis=0)
    u_ffn = dot(h2, a_ffn).astype(BF16)
    pack_3, _, _ = lax.optimization_barrier((pack_3, full_2, h2_own))
    full_3 = gather(pack_3)
    g_pre, u_pre, acc, ud = ffn_fwd(
        h2, full_1, counts[0], 0, u_ffn, bgu, ad_t, b_d, None, None
    )
    g_pre, u_pre, acc, ud = ffn_fwd(
        h2, full_2, counts[1], counts[0], u_ffn, bgu, ad_t, b_d, (acc, ud, g_pre, u_pre), None
    )
    at = counts[0] + counts[1]
    fwd_parts, ud_parts, ple_parts = [], [], []
    for s in range(2):
        g_pre, u_pre, own, peer, ud_s = ffn_fwd(
            h2, full_3, counts[2], at, u_ffn, bgu, ad_t, b_d, (acc, ud, g_pre, u_pre), s
        )
        fwd_parts.append((own, swap(peer)))
        ud_parts.append(ud_s)
    layer_out = []
    for s in range(2):
        own, recv = fwd_parts[s]
        whole, d_ffn_s, d_first_s = ple_both(
            combined, own, recv, out_grad, per_layer_input, full_2, ple_column, norm_gains,
            layer_out, s,
        )
        layer_out = [whole]
        ple_parts.append((d_ffn_s, swap(d_ffn_s), d_first_s))
    common = (g_pre, u_pre, bgu, ad_t, b_d, u_ffn.T, a_ffn.T)
    lau_column = lau_at // (2 * lr)
    (own_0, recv_0, first_0), (own_1, recv_1, first_1) = ple_parts
    d_ffn_parts = [own_0, recv_0, own_1, recv_1]
    *grads_0, d_h2_own_0, d_h2_peer_0 = ffn_bwd(
        own_0, recv_0, (full_1, full_2, full_3), counts, 0, *common, 0, None, True
    )
    d_h2_recv_0 = swap(d_h2_peer_0)
    own_1, _ = lax.optimization_barrier((own_1, d_h2_peer_0))
    dbg_1, dbu_1, gad_1, du_1, acc_1 = ffn_bwd(
        own_1, recv_1, (full_1, full_2), counts[:2], 0, *common, 1, None, False
    )
    d_h2_recv_0, acc_1 = lax.optimization_barrier((d_h2_recv_0, acc_1))
    d_attn_0, *branch = between_bwd(
        first_0, combined, d_h2_own_0, d_h2_recv_0, attn_proj, laurel_low, full_1, lau_column,
        norm_gains, [], 0,
    )
    d_attn_recv_0 = swap(d_attn_0)
    acc_1, _ = lax.optimization_barrier((acc_1, d_attn_0))
    *grads_1, d_h2_own_1, d_h2_peer_1 = ffn_bwd(
        own_1, recv_1, (full_3,), counts[2:], at, *common, 1, (acc_1, du_1, dbg_1, dbu_1, gad_1),
        True,
    )
    d_attn_1, *branch = between_bwd(
        first_1, combined, d_h2_own_1, swap(d_h2_peer_1), attn_proj, laurel_low, full_1,
        lau_column, norm_gains, branch, 1,
    )
    d_branch, d_norm = branch
    bwd_parts = [grads_0, grads_1]
    d_attn_own = [d_attn_0, d_attn_1]
    d_attn_peer = [d_attn_recv_0, swap(d_attn_1)]

    tag = jnp.full((1, 128), a, BF16)

    def onehot_of(ids):
        return (ids[None, :] == jnp.arange(adapters, dtype=F32)[:, None]).astype(BF16)

    def over_sequences(grad):
        return jnp.concatenate(
            [grad.astype(BF16), jnp.broadcast_to(tag, (grad.shape[0], 128))], axis=1
        )

    def gathered(send):
        got = lax.all_gather(send, "dp", axis=0, tiled=False)
        return got, onehot_of(got[:, 0, send.shape[1] - 1].astype(F32))

    def summed(send, m):
        got, onehot = gathered(send)
        return jnp.einsum("as,snm->anm", onehot, got[:, :, :m], preferred_element_type=F32)

    send_ffn = over_sequences(
        jnp.concatenate(
            [
                2.0 * (bwd_parts[0][0] + bwd_parts[1][0]),
                2.0 * (bwd_parts[0][1] + bwd_parts[1][1]),
                bwd_parts[0][2] + bwd_parts[1][2],
            ],
            axis=0,
        )
    )
    send_ffn, d_attn_peer[0] = lax.optimization_barrier((send_ffn, d_attn_peer[0]))
    got_ffn, hot_ffn = gathered(send_ffn)

    d_ffn_all = jnp.concatenate(d_ffn_parts, axis=0)
    du_ffn = jnp.concatenate([bwd_parts[0][3], bwd_parts[1][3]], axis=0).astype(BF16)
    ud_low = jnp.concatenate(ud_parts, axis=0).astype(BF16)
    shared_ffn = jnp.concatenate(
        [dot_tn(h2, du_ffn).astype(BF16), (2.0 * dot_tn(d_ffn_all, ud_low)).astype(BF16)], axis=1
    )
    pieces = d_attn_own + d_attn_peer
    pieces, _, shared_ffn = lax.optimization_barrier((pieces, send_ffn, shared_ffn))
    d_raw, du_attn = attention_bwd(
        pieces, t.astype(jnp.int32).reshape(1), full_1, wo_at // HD, b_o, a_o.T, queries, keys,
        values, probs, raw, head_gains, cos, sin,
    )
    d_u = dot_nt(d_raw, b_qkv).astype(BF16)
    d_h_peer = (dot_nt(theirs(d_raw), w_qkv) + dot_nt(theirs(d_u), qkv_in)).astype(BF16)
    d_h_recv = swap(d_h_peer)
    d_raw, d_u, _, got_ffn = lax.optimization_barrier((d_raw, d_u, d_h_peer, got_ffn))

    d_attn_all = in_order(
        jnp.concatenate(d_attn_own, axis=0), jnp.concatenate(d_attn_peer, axis=0)
    )
    send = jnp.concatenate(
        [
            shared_ffn,
            (2.0 * dot_tn(d_attn_all, u_attn)).astype(BF16),
            dot_tn(h_all, d_u).astype(BF16),
            jnp.broadcast_to(tag[:, :1], (width, 1)),
        ],
        axis=1,
    )
    got = lax.all_to_all(send, ("dp", "tensor"), 0, 0, tiled=True).reshape(2 * dp, -1, send.shape[1])
    grad_b = 2.0 * dot_tn(u_qkv, d_raw)
    grad_heads = jnp.concatenate(
        [
            grad_b[:RANK, :q_width],
            grad_b[RANK : 2 * RANK, q_width : q_width + HD],
            grad_b[2 * RANK :, q_width + HD :],
            dot_tn(du_attn.astype(BF16), context),
        ],
        axis=1,
    )
    sum_heads = summed(over_sequences(grad_heads), qkv_width + q_width)
    d_h_own = dot_nt(mine(d_raw), w_qkv) + dot_nt(mine(d_u), qkv_in)
    out_ffn_out, out_down_in = ffn_adapter_sums(got_ffn, hot_ffn.astype(F32), units)
    d_h_own, out_ffn_out, out_down_in = lax.optimization_barrier((d_h_own, out_ffn_out, out_down_in))
    onehot = onehot_of(got[:, 0, send.shape[1] - 1].astype(F32))
    shared = jnp.einsum("as,snm->anm", onehot, got, preferred_element_type=F32)
    input_grad = final_bwd(hidden_in, d_norm, d_branch, d_h_own, d_h_recv, norm_gains)
    return (
        layer_out[0],
        input_grad,
        shared[:, :, 4 * RANK : 7 * RANK],
        sum_heads[:, :, None, :qkv_width],
        jnp.swapaxes(sum_heads[:, :, qkv_width:], 1, 2),
        jnp.swapaxes(shared[:, :, 3 * RANK : 4 * RANK], 1, 2),
        shared[:, :, : 2 * RANK],
        out_ffn_out,
        jnp.swapaxes(out_down_in, 1, 2),
        jnp.swapaxes(shared[:, :, 2 * RANK : 3 * RANK], 1, 2),
    )


def solution(mesh):
    in_specs = (
        P(("dp", "tensor"), None),
        P(("dp", "tensor"), None),
        P(("dp", "tensor"), None),
        P("dp"),
        P("dp", "tensor", None),
        P("tensor", "dp"),
        P("dp", None, "tensor"),
        P("tensor", "dp"),
        P("dp", None),
        P(None, "dp"),
        P("dp", None),
        P(None, "dp"),
        P(),
        P(),
        P(),
        P(None, None, "tensor", None),
        P(None, "tensor", None),
        P(),
        P(),
        P(None, None, None, "tensor"),
        P(None, "tensor", None),
        P(),
    )
    out_specs = (
        P(("dp", "tensor"), None),
        P(("dp", "tensor"), None),
        P(None, ("dp", "tensor"), None),
        P(None, None, "tensor", None),
        P(None, "tensor", None),
        P(None, None, ("dp", "tensor")),
        P(None, ("dp", "tensor"), None),
        P(None, None, None, "tensor"),
        P(None, "tensor", None),
        P(None, None, ("dp", "tensor")),
    )
    return jax.shard_map(
        on_device, mesh=mesh, in_specs=in_specs, out_specs=out_specs, check_vma=False
    )
```

```python
import functools

import jax
import jax.numpy as jnp
from jax import lax
from jax.experimental import pallas as pl
from jax.experimental.pallas import tpu as pltpu
from jax.sharding import PartitionSpec as P

HEADS = 8
KV = 2
HD = 256
WIN = 512
BLK = 256
RANK = 16
UB = 512
GB = 2 * UB

NORM_EPSILON = 1e-06
RSQRT_TWO = 0.7071067811865476
ROPE_BASE = 10000.0
NEG_BIG = -1e30
GELU_A = 0.7978845608028654
GELU_B = 0.044715

F32 = jnp.float32
BF16 = jnp.bfloat16
VMEM_LIMIT = 58 * 1024 * 1024
DOWN_CHUNK = 512


def dot(a, b):
    return lax.dot_general(a, b, (((1,), (0,)), ((), ())), preferred_element_type=F32)


def dot_nt(a, b):
    return lax.dot_general(a, b, (((1,), (1,)), ((), ())), preferred_element_type=F32)


def dot_tn(a, b):
    return lax.dot_general(a, b, (((0,), (0,)), ((), ())), preferred_element_type=F32)


def inv_rms(v):
    return lax.rsqrt(jnp.mean(v * v, axis=-1, keepdims=True) + NORM_EPSILON)


def normed(v, gains):
    return v * inv_rms(v) * gains


def norm_back(v, gains, cotangent):
    r = inv_rms(v)
    gc = gains * cotangent
    return r * gc - v * (r * r * r * jnp.mean(v * gc, axis=-1, keepdims=True))


def gelu_tanh(v):
    return 0.5 * v * (1.0 + jnp.tanh(GELU_A * (v + GELU_B * v * v * v)))


def gelu_both(v):
    v2 = v * v
    th = jnp.tanh(GELU_A * v * (1.0 + GELU_B * v2))
    half = 0.5 * (1.0 + th)
    slope = half + 0.5 * v * (1.0 - th * th) * (GELU_A * (1.0 + 3.0 * GELU_B * v2))
    return v * half, slope


def const_spec(shape):
    return pl.BlockSpec(shape, lambda *_: (0,) * len(shape), pipeline_mode=pl.Buffered(1))


def any_spec():
    return pl.BlockSpec(memory_space=pl.ANY)


def params():
    return pltpu.CompilerParams(vmem_limit_bytes=VMEM_LIMIT)


def pack_shards(gate_up, first, count, rest, rows, name):
    width = count * GB + sum(n for _, n in rest)

    def body(*refs):
        out = refs[-1]
        for b in range(count):
            cs = slice(b * UB, (b + 1) * UB)
            out[:, b * GB : b * GB + UB] = refs[0][:, 0, cs]
            out[:, b * GB + UB : (b + 1) * GB] = refs[0][:, 1, cs]
        at = count * GB
        for ref, (value, n) in zip(refs[1 if count else 0 : -1], rest):
            out[:, at : at + n] = ref[...] if value.shape == (rows, n) else ref[...].T
            at += n

    block = (pl.Element(rows), pl.Element(2), pl.Element(count * UB))
    gate_spec = [pl.BlockSpec(block, lambda i: (0, 0, first * UB))] if count else []
    return pl.pallas_call(
        body,
        grid=(1,),
        in_specs=gate_spec + [const_spec(v.shape) for v, _ in rest],
        out_specs=const_spec((rows, width)),
        out_shape=jax.ShapeDtypeStruct((rows, width), BF16),
        compiler_params=params(),
        name=name,
    )(*([gate_up] if count else []), *[v for v, _ in rest])


def ffn_up(h2, packed, blocks, first, u_low, bgu, ad_t, prev):
    rows, width = h2.shape
    units = ad_t.shape[1]
    tile = rows // 2
    sub = 256

    def body(*refs):
        h_ref, w_ref, ul_ref, bgu_ref, ad_ref = refs[:5]
        g_out, u_out, hid_out, ud_out = refs[-4:]
        j = pl.program_id(0)

        @pl.when(j == 0)
        def _():
            if prev is None:
                ud_out[...] = jnp.zeros_like(ud_out)
            else:
                ud_out[...] = refs[5][...]

        for k in range(rows // tile):
            at_rows = slice(k * tile, (k + 1) * tile)
            h = h_ref[at_rows, :]
            ul = ul_ref[at_rows, :]
            for n in range(UB // sub):
                cs = slice(n * sub, (n + 1) * sub)
                us = slice(UB + n * sub, UB + (n + 1) * sub)
                g = dot(h, w_ref[:, cs]) + dot(ul, bgu_ref[:, cs])
                u = dot(h, w_ref[:, us]) + dot(ul, bgu_ref[:, us])
                g_out[at_rows, cs] = g.astype(BF16)
                u_out[at_rows, cs] = u.astype(BF16)
                hid_out[at_rows, cs] = (gelu_tanh(g) * u).astype(BF16)
            ud_out[at_rows, :] += dot_nt(hid_out[at_rows, :], ad_ref[...])

    in_specs = [
        const_spec((rows, width)),
        pl.BlockSpec((width, GB), lambda j: (0, j)),
        const_spec((rows, 2 * RANK)),
        pl.BlockSpec((2 * RANK, GB), lambda j: (0, first + j)),
        pl.BlockSpec((RANK, UB), lambda j: (0, first + j)),
    ]
    args = [h2, packed, u_low, bgu, ad_t]
    aliases = {}
    if prev is not None:
        in_specs += [const_spec((rows, RANK)), any_spec(), any_spec(), any_spec()]
        args += list(prev)
        aliases = {6: 0, 7: 1, 8: 2}
    unit_block = pl.BlockSpec((rows, UB), lambda j: (0, first + j))
    shape = jax.ShapeDtypeStruct
    g, u, hidden, ud = pl.pallas_call(
        body,
        grid=(blocks,),
        in_specs=in_specs,
        out_specs=[unit_block] * 3 + [const_spec((rows, RANK))],
        out_shape=[shape((rows, units), BF16)] * 3 + [shape((rows, RANK), F32)],
        input_output_aliases=aliases,
        compiler_params=params(),
        cost_estimate=pl.CostEstimate(
            flops=4 * rows * width * UB * blocks,
            bytes_accessed=2 * width * GB * blocks,
            transcendentals=rows * UB * blocks,
        ),
        name="ffn_up",
    )(*args)
    return ud, g, u, hidden


def ffn_down(hidden, packed, ud, bd, rb):
    rows, units = hidden.shape
    width = packed.shape[0]
    r = rows // 2
    half = r // 2
    chunk = DOWN_CHUNK

    def body(h_ref, w_ref, ud_ref, bd_ref, own_out, peer_out):
        total = dot_nt(h_ref[...], w_ref[...]) + dot(ud_ref[...].astype(BF16), bd_ref[...])
        own_out[...] = total[:half]
        peer_out[...] = total[half:].astype(BF16)

    row_const = lambda n: pl.BlockSpec((r, n), lambda j: (rb, 0), pipeline_mode=pl.Buffered(1))
    column = pl.BlockSpec((half, chunk), lambda j: (0, j))
    return pl.pallas_call(
        body,
        grid=(width // chunk,),
        in_specs=[
            row_const(units),
            pl.BlockSpec((chunk, units), lambda j: (j, 0)),
            row_const(RANK),
            pl.BlockSpec((RANK, chunk), lambda j: (0, j)),
        ],
        out_specs=[column, column],
        out_shape=[
            jax.ShapeDtypeStruct((half, width), F32),
            jax.ShapeDtypeStruct((half, width), BF16),
        ],
        compiler_params=params(),
        cost_estimate=pl.CostEstimate(
            flops=2 * r * width * units, bytes_accessed=2 * width * units, transcendentals=0
        ),
        name="ffn_down",
    )(hidden, packed, ud, bd)


def ffn_bwd(own, peer, packs, split, first, blocks, g_pre, u_pre, bgu, ad_t, bd, u_t, a_in_t, rb, base, prev, last):
    half, width = own.shape
    r = 2 * half
    units = ad_t.shape[1]
    sub = 256

    def body(*refs):
        own_ref, peer_ref, g_ref, u_ref, bgu_ref, ad_ref, bd_ref, ut_ref, ain_ref = refs[:9]
        pack_refs = refs[9 : 9 + len(packs)]
        at = 9 + len(packs)
        if base is not None:
            base_ref = refs[at]
            at += 1
        if prev is not None:
            acc_in, du_in = refs[at : at + 2]
            at += 3
        grad_out, du_out = refs[at : at + 2]
        if last:
            own_out, peer_out = refs[at + 2 : at + 4]
            at += 4
        else:
            acc_out = refs[at + 2]
            at += 3
        df, acc, wbuf, dd, du, dgu, hs, sem, acc_sem = refs[at:]
        j = pl.program_id(0)
        slot = lax.rem(j, 2)

        def copy(ref, column, where, part):
            lo, n = ((2 * UB, UB), (0, 2 * UB))[part]
            return pltpu.make_async_copy(
                ref.at[:, pl.ds(column, n)], wbuf.at[where, :, pl.ds(lo, n)], sem.at[where, part]
            )

        def fetch(step, where):
            block = first + step
            copy(pack_refs[2], pl.multiple_of(block * UB, UB), where, 0).start()

            @pl.when(block < split)
            def _():
                copy(pack_refs[0], pl.multiple_of(block * GB, GB), where, 1).start()

            @pl.when(block >= split)
            def _():
                copy(pack_refs[1], pl.multiple_of((block - split) * GB, GB), where, 1).start()

        @pl.when(j == 0)
        def _():
            fetch(j, 0)
            df[0:half, :] = own_ref[...]
            df[half:r, :] = peer_ref[...]
            if prev is None:
                acc[...] = jnp.zeros_like(acc)
                du[...] = jnp.zeros_like(du)
            else:
                pltpu.make_async_copy(acc_in, acc, acc_sem).start()
                du[...] = du_in[...]
            dd[...] = dot_nt(df[...], bd_ref[...]).astype(BF16)

        @pl.when(j + 1 < blocks)
        def _():
            fetch(j + 1, 1 - slot)

        copy(pack_refs[2], 0, slot, 0).wait()
        for n in range(UB // sub):
            cs = slice(n * sub, (n + 1) * sub)
            dh = dot(df[...], wbuf[slot, :, 2 * UB + n * sub : 2 * UB + (n + 1) * sub])
            dh += dot(dd[...], ad_ref[:, cs])
            g = g_ref[:, cs].astype(F32)
            u = u_ref[:, cs].astype(F32)
            act, slope = gelu_both(g)
            dgu[:, cs] = (dh * u * slope).astype(BF16)
            dgu[:, UB + n * sub : UB + (n + 1) * sub] = (dh * act).astype(BF16)
            hs[:, cs] = (act * u).astype(BF16)
        copy(pack_refs[0], 0, slot, 1).wait()
        if prev is not None:

            @pl.when(j == 0)
            def _():
                pltpu.make_async_copy(acc_in, acc, acc_sem).wait()

        d_both = dgu[...]
        for c in range(width // 512):
            cc = slice(c * 512, (c + 1) * 512)
            acc[:, cc] += dot_nt(d_both, wbuf[slot, cc, 0 : 2 * UB])
        du[...] += dot_nt(d_both, bgu_ref[...])
        both = dot(ut_ref[...], d_both)
        rows = (2.0 * both[:RANK, :UB], 2.0 * both[RANK:, UB:], dot_tn(dd[...], hs[...]))
        for m, row in enumerate(rows):
            ms = slice(m * RANK, (m + 1) * RANK)
            if base is not None:
                row = row + base_ref[ms, :]
            grad_out[ms, :] = row.astype(grad_out.dtype)

        @pl.when(j == blocks - 1)
        def _():
            du_out[...] = du[...]
            if last:
                total = acc[...] + dot(du[...].astype(BF16), ain_ref[...])
                own_out[...] = total[:half]
                peer_out[...] = total[half:].astype(BF16)
            else:
                acc_out[...] = acc[...]

    rows_block = lambda: pl.BlockSpec((r, UB), lambda j: (rb, first + j))
    unit_block = lambda: pl.BlockSpec((RANK, UB), lambda j: (0, first + j))
    shape = jax.ShapeDtypeStruct
    in_specs = [
        const_spec((half, width)),
        const_spec((half, width)),
        rows_block(),
        rows_block(),
        pl.BlockSpec((2 * RANK, 2 * UB), lambda j: (0, first + j)),
        unit_block(),
        const_spec((RANK, width)),
        pl.BlockSpec((2 * RANK, r), lambda j: (0, rb), pipeline_mode=pl.Buffered(1)),
        const_spec((2 * RANK, width)),
    ] + [any_spec() for _ in packs]
    args = [own, peer, g_pre, u_pre, bgu, ad_t, bd, u_t, a_in_t, *packs]
    aliases = {}
    grad_block = lambda: pl.BlockSpec((3 * RANK, UB), lambda j: (0, first + j))
    if base is not None:
        in_specs.append(grad_block())
        args.append(base)
    if prev is not None:
        aliases = {len(args) + 2: 0}
        in_specs += [any_spec(), const_spec((r, 2 * RANK)), any_spec()]
        args += list(prev)
    out_specs = [grad_block(), const_spec((r, 2 * RANK))]
    out_shape = [shape((3 * RANK, units), F32 if base is None else BF16), shape((r, 2 * RANK), F32)]
    if last:
        out_specs += [const_spec((half, width)), const_spec((half, width))]
        out_shape += [shape((half, width), F32), shape((half, width), BF16)]
    else:
        out_specs += [const_spec((r, width))]
        out_shape += [shape((r, width), F32)]
    return pl.pallas_call(
        body,
        grid=(blocks,),
        in_specs=in_specs,
        out_specs=out_specs,
        out_shape=out_shape,
        scratch_shapes=[
            pltpu.VMEM((r, width), BF16),
            pltpu.VMEM((r, width), F32),
            pltpu.VMEM((2, width, 3 * UB), BF16),
            pltpu.VMEM((r, RANK), BF16),
            pltpu.VMEM((r, 2 * RANK), F32),
            pltpu.VMEM((r, 2 * UB), BF16),
            pltpu.VMEM((r, UB), BF16),
            pltpu.SemaphoreType.DMA((2, 2)),
            pltpu.SemaphoreType.DMA,
        ],
        input_output_aliases=aliases,
        compiler_params=params(),
        cost_estimate=pl.CostEstimate(
            flops=6 * r * width * UB * blocks,
            bytes_accessed=6 * width * UB * blocks,
            transcendentals=r * UB * blocks,
        ),
        name="ffn_bwd",
    )(*args)


def ple_both(combined, ffn_own, ffn_recv, out_grad, ple_in, packed, column, gains, prev, rb):
    half, width = ffn_own.shape
    rows = combined.shape[0]
    pd = ple_in.shape[1]
    tile = half // 2

    def body(c_ref, fo_ref, fr_ref, og_ref, pi_ref, w_ref, gain_ref, *refs):
        out_ref, dffn_ref, dfirst_ref = refs[-3:]
        ffn = fo_ref[...] + fr_ref[...].astype(F32)
        y = c_ref[...] + normed(ffn, gain_ref[4:5, :])
        pre = dot(y.astype(BF16), w_ref[:, 0:pd])
        side = pi_ref[...].astype(F32)
        act, slope = gelu_both(pre)
        wide = dot_nt((act * side).astype(BF16), w_ref[:, pd : 2 * pd])
        out_ref[...] = (y + normed(wide, gain_ref[5:6, :])).astype(BF16)
        cot = og_ref[...].astype(F32)
        d_wide = norm_back(wide, gain_ref[5:6, :], cot).astype(BF16)
        d_pre = (dot(d_wide, w_ref[:, pd : 2 * pd]) * side * slope).astype(BF16)
        d_first = cot + dot_nt(d_pre, w_ref[:, 0:pd])
        dfirst_ref[...] = d_first
        dffn_ref[...] = norm_back(ffn, gain_ref[4:5, :], d_first).astype(BF16)

    n = half // tile
    here = lambda w: pl.BlockSpec((tile, w), lambda i: (i, 0))
    there = lambda w: pl.BlockSpec((tile, w), lambda i: (rb * n + i, 0))
    shape = jax.ShapeDtypeStruct
    return pl.pallas_call(
        body,
        grid=(n,),
        in_specs=[
            there(width),
            here(width),
            here(width),
            there(width),
            there(pd),
            pl.BlockSpec((width, 2 * pd), lambda i: (0, column), pipeline_mode=pl.Buffered(1)),
            const_spec(gains.shape),
        ]
        + [any_spec() for _ in prev],
        out_specs=[there(width), here(width), here(width)],
        out_shape=[
            shape((rows, width), BF16),
            shape((half, width), BF16),
            shape((half, width), F32),
        ],
        input_output_aliases={7: 0} if prev else {},
        compiler_params=params(),
        cost_estimate=pl.CostEstimate(
            flops=8 * half * width * pd, bytes_accessed=20 * half * width, transcendentals=0
        ),
        name="ple_both",
    )(combined, ffn_own, ffn_recv, out_grad, ple_in, packed, gains, *prev)


def between_bwd(d_first, combined, dh_own, dh_recv, attn_proj, low, packed, column, gains, prev, rb):
    half, width = d_first.shape
    rows = combined.shape[0]
    lr = low.shape[1]
    tile = half // 2

    def body(df_ref, c_ref, ho_ref, hr_ref, ap_ref, low_ref, w_ref, gain_ref, *refs):
        da_ref, db_ref, dn_ref = refs[-3:]
        d_h2 = ho_ref[...] + hr_ref[...].astype(F32)
        d_comb = df_ref[...] + norm_back(c_ref[...], gain_ref[3:4, :], d_h2)
        d_branch = d_comb * RSQRT_TWO
        db_ref[...] = d_branch
        da_ref[...] = norm_back(ap_ref[...], gain_ref[1:2, :], d_branch).astype(BF16)
        wide = dot_nt(low_ref[...], w_ref[:, lr : 2 * lr])
        d_wide = norm_back(wide, gain_ref[2:3, :], d_branch).astype(BF16)
        d_low = dot(d_wide, w_ref[:, lr : 2 * lr]).astype(BF16)
        dn_ref[...] = d_branch + dot_nt(d_low, w_ref[:, 0:lr])

    n = half // tile
    here = lambda w: pl.BlockSpec((tile, w), lambda i: (i, 0))
    there = lambda w: pl.BlockSpec((tile, w), lambda i: (rb * n + i, 0))
    shape = jax.ShapeDtypeStruct
    return pl.pallas_call(
        body,
        grid=(n,),
        in_specs=[
            here(width),
            there(width),
            here(width),
            here(width),
            there(width),
            there(lr),
            pl.BlockSpec((width, 2 * lr), lambda i: (0, column), pipeline_mode=pl.Buffered(1)),
            const_spec(gains.shape),
        ]
        + [any_spec() for _ in prev],
        out_specs=[here(width), there(width), there(width)],
        out_shape=[
            shape((half, width), BF16),
            shape((rows, width), F32),
            shape((rows, width), F32),
        ],
        input_output_aliases={8: 1, 9: 2} if prev else {},
        compiler_params=params(),
        cost_estimate=pl.CostEstimate(
            flops=6 * half * width * lr, bytes_accessed=26 * half * width, transcendentals=0
        ),
        name="between_bwd",
    )(d_first, combined, dh_own, dh_recv, attn_proj, low, packed, gains, *prev)


def attention_bwd(pieces, turn, packed, qkv_column, wo_column, bo, ao_t, q, k, v, probs, raw, gains, cos, sin,
                  context, u_t, b_qkv, a_in_t):
    length, q_width = q.shape
    width = packed.shape[0]
    heads = q_width // HD
    half_hd = HD // 2
    scale = HD ** (-0.5)
    n_blocks = length // BLK
    span = WIN // BLK
    quarter = pieces[0].shape[0]
    count = len(pieces)
    total = q_width + 2 * HD
    here = length // 2

    def unrotate(d, cos_v, sin_v):
        d1, d2 = d[:, :half_hd], d[:, half_hd:]
        return jnp.concatenate([d1 * cos_v + d2 * sin_v, d2 * cos_v - d1 * sin_v], axis=1)

    def body(turn_ref, *refs):
        piece_refs = refs[:count]
        (wo_ref, w_any, bo_ref, ao_ref, q_ref, k_ref, v_ref, p_ref, rq_ref, rk_ref, gain_ref, cos_ref,
         sin_ref, ctx_ref, ut_ref, b_ref, ain_ref, peer_0, peer_1, draw, du_out, heads_out,
         da, du, dk, dv, wq, sem) = refs[count:]
        hh = pl.program_id(0)
        weights = pltpu.make_async_copy(w_any.at[:, pl.ds(qkv_column, total)], wq, sem)

        @pl.when(hh == 0)
        def _():
            weights.start()
            shift = turn_ref[0] * here
            for i, ref in enumerate(piece_refs):
                place = lax.rem(shift + i * quarter, length)
                da[pl.ds(pl.multiple_of(place, quarter), quarter), :] = ref[...]
            du[...] = dot_nt(da[...], bo_ref[...]).astype(BF16)
            dk[...] = jnp.zeros_like(dk)
            dv[...] = jnp.zeros_like(dv)

        dctx = (dot(da[...], wo_ref[...]) + dot(du[...], ao_ref[...])).astype(BF16)
        cos_v, sin_v = cos_ref[...], sin_ref[...]
        column = pl.multiple_of(hh * HD, HD)
        for i in range(n_blocks):
            low, high = max(0, i - span + 1) * BLK, (i + 1) * BLK
            rows = slice(i * BLK, (i + 1) * BLK)
            d_i = dctx[rows]
            p_i = p_ref[0, rows, low:high]
            p_f = p_i.astype(F32)
            dp = dot_nt(d_i, v_ref[low:high, :])
            ds = p_f * (dp - jnp.sum(p_f * dp, axis=-1, keepdims=True))
            ds = ds.astype(BF16)
            dq = dot(ds, k_ref[low:high, :]) * scale
            dk[low:high, :] += dot_tn(ds, q_ref[rows, :])
            dv[low:high, :] += dot_tn(p_i, d_i)
            back = norm_back(rq_ref[rows, :], gain_ref[0:1, :], unrotate(dq, cos_v[rows], sin_v[rows]))
            draw[rows, pl.ds(column, HD)] = back.astype(BF16)
        heads_out[:, pl.ds(column, HD)] = (
            2.0 * dot(ut_ref[0:RANK, :], draw[:, pl.ds(column, HD)])
        ).astype(BF16)
        heads_out[:, pl.ds(pl.multiple_of(total + hh * HD, HD), HD)] = dot_tn(
            du[...], ctx_ref[...]
        ).astype(BF16)

        @pl.when(hh == heads - 1)
        def _():
            back = norm_back(rk_ref[...], gain_ref[1:2, :], unrotate(dk[...] * scale, cos_v, sin_v))
            at_k, at_v = slice(q_width, q_width + HD), slice(q_width + HD, total)
            draw[:, at_k] = back.astype(BF16)
            draw[:, at_v] = dv[...].astype(BF16)
            for m, where in ((1, at_k), (2, at_v)):
                got = dot(ut_ref[m * RANK : (m + 1) * RANK, :], draw[:, where])
                heads_out[:, where] = (2.0 * got).astype(BF16)
            du_out[...] = dot_nt(draw[...], b_ref[...]).astype(BF16)
            weights.wait()
            theirs = pl.multiple_of((1 - turn_ref[0]) * here, here)
            d_rows = draw[pl.ds(theirs, here), :]
            u_rows = du_out[pl.ds(theirs, here), :]
            for c in range(width // 512):
                cc = slice(c * 512, (c + 1) * 512)
                got = dot_nt(d_rows, wq[cc, :]) + dot(u_rows, ain_ref[:, cc])
                peer_0[:, cc] = got[: here // 2].astype(BF16)
                peer_1[:, cc] = got[here // 2 :].astype(BF16)

    shape = jax.ShapeDtypeStruct
    head_block = lambda: pl.BlockSpec((length, HD), lambda h: (0, h))
    return pl.pallas_call(
        body,
        grid=(heads,),
        in_specs=[pl.BlockSpec(memory_space=pltpu.SMEM)]
        + [const_spec(piece.shape) for piece in pieces]
        + [
            pl.BlockSpec((width, HD), lambda h: (0, wo_column + h)),
            any_spec(),
            const_spec(bo.shape),
            pl.BlockSpec((RANK, HD), lambda h: (0, h)),
            head_block(),
            const_spec(k.shape),
            const_spec(v.shape),
            pl.BlockSpec((1, length, length), lambda h: (h, 0, 0)),
            head_block(),
            pl.BlockSpec((length, HD), lambda h: (0, heads), pipeline_mode=pl.Buffered(1)),
            const_spec(gains.shape),
            const_spec(cos.shape),
            const_spec(sin.shape),
            head_block(),
            const_spec(u_t.shape),
            const_spec(b_qkv.shape),
            const_spec(a_in_t.shape),
        ],
        out_specs=[
            const_spec((here // 2, width)),
            const_spec((here // 2, width)),
            const_spec((length, total)),
            const_spec((length, 3 * RANK)),
            const_spec((RANK, total + q_width)),
        ],
        out_shape=[
            shape((here // 2, width), BF16),
            shape((here // 2, width), BF16),
            shape((length, total), BF16),
            shape((length, 3 * RANK), BF16),
            shape((RANK, total + q_width), BF16),
        ],
        scratch_shapes=[
            pltpu.VMEM((length, width), BF16),
            pltpu.VMEM((length, RANK), BF16),
            pltpu.VMEM((length, HD), F32),
            pltpu.VMEM((length, HD), F32),
            pltpu.VMEM((width, total), BF16),
            pltpu.SemaphoreType.DMA,
        ],
        compiler_params=params(),
        cost_estimate=pl.CostEstimate(flops=1024 * 1024, bytes_accessed=1024 * 1024, transcendentals=0),
        name="attention_bwd",
    )(turn, *pieces, packed, packed, bo, ao_t, q, k, v, probs, raw, raw, gains, cos, sin, context, u_t, b_qkv,
      a_in_t)


def final_bwd(x, d_norm, d_branch, dh_own, dh_recv, gains, prev, rb):
    rows, width = x.shape
    half = rows // 2
    tile = half // 2

    def body(x_ref, dn_ref, db_ref, ho_ref, hr_ref, gain_ref, *refs):
        out_ref = refs[-1]
        total = dn_ref[...] + ho_ref[...] + hr_ref[...].astype(F32)
        out_ref[...] = db_ref[...] + norm_back(x_ref[...].astype(F32), gain_ref[0:1, :], total)

    n = half // tile
    here = pl.BlockSpec((tile, width), lambda i: (i, 0))
    there = pl.BlockSpec((tile, width), lambda i: (rb * n + i, 0))
    return pl.pallas_call(
        body,
        grid=(n,),
        in_specs=[there] * 4 + [here, const_spec(gains.shape)] + [any_spec() for _ in prev],
        out_specs=there,
        out_shape=jax.ShapeDtypeStruct((rows, width), F32),
        input_output_aliases={6: 0} if prev else {},
        compiler_params=params(),
        cost_estimate=pl.CostEstimate(
            flops=20 * half * width, bytes_accessed=20 * half * width, transcendentals=0
        ),
        name="final_bwd",
    )(x, d_norm, d_branch, dh_own, dh_recv, gains, *prev)


def add_by_adapter(ids_ref, got_ref, total, seqs, share):
    total[...] = jnp.zeros_like(total)

    def step(i, carry):
        where = ids_ref[i // share]
        total[where] += got_ref[i].astype(F32)
        return carry

    lax.fori_loop(0, seqs, step, 0)


def ffn_adapter_sums(got, ids, adapters, units):
    seqs = got.shape[0]
    tile = 1024

    def body(ids_ref, got_ref, out_ref, down_ref, total):
        add_by_adapter(ids_ref, got_ref, total, seqs, 1)
        out_ref[:, :, 0, :] = total[:, :RANK, :]
        out_ref[:, :, 1, :] = total[:, RANK : 2 * RANK, :]
        down_ref[...] = total[:, 2 * RANK :, :]

    return pl.pallas_call(
        body,
        grid=(units // tile,),
        in_specs=[
            pl.BlockSpec(memory_space=pltpu.SMEM),
            pl.BlockSpec((seqs, 3 * RANK, tile), lambda i: (0, 0, i)),
        ],
        out_specs=[
            pl.BlockSpec((adapters, RANK, 2, tile), lambda i: (0, 0, 0, i)),
            pl.BlockSpec((adapters, RANK, tile), lambda i: (0, 0, i)),
        ],
        out_shape=[
            jax.ShapeDtypeStruct((adapters, RANK, 2, units), F32),
            jax.ShapeDtypeStruct((adapters, RANK, units), F32),
        ],
        scratch_shapes=[pltpu.VMEM((adapters, 3 * RANK, tile), F32)],
        compiler_params=params(),
        cost_estimate=pl.CostEstimate(
            flops=6 * seqs * RANK * units, bytes_accessed=6 * seqs * RANK * units, transcendentals=0
        ),
        name="adapter_sums",
    )(ids, got)


def shared_sums(got, ids, adapters):
    seqs, rows, columns = got.shape
    cuts = (2 * RANK, RANK, RANK, 3 * RANK)

    def body(ids_ref, got_ref, *refs):
        total = refs[-1]
        add_by_adapter(ids_ref, got_ref, total, seqs, 2)
        for n in range(adapters):
            flipped = total[n].T
            at = 0
            for ref, cut in zip(refs, cuts):
                ref[n] = flipped[at : at + cut, :]
                at += cut

    return pl.pallas_call(
        body,
        grid=(1,),
        in_specs=[pl.BlockSpec(memory_space=pltpu.SMEM), const_spec(got.shape)],
        out_specs=[const_spec((adapters, cut, rows)) for cut in cuts],
        out_shape=[jax.ShapeDtypeStruct((adapters, cut, rows), F32) for cut in cuts],
        scratch_shapes=[pltpu.VMEM((adapters, rows, columns), F32)],
        compiler_params=params(),
        name="shared_sums",
    )(ids, got)


def head_sums(got, ids, adapters, qkv_width):
    seqs, rank, columns = got.shape
    rest = columns - qkv_width

    def body(ids_ref, got_ref, qkv_ref, attn_ref, total):
        add_by_adapter(ids_ref, got_ref, total, seqs, 1)
        qkv_ref[:, :, 0, :] = total[:, :, :qkv_width]
        attn_ref[...] = total[:, :, qkv_width:]

    return pl.pallas_call(
        body,
        grid=(1,),
        in_specs=[pl.BlockSpec(memory_space=pltpu.SMEM), const_spec(got.shape)],
        out_specs=[const_spec((adapters, rank, 1, qkv_width)), const_spec((adapters, rank, rest))],
        out_shape=[
            jax.ShapeDtypeStruct((adapters, rank, 1, qkv_width), F32),
            jax.ShapeDtypeStruct((adapters, rank, rest), F32),
        ],
        scratch_shapes=[pltpu.VMEM((adapters, rank, columns), F32)],
        compiler_params=params(),
        name="head_sums",
    )(ids, got)


def rope_tables(length):
    half_dim = HD // 2
    inverse = ROPE_BASE ** (-jnp.arange(half_dim, dtype=F32) / half_dim)
    angles = jnp.arange(length, dtype=F32)[:, None] * inverse[None, :]
    return jnp.cos(angles), jnp.sin(angles)


def rotate(values, cos, sin):
    half_dim = HD // 2
    a, b = values[..., :half_dim], values[..., half_dim:]
    return jnp.concatenate([a * cos - b * sin, b * cos + a * sin], axis=-1)


def on_device(
    hidden_in,
    per_layer_input,
    out_grad,
    adapter_ids,
    weight_qkv,
    weight_attn_out,
    weight_gate_up,
    weight_down,
    laurel_left,
    laurel_right,
    per_layer_gate,
    per_layer_proj,
    norm_gains,
    head_gains,
    adapter_qkv_in,
    adapter_qkv_out,
    adapter_attn_in,
    adapter_attn_out,
    adapter_ffn_in,
    adapter_ffn_out,
    adapter_down_in,
    adapter_down_out,
):
    rows_here, width = hidden_in.shape
    dp = lax.axis_size("dp")
    length = rows_here * 2
    half = rows_here // 2
    per_group = HEADS // KV
    q_width = per_group * HD
    qkv_width = q_width + 2 * HD
    units = weight_down.shape[0]
    blocks = units // UB
    adapters = adapter_qkv_in.shape[0]
    a = adapter_ids[0]
    t = lax.axis_index("tensor")

    def swap(v):
        return lax.ppermute(v, "tensor", [(0, 1), (1, 0)])

    def in_order(own, other):
        first = jnp.where(t == 0, own, other)
        second = jnp.where(t == 0, other, own)
        return jnp.concatenate([first, second], axis=0)

    def mine(v):
        return lax.dynamic_slice_in_dim(v, t * rows_here, rows_here, axis=0)

    def theirs(v):
        return lax.dynamic_slice_in_dim(v, (1 - t) * rows_here, rows_here, axis=0)

    split = blocks // 4
    rows_packed = laurel_left.shape[0]
    lr = laurel_left.shape[1]
    pd = per_layer_gate.shape[1]
    pack_1 = pack_shards(
        weight_gate_up, 0, split,
        [(weight_qkv[:, 0, :], qkv_width), (weight_attn_out, q_width), (laurel_left.T, lr), (laurel_right, lr)],
        rows_packed, "pack_1",
    )
    gather = lambda v: lax.all_gather(v, "dp", axis=0, tiled=True)
    full_1 = gather(pack_1)
    x_peer = swap(hidden_in)
    pack_2 = pack_shards(weight_gate_up, split, blocks - split, [], rows_packed, "pack_2")
    pack_3 = pack_shards(
        None, 0, 0, [(weight_down, units), (per_layer_gate, pd), (per_layer_proj, pd)],
        rows_packed, "pack_3",
    )
    qkv_at = split * GB
    w_qkv = full_1[:, qkv_at : qkv_at + qkv_width]
    wo_at = qkv_at + qkv_width
    w_o_t = full_1[:, wo_at : wo_at + q_width]
    lau_at = wo_at + q_width
    left = full_1[:, lau_at : lau_at + lr]
    right_t = full_1[:, lau_at + lr : lau_at + 2 * lr]
    ple_column = units // (2 * pd)

    two = jnp.asarray(2.0, BF16)
    qkv_in = adapter_qkv_in[a]
    raw_out = adapter_qkv_out[a].reshape(RANK, qkv_width) * two
    column = jnp.arange(qkv_width)
    member = (column >= q_width).astype(jnp.int32) + (column >= q_width + HD).astype(jnp.int32)
    pick = (jnp.arange(3)[:, None] == member[None, :]).astype(BF16)
    b_qkv = (pick[:, None, :] * raw_out[None]).reshape(3 * RANK, qkv_width)
    a_o = adapter_attn_in[a]
    b_o = adapter_attn_out[a] * two
    a_ffn = adapter_ffn_in[a]
    b_ffn = adapter_ffn_out[a] * two
    b_unit = jnp.swapaxes(b_ffn.reshape(RANK, 2, blocks, UB), 1, 2)
    side = (jnp.arange(2)[:, None] == jnp.arange(2)[None, :]).astype(BF16)
    bgu = (side[:, None, None, :, None] * b_unit[None]).reshape(2 * RANK, 2 * units)
    ad_t = adapter_down_in[a].T
    b_d = adapter_down_out[a] * two

    cos, sin = rope_tables(length)
    x_float = hidden_in.astype(F32)
    x_norm = normed(x_float, norm_gains[0])
    h_own = x_norm.astype(BF16)
    x_all = in_order(hidden_in, x_peer)
    h_all = normed(x_all.astype(F32), norm_gains[0]).astype(BF16)
    u_qkv = dot(h_all, qkv_in).astype(BF16)
    ids = lax.all_gather(jnp.full((16, 128), a, BF16), "dp", axis=0, tiled=False)[:, 0, 0]
    ids = ids.astype(jnp.int32)
    pack_2, _, h_all, u_qkv, bgu, ids = lax.optimization_barrier(
        (pack_2, full_1, h_all, u_qkv, bgu, ids)
    )
    full_2 = gather(pack_2)
    raw = dot(h_all, w_qkv) + dot(u_qkv, b_qkv)
    q_raw = raw[:, :q_width].reshape(length, per_group, HD)
    k_raw = raw[:, q_width : q_width + HD]
    queries = rotate(normed(q_raw, head_gains[0]), cos[:, None], sin[:, None]).astype(BF16)
    keys = rotate(normed(k_raw, head_gains[1]), cos, sin).astype(BF16)
    values = raw[:, q_width + HD :].astype(BF16)
    index = jnp.arange(length) // BLK
    distance = index[:, None] - index[None, :]
    allowed = ((distance >= 0) & (distance < WIN // BLK))[None]
    scores = jnp.einsum("lqd,md->qlm", queries, keys, preferred_element_type=F32) * HD ** (-0.5)
    scores = jnp.where(allowed, scores, NEG_BIG)
    shifted = jnp.exp(scores - jnp.max(scores, axis=-1, keepdims=True))
    probs = (shifted / jnp.sum(shifted, axis=-1, keepdims=True)).astype(BF16)
    context = (
        jnp.einsum("qlm,md->lqd", probs, values, preferred_element_type=F32)
        .reshape(length, q_width)
        .astype(BF16)
    )
    queries = queries.reshape(length, q_width)
    u_attn_f = dot(context, a_o)
    u_attn = u_attn_f.astype(BF16)
    attn_part = dot_nt(context, w_o_t) + dot(u_attn, b_o)
    attn_recv = swap(theirs(attn_part).astype(BF16))
    attn_proj = mine(attn_part) + attn_recv.astype(F32)
    laurel_low = dot(h_own, left).astype(BF16)
    laurel_wide = dot_nt(laurel_low, right_t)
    combined = (
        x_float + normed(attn_proj, norm_gains[1]) + x_norm + normed(laurel_wide, norm_gains[2])
    ) * RSQRT_TWO
    h2_own = normed(combined, norm_gains[3]).astype(BF16)

    h2_peer = swap(h2_own)
    h2 = jnp.concatenate([h2_own[:half], h2_peer[:half], h2_own[half:], h2_peer[half:]], axis=0)
    u_ffn = dot(h2, a_ffn).astype(BF16)
    u_qkv_t, qkv_in_t, a_o_t, a_ffn_t, u_ffn_t = u_qkv.T, qkv_in.T, a_o.T, a_ffn.T, u_ffn.T
    pack_3, _, _ = lax.optimization_barrier((pack_3, full_2, h2_own))
    full_3 = gather(pack_3)
    partial = ffn_up(h2, full_1, split, 0, u_ffn, bgu, ad_t, None)
    ud, g_pre, u_pre, hidden = ffn_up(
        h2, full_2, blocks - split, split, u_ffn, bgu, ad_t, partial
    )
    (queries, keys, values, raw, context, u_qkv_t, qkv_in_t, a_o_t, a_ffn_t, u_ffn_t, b_qkv, b_o, cos, sin, hidden) = (
        lax.optimization_barrier(
            (queries, keys, values, raw, context, u_qkv_t, qkv_in_t, a_o_t, a_ffn_t, u_ffn_t, b_qkv, b_o, cos, sin, hidden)
        )
    )
    fwd_parts, ple_parts = [], []
    for s in range(2):
        own, peer = ffn_down(hidden, full_3, ud, b_d, s)
        if s == 0:
            hidden, peer = lax.optimization_barrier((hidden, peer))
        fwd_parts.append((own, swap(peer)))
    layer_out = []
    for s in range(2):
        own, recv = fwd_parts[s]
        whole, d_ffn_s, d_first_s = ple_both(
            combined, own, recv, out_grad, per_layer_input, full_3, ple_column, norm_gains,
            layer_out, s,
        )
        layer_out = [whole]
        ple_parts.append((d_ffn_s, swap(d_ffn_s), d_first_s))
    packs, early = (full_1, full_2, full_3), blocks * 5 // 8
    common = (g_pre, u_pre, bgu, ad_t, b_d, u_ffn_t, a_ffn_t)
    lau_column = lau_at // (2 * lr)
    (own_0, recv_0, first_0), (own_1, recv_1, first_1) = ple_parts
    d_ffn_parts = [own_0, recv_0, own_1, recv_1]
    grad_ffn, du_0, d_h2_own_0, d_h2_peer_0 = ffn_bwd(
        own_0, recv_0, packs, split, 0, blocks, *common, 0, None, None, True
    )
    d_h2_recv_0 = swap(d_h2_peer_0)
    own_1, _ = lax.optimization_barrier((own_1, d_h2_peer_0))
    send_ffn, du_1, acc_1 = ffn_bwd(
        own_1, recv_1, packs, split, 0, early, *common, 1, grad_ffn, None, False
    )
    d_h2_recv_0, acc_1 = lax.optimization_barrier((d_h2_recv_0, acc_1))
    d_attn_0, *branch = between_bwd(
        first_0, combined, d_h2_own_0, d_h2_recv_0, attn_proj, laurel_low, full_1, lau_column,
        norm_gains, [], 0,
    )
    d_attn_recv_0 = swap(d_attn_0)
    acc_1, _ = lax.optimization_barrier((acc_1, d_attn_0))
    send_ffn, du_1, d_h2_own_1, d_h2_peer_1 = ffn_bwd(
        own_1, recv_1, packs, split, early, blocks - early, *common, 1, grad_ffn,
        (acc_1, du_1, send_ffn), True,
    )
    send_ffn, d_attn_recv_0 = lax.optimization_barrier((send_ffn, d_attn_recv_0))
    got_ffn = lax.all_gather(send_ffn, "dp", axis=0, tiled=False)
    d_attn_1, *branch = between_bwd(
        first_1, combined, d_h2_own_1, swap(d_h2_peer_1), attn_proj, laurel_low, full_1,
        lau_column, norm_gains, branch, 1,
    )
    d_branch, d_norm = branch
    d_attn_recv_1 = swap(d_attn_1)

    d_ffn_all = jnp.concatenate(d_ffn_parts, axis=0)
    du_ffn = jnp.concatenate([du_0, du_1], axis=0).astype(BF16)
    ud_low = ud.astype(BF16)
    shared_ffn = jnp.concatenate(
        [dot_tn(h2, du_ffn).astype(BF16), (2.0 * dot_tn(d_ffn_all, ud_low)).astype(BF16)], axis=1
    )

    pieces = [d_attn_0, d_attn_1, d_attn_recv_0, d_attn_recv_1]
    pieces, shared_ffn = lax.optimization_barrier((pieces, shared_ffn))
    d_h_peer_0, d_h_peer_1, d_raw, d_u, send_heads = attention_bwd(
        pieces, t.astype(jnp.int32).reshape(1), full_1, qkv_at, wo_at // HD, b_o, a_o_t, queries, keys,
        values, probs, raw, head_gains, cos, sin, context, u_qkv_t, b_qkv, qkv_in_t,
    )
    d_h_recv_0 = swap(d_h_peer_0)
    d_raw, d_u, got_ffn = lax.optimization_barrier((d_raw, d_u, got_ffn))
    got_heads = lax.all_gather(send_heads, "dp", axis=0, tiled=False)
    d_attn_all = in_order(
        jnp.concatenate([d_attn_0, d_attn_1], axis=0),
        jnp.concatenate([d_attn_recv_0, d_attn_recv_1], axis=0),
    )
    send = jnp.concatenate(
        [
            shared_ffn,
            (2.0 * dot_tn(d_attn_all, u_attn)).astype(BF16),
            dot_tn(h_all, d_u).astype(BF16),
        ],
        axis=1,
    )
    send, d_h_peer_1 = lax.optimization_barrier((send, d_h_peer_1))
    d_h_recv_1 = swap(d_h_peer_1)
    got = lax.all_to_all(send, ("dp", "tensor"), 0, 0, tiled=True).reshape(2 * dp, -1, send.shape[1])
    out_ffn_out, out_down_in = ffn_adapter_sums(got_ffn, ids, adapters, units)
    d_h_own = dot_nt(mine(d_raw), w_qkv) + dot_nt(mine(d_u), qkv_in)
    got, out_ffn_out, out_down_in, d_h_own = lax.optimization_barrier(
        (got, out_ffn_out, out_down_in, d_h_own)
    )
    out_ffn_in, out_down_out, out_attn_out, out_qkv_in = shared_sums(got, ids, adapters)
    d_h_own, out_qkv_in = lax.optimization_barrier((d_h_own, out_qkv_in))
    final_args = (hidden_in, d_norm, d_branch, d_h_own)
    input_grad = final_bwd(*final_args, d_h_recv_0, norm_gains, [], 0)
    input_grad = final_bwd(*final_args, d_h_recv_1, norm_gains, [input_grad], 1)
    got_heads, input_grad = lax.optimization_barrier((got_heads, input_grad))
    out_qkv_out, out_attn_in = head_sums(got_heads, ids, adapters, qkv_width)
    return (
        layer_out[0],
        input_grad,
        jnp.swapaxes(out_qkv_in, 1, 2),
        out_qkv_out,
        jnp.swapaxes(out_attn_in, 1, 2),
        out_attn_out,
        jnp.swapaxes(out_ffn_in, 1, 2),
        out_ffn_out,
        jnp.swapaxes(out_down_in, 1, 2),
        out_down_out,
    )


def solution(mesh):
    in_specs = (
        P(("dp", "tensor"), None),
        P(("dp", "tensor"), None),
        P(("dp", "tensor"), None),
        P("dp"),
        P("dp", "tensor", None),
        P("tensor", "dp"),
        P("dp", None, "tensor"),
        P("tensor", "dp"),
        P("dp", None),
        P(None, "dp"),
        P("dp", None),
        P(None, "dp"),
        P(),
        P(),
        P(),
        P(None, None, "tensor", None),
        P(None, "tensor", None),
        P(),
        P(),
        P(None, None, None, "tensor"),
        P(None, "tensor", None),
        P(),
    )
    out_specs = (
        P(("dp", "tensor"), None),
        P(("dp", "tensor"), None),
        P(None, ("dp", "tensor"), None),
        P(None, None, "tensor", None),
        P(None, "tensor", None),
        P(None, None, ("dp", "tensor")),
        P(None, ("dp", "tensor"), None),
        P(None, None, None, "tensor"),
        P(None, "tensor", None),
        P(None, None, ("dp", "tensor")),
    )
    return jax.shard_map(
        on_device, mesh=mesh, in_specs=in_specs, out_specs=out_specs, check_vma=False
    )
```

```python
import functools

import jax
import jax.numpy as jnp
from jax import lax
from jax.experimental import pallas as pl
from jax.experimental.pallas import tpu as pltpu
from jax.sharding import PartitionSpec as P

HEADS = 8
KV = 2
HD = 256
WIN = 512
BLK = 256
RANK = 16
UB = 512
GB = 2 * UB

NORM_EPSILON = 1e-06
RSQRT_TWO = 0.7071067811865476
ROPE_BASE = 10000.0
NEG_BIG = -1e30
GELU_A = 0.7978845608028654
GELU_B = 0.044715

F32 = jnp.float32
BF16 = jnp.bfloat16
VMEM_LIMIT = 63 * 1024 * 1024
DOWN_CHUNK = 512
STREAMS = 3


def dot(a, b):
    return lax.dot_general(a, b, (((1,), (0,)), ((), ())), preferred_element_type=F32)


def dot_nt(a, b):
    return lax.dot_general(a, b, (((1,), (1,)), ((), ())), preferred_element_type=F32)


def dot_tn(a, b):
    return lax.dot_general(a, b, (((0,), (0,)), ((), ())), preferred_element_type=F32)


def inv_rms(v):
    return lax.rsqrt(jnp.mean(v * v, axis=-1, keepdims=True) + NORM_EPSILON)


def normed(v, gains):
    return v * inv_rms(v) * gains


def norm_back(v, gains, cotangent):
    r = inv_rms(v)
    gc = gains * cotangent
    return r * gc - v * (r * r * r * jnp.mean(v * gc, axis=-1, keepdims=True))


def gelu_tanh(v):
    return 0.5 * v * (1.0 + jnp.tanh(GELU_A * (v + GELU_B * v * v * v)))


def gelu_both(v):
    v2 = v * v
    th = jnp.tanh(GELU_A * v * (1.0 + GELU_B * v2))
    half = 0.5 * (1.0 + th)
    slope = half + 0.5 * v * (1.0 - th * th) * (GELU_A * (1.0 + 3.0 * GELU_B * v2))
    return v * half, slope


def const_spec(shape):
    return pl.BlockSpec(shape, lambda *_: (0,) * len(shape), pipeline_mode=pl.Buffered(1))


def any_spec():
    return pl.BlockSpec(memory_space=pl.ANY)


def params():
    return pltpu.CompilerParams(vmem_limit_bytes=VMEM_LIMIT)


def pack_shards(gate_up, first, count, rest, rows, name):
    width = count * GB + sum(n for _, n in rest)

    def body(*refs):
        out = refs[-1]
        for b in range(count):
            cs = slice(b * UB, (b + 1) * UB)
            out[:, b * GB : b * GB + UB] = refs[0][:, 0, cs]
            out[:, b * GB + UB : (b + 1) * GB] = refs[0][:, 1, cs]
        at = count * GB
        for ref, (value, n) in zip(refs[1 if count else 0 : -1], rest):
            out[:, at : at + n] = ref[...] if value.shape == (rows, n) else ref[...].T
            at += n

    block = (pl.Element(rows), pl.Element(2), pl.Element(count * UB))
    gate_spec = [pl.BlockSpec(block, lambda i: (0, 0, first * UB))] if count else []
    return pl.pallas_call(
        body,
        grid=(1,),
        in_specs=gate_spec + [const_spec(v.shape) for v, _ in rest],
        out_specs=const_spec((rows, width)),
        out_shape=jax.ShapeDtypeStruct((rows, width), BF16),
        compiler_params=params(),
        name=name,
    )(*([gate_up] if count else []), *[v for v, _ in rest])


def ffn_up(h2, packed, blocks, first, u_low, bgu, ad_t, prev):
    rows, width = h2.shape
    units = ad_t.shape[1]
    tile = rows // 2
    sub = 256

    def body(*refs):
        h_ref, w_ref, ul_ref, bgu_ref, ad_ref = refs[:5]
        g_out, u_out, hid_out, ud_out = refs[-4:]
        j = pl.program_id(0)

        @pl.when(j == 0)
        def _():
            if prev is None:
                ud_out[...] = jnp.zeros_like(ud_out)
            else:
                ud_out[...] = refs[5][...]

        for k in range(rows // tile):
            at_rows = slice(k * tile, (k + 1) * tile)
            h = h_ref[at_rows, :]
            ul = ul_ref[at_rows, :]
            for n in range(UB // sub):
                cs = slice(n * sub, (n + 1) * sub)
                us = slice(UB + n * sub, UB + (n + 1) * sub)
                g = dot(h, w_ref[:, cs]) + dot(ul, bgu_ref[:, cs])
                u = dot(h, w_ref[:, us]) + dot(ul, bgu_ref[:, us])
                g_out[at_rows, cs] = g.astype(BF16)
                u_out[at_rows, cs] = u.astype(BF16)
                hid_out[at_rows, cs] = (gelu_tanh(g) * u).astype(BF16)
            ud_out[at_rows, :] += dot_nt(hid_out[at_rows, :], ad_ref[...])

    in_specs = [
        const_spec((rows, width)),
        pl.BlockSpec((width, GB), lambda j: (0, j)),
        const_spec((rows, 2 * RANK)),
        pl.BlockSpec((2 * RANK, GB), lambda j: (0, first + j)),
        pl.BlockSpec((RANK, UB), lambda j: (0, first + j)),
    ]
    args = [h2, packed, u_low, bgu, ad_t]
    aliases = {}
    if prev is not None:
        in_specs += [const_spec((rows, RANK)), any_spec(), any_spec(), any_spec()]
        args += list(prev)
        aliases = {6: 0, 7: 1, 8: 2}
    unit_block = pl.BlockSpec((rows, UB), lambda j: (0, first + j))
    shape = jax.ShapeDtypeStruct
    g, u, hidden, ud = pl.pallas_call(
        body,
        grid=(blocks,),
        in_specs=in_specs,
        out_specs=[unit_block] * 3 + [const_spec((rows, RANK))],
        out_shape=[shape((rows, units), BF16)] * 3 + [shape((rows, RANK), F32)],
        input_output_aliases=aliases,
        compiler_params=params(),
        cost_estimate=pl.CostEstimate(
            flops=4 * rows * width * UB * blocks,
            bytes_accessed=2 * width * GB * blocks,
            transcendentals=rows * UB * blocks,
        ),
        name="ffn_up",
    )(*args)
    return ud, g, u, hidden


def ffn_down(hidden, packed, ud, bd, rb, streams):
    rows, units = hidden.shape
    width = packed.shape[0]
    part = rows // (2 * STREAMS)
    r = 2 * part * streams
    chunk = DOWN_CHUNK

    def body(h_ref, w_ref, ud_ref, bd_ref, *outs):
        total = dot_nt(h_ref[...], w_ref[...]) + dot(ud_ref[...].astype(BF16), bd_ref[...])
        for n, out in enumerate(outs):
            out[...] = total[n * part : (n + 1) * part].astype(out.dtype)

    row_const = lambda n: pl.BlockSpec((r, n), lambda j: (rb, 0), pipeline_mode=pl.Buffered(1))
    column = pl.BlockSpec((part, chunk), lambda j: (0, j))
    shape = jax.ShapeDtypeStruct
    return pl.pallas_call(
        body,
        grid=(width // chunk,),
        in_specs=[
            row_const(units),
            pl.BlockSpec((chunk, units), lambda j: (j, 0)),
            row_const(RANK),
            pl.BlockSpec((RANK, chunk), lambda j: (0, j)),
        ],
        out_specs=[column] * (2 * streams),
        out_shape=[shape((part, width), F32), shape((part, width), BF16)] * streams,
        compiler_params=params(),
        cost_estimate=pl.CostEstimate(
            flops=2 * r * width * units, bytes_accessed=2 * width * units, transcendentals=0
        ),
        name="ffn_down",
    )(hidden, packed, ud, bd)


def ffn_bwd(own, peer, packs, split, g_pre, u_pre, bgu, ad_t, bd, u_t, a_in_t, h2, ud_t, rb, base, grad_type):
    half, width = own.shape
    r = 2 * half
    units = ad_t.shape[1]
    first, blocks = 0, units // UB
    sub = 256

    def body(*refs):
        own_ref, peer_ref, g_ref, u_ref, bgu_ref, ad_ref, bd_ref, ut_ref, ain_ref = refs[:9]
        pack_refs = refs[9 : 9 + len(packs)]
        at = 9 + len(packs)
        h2_any, udt_ref = refs[at : at + 2]
        at += 2
        if base is not None:
            base_ref, base_in = refs[at : at + 2]
            at += 2
        grad_out, in_out, own_out, peer_out = refs[at : at + 4]
        at += 4
        df, acc, wbuf, dd, du, dgu, hs, sem, h2_sem = refs[at:]
        j = pl.program_id(0)
        slot = lax.rem(j, 2)

        def copy(ref, column, where, part):
            lo, n = ((2 * UB, UB), (0, 2 * UB))[part]
            return pltpu.make_async_copy(
                ref.at[:, pl.ds(column, n)], wbuf.at[where, :, pl.ds(lo, n)], sem.at[where, part]
            )

        def fetch(step, where):
            block = first + step
            copy(pack_refs[2], pl.multiple_of(block * UB, UB), where, 0).start()

            @pl.when(block < split)
            def _():
                copy(pack_refs[0], pl.multiple_of(block * GB, GB), where, 1).start()

            @pl.when(block >= split)
            def _():
                copy(pack_refs[1], pl.multiple_of((block - split) * GB, GB), where, 1).start()

        @pl.when(j == 0)
        def _():
            fetch(j, 0)
            df[0:half, :] = own_ref[...]
            df[half:r, :] = peer_ref[...]
            acc[...] = jnp.zeros_like(acc)
            du[...] = jnp.zeros_like(du)
            dd[...] = dot_nt(df[...], bd_ref[...]).astype(BF16)

        @pl.when(j + 1 < blocks)
        def _():
            fetch(j + 1, 1 - slot)

        copy(pack_refs[2], 0, slot, 0).wait()
        for n in range(UB // sub):
            cs = slice(n * sub, (n + 1) * sub)
            dh = dot(df[...], wbuf[slot, :, 2 * UB + n * sub : 2 * UB + (n + 1) * sub])
            dh += dot(dd[...], ad_ref[:, cs])
            g = g_ref[:, cs].astype(F32)
            u = u_ref[:, cs].astype(F32)
            act, slope = gelu_both(g)
            dgu[:, cs] = (dh * u * slope).astype(BF16)
            dgu[:, UB + n * sub : UB + (n + 1) * sub] = (dh * act).astype(BF16)
            hs[:, cs] = (act * u).astype(BF16)
        copy(pack_refs[0], 0, slot, 1).wait()
        d_both = dgu[...]
        for c in range(width // 512):
            cc = slice(c * 512, (c + 1) * 512)
            acc[:, cc] += dot_nt(d_both, wbuf[slot, cc, 0 : 2 * UB])
        du[...] += dot_nt(d_both, bgu_ref[...])
        both = dot(ut_ref[...], d_both)
        rows = (2.0 * both[:RANK, :UB], 2.0 * both[RANK:, UB:], dot_tn(dd[...], hs[...]))
        for m, row in enumerate(rows):
            ms = slice(m * RANK, (m + 1) * RANK)
            if base is not None:
                row = row + base_ref[ms, :]
            grad_out[ms, :] = row.astype(grad_out.dtype)

        @pl.when(j == blocks - 1)
        def _():
            down = dot(udt_ref[...], df[...])
            rows_copy = pltpu.make_async_copy(h2_any.at[pl.ds(rb * r, r), :], df, h2_sem)
            rows_copy.start()
            du_low = du[...].astype(BF16)
            total = acc[...] + dot(du_low, ain_ref[...])
            own_out[...] = total[:half]
            peer_out[...] = total[half:].astype(BF16)
            rows_copy.wait()
            up = dot_tn(du_low, df[...])
            down = 2.0 * down
            if base is not None:
                up = up + base_in[0 : 2 * RANK, :]
                down = down + base_in[2 * RANK : 3 * RANK, :]
            in_out[0 : 2 * RANK, :] = up
            in_out[2 * RANK : 3 * RANK, :] = down

    rows_block = lambda: pl.BlockSpec((r, UB), lambda j: (rb, first + j))
    unit_block = lambda: pl.BlockSpec((RANK, UB), lambda j: (0, first + j))
    shape = jax.ShapeDtypeStruct
    in_specs = [
        const_spec((half, width)),
        const_spec((half, width)),
        rows_block(),
        rows_block(),
        pl.BlockSpec((2 * RANK, 2 * UB), lambda j: (0, first + j)),
        unit_block(),
        const_spec((RANK, width)),
        pl.BlockSpec((2 * RANK, r), lambda j: (0, rb), pipeline_mode=pl.Buffered(1)),
        const_spec((2 * RANK, width)),
    ] + [any_spec() for _ in packs]
    args = [own, peer, g_pre, u_pre, bgu, ad_t, bd, u_t, a_in_t, *packs]
    grad_block = lambda: pl.BlockSpec((3 * RANK, UB), lambda j: (0, first + j))
    in_specs += [
        any_spec(),
        pl.BlockSpec((RANK, r), lambda j: (0, rb), pipeline_mode=pl.Buffered(1)),
    ]
    args += [h2, ud_t]
    if base is not None:
        in_specs += [grad_block(), const_spec((3 * RANK, width))]
        args += list(base)
    out_specs = [
        grad_block(),
        const_spec((3 * RANK, width)),
        const_spec((half, width)),
        const_spec((half, width)),
    ]
    out_shape = [
        shape((3 * RANK, units), grad_type),
        shape((3 * RANK, width), F32),
        shape((half, width), F32),
        shape((half, width), BF16),
    ]
    return pl.pallas_call(
        body,
        grid=(blocks,),
        in_specs=in_specs,
        out_specs=out_specs,
        out_shape=out_shape,
        scratch_shapes=[
            pltpu.VMEM((r, width), BF16),
            pltpu.VMEM((r, width), F32),
            pltpu.VMEM((2, width, 3 * UB), BF16),
            pltpu.VMEM((r, RANK), BF16),
            pltpu.VMEM((r, 2 * RANK), F32),
            pltpu.VMEM((r, 2 * UB), BF16),
            pltpu.VMEM((r, UB), BF16),
            pltpu.SemaphoreType.DMA((2, 2)),
            pltpu.SemaphoreType.DMA,
        ],
        compiler_params=params(),
        cost_estimate=pl.CostEstimate(
            flops=6 * r * width * UB * blocks,
            bytes_accessed=6 * width * UB * blocks,
            transcendentals=r * UB * blocks,
        ),
        name="ffn_bwd",
    )(*args)


def ple_both(combined, ffn_own, ffn_recv, out_grad, ple_in, packed, column, gains, prev, rb):
    half, width = ffn_own.shape
    rows = combined.shape[0]
    pd = ple_in.shape[1]
    tile = half

    def body(c_ref, fo_ref, fr_ref, og_ref, pi_ref, w_ref, gain_ref, *refs):
        out_ref, dffn_ref, dfirst_ref = refs[-3:]
        ffn = fo_ref[...] + fr_ref[...].astype(F32)
        y = c_ref[...] + normed(ffn, gain_ref[4:5, :])
        pre = dot(y.astype(BF16), w_ref[:, 0:pd])
        side = pi_ref[...].astype(F32)
        act, slope = gelu_both(pre)
        wide = dot_nt((act * side).astype(BF16), w_ref[:, pd : 2 * pd])
        out_ref[...] = (y + normed(wide, gain_ref[5:6, :])).astype(BF16)
        cot = og_ref[...].astype(F32)
        d_wide = norm_back(wide, gain_ref[5:6, :], cot).astype(BF16)
        d_pre = (dot(d_wide, w_ref[:, pd : 2 * pd]) * side * slope).astype(BF16)
        d_first = cot + dot_nt(d_pre, w_ref[:, 0:pd])
        dfirst_ref[...] = d_first
        dffn_ref[...] = norm_back(ffn, gain_ref[4:5, :], d_first).astype(BF16)

    n = half // tile
    here = lambda w: pl.BlockSpec((tile, w), lambda i: (i, 0))
    there = lambda w: pl.BlockSpec((tile, w), lambda i: (rb * n + i, 0))
    shape = jax.ShapeDtypeStruct
    return pl.pallas_call(
        body,
        grid=(n,),
        in_specs=[
            there(width),
            here(width),
            here(width),
            there(width),
            there(pd),
            pl.BlockSpec((width, 2 * pd), lambda i: (0, column), pipeline_mode=pl.Buffered(1)),
            const_spec(gains.shape),
        ]
        + [any_spec() for _ in prev],
        out_specs=[there(width), here(width), here(width)],
        out_shape=[
            shape((rows, width), BF16),
            shape((half, width), BF16),
            shape((half, width), F32),
        ],
        input_output_aliases={7: 0} if prev else {},
        compiler_params=params(),
        cost_estimate=pl.CostEstimate(
            flops=8 * half * width * pd, bytes_accessed=20 * half * width, transcendentals=0
        ),
        name="ple_both",
    )(combined, ffn_own, ffn_recv, out_grad, ple_in, packed, gains, *prev)


def between_bwd(d_first, combined, dh_own, dh_recv, attn_proj, low, packed, column, gains, prev, rb):
    half, width = d_first.shape
    rows = combined.shape[0]
    lr = low.shape[1]
    tile = half

    def body(df_ref, c_ref, ho_ref, hr_ref, ap_ref, low_ref, w_ref, gain_ref, *refs):
        da_ref, db_ref, dn_ref = refs[-3:]
        d_h2 = ho_ref[...] + hr_ref[...].astype(F32)
        d_comb = df_ref[...] + norm_back(c_ref[...], gain_ref[3:4, :], d_h2)
        d_branch = d_comb * RSQRT_TWO
        db_ref[...] = d_branch
        da_ref[...] = norm_back(ap_ref[...], gain_ref[1:2, :], d_branch).astype(BF16)
        wide = dot_nt(low_ref[...], w_ref[:, lr : 2 * lr])
        d_wide = norm_back(wide, gain_ref[2:3, :], d_branch).astype(BF16)
        d_low = dot(d_wide, w_ref[:, lr : 2 * lr]).astype(BF16)
        dn_ref[...] = d_branch + dot_nt(d_low, w_ref[:, 0:lr])

    n = half // tile
    here = lambda w: pl.BlockSpec((tile, w), lambda i: (i, 0))
    there = lambda w: pl.BlockSpec((tile, w), lambda i: (rb * n + i, 0))
    shape = jax.ShapeDtypeStruct
    return pl.pallas_call(
        body,
        grid=(n,),
        in_specs=[
            here(width),
            there(width),
            here(width),
            here(width),
            there(width),
            there(lr),
            pl.BlockSpec((width, 2 * lr), lambda i: (0, column), pipeline_mode=pl.Buffered(1)),
            const_spec(gains.shape),
        ]
        + [any_spec() for _ in prev],
        out_specs=[here(width), there(width), there(width)],
        out_shape=[
            shape((half, width), BF16),
            shape((rows, width), F32),
            shape((rows, width), F32),
        ],
        input_output_aliases={8: 1, 9: 2} if prev else {},
        compiler_params=params(),
        cost_estimate=pl.CostEstimate(
            flops=6 * half * width * lr, bytes_accessed=26 * half * width, transcendentals=0
        ),
        name="between_bwd",
    )(d_first, combined, dh_own, dh_recv, attn_proj, low, packed, gains, *prev)


def attention_bwd(pieces, turn, packed, qkv_column, wo_column, bo, ao_t, q, k, v, probs, raw, gains, cos, sin,
                  context, u_t, b_qkv, a_in_t, u_attn_t):
    length, q_width = q.shape
    width = packed.shape[0]
    heads = q_width // HD
    half_hd = HD // 2
    scale = HD ** (-0.5)
    n_blocks = length // BLK
    span = WIN // BLK
    quarter = pieces[0].shape[0]
    count = len(pieces)
    total = q_width + 2 * HD
    here = length // 2

    def unrotate(d, cos_v, sin_v):
        d1, d2 = d[:, :half_hd], d[:, half_hd:]
        return jnp.concatenate([d1 * cos_v + d2 * sin_v, d2 * cos_v - d1 * sin_v], axis=1)

    def body(turn_ref, *refs):
        piece_refs = refs[:count]
        (wo_ref, w_any, bo_ref, ao_ref, q_ref, k_ref, v_ref, p_ref, rq_ref, rk_ref, gain_ref, cos_ref,
         sin_ref, ctx_ref, ut_ref, b_ref, ain_ref, uat_ref, peer_0, peer_1, draw, du_out, heads_out, out_rows,
         da, du, dk, dv, wq, sem) = refs[count:]
        hh = pl.program_id(0)
        weights = pltpu.make_async_copy(w_any.at[:, pl.ds(qkv_column, total)], wq, sem)

        @pl.when(hh == 0)
        def _():
            weights.start()
            shift = turn_ref[0] * here
            for i, ref in enumerate(piece_refs):
                place = lax.rem(shift + i * quarter, length)
                da[pl.ds(pl.multiple_of(place, quarter), quarter), :] = ref[...]
            du[...] = dot_nt(da[...], bo_ref[...]).astype(BF16)
            dk[...] = jnp.zeros_like(dk)
            dv[...] = jnp.zeros_like(dv)

        dctx = (dot(da[...], wo_ref[...]) + dot(du[...], ao_ref[...])).astype(BF16)
        cos_v, sin_v = cos_ref[...], sin_ref[...]
        column = pl.multiple_of(hh * HD, HD)
        for i in range(n_blocks):
            low, high = max(0, i - span + 1) * BLK, (i + 1) * BLK
            rows = slice(i * BLK, (i + 1) * BLK)
            d_i = dctx[rows]
            p_i = p_ref[0, rows, low:high]
            p_f = p_i.astype(F32)
            dp = dot_nt(d_i, v_ref[low:high, :])
            ds = p_f * (dp - jnp.sum(p_f * dp, axis=-1, keepdims=True))
            ds = ds.astype(BF16)
            dq = dot(ds, k_ref[low:high, :]) * scale
            dk[low:high, :] += dot_tn(ds, q_ref[rows, :])
            dv[low:high, :] += dot_tn(p_i, d_i)
            back = norm_back(rq_ref[rows, :], gain_ref[0:1, :], unrotate(dq, cos_v[rows], sin_v[rows]))
            draw[rows, pl.ds(column, HD)] = back.astype(BF16)
        heads_out[:, pl.ds(column, HD)] = (
            2.0 * dot(ut_ref[0:RANK, :], draw[:, pl.ds(column, HD)])
        ).astype(BF16)
        heads_out[:, pl.ds(pl.multiple_of(total + hh * HD, HD), HD)] = dot_tn(
            du[...], ctx_ref[...]
        ).astype(BF16)

        @pl.when(hh == heads - 1)
        def _():
            back = norm_back(rk_ref[...], gain_ref[1:2, :], unrotate(dk[...] * scale, cos_v, sin_v))
            at_k, at_v = slice(q_width, q_width + HD), slice(q_width + HD, total)
            draw[:, at_k] = back.astype(BF16)
            draw[:, at_v] = dv[...].astype(BF16)
            for m, where in ((1, at_k), (2, at_v)):
                got = dot(ut_ref[m * RANK : (m + 1) * RANK, :], draw[:, where])
                heads_out[:, where] = (2.0 * got).astype(BF16)
            du_out[...] = dot_nt(draw[...], b_ref[...]).astype(BF16)
            out_rows[...] = (2.0 * dot(uat_ref[...], da[...])).astype(BF16)
            weights.wait()
            theirs = pl.multiple_of((1 - turn_ref[0]) * here, here)
            d_rows = draw[pl.ds(theirs, here), :]
            u_rows = du_out[pl.ds(theirs, here), :]
            for c in range(width // 512):
                cc = slice(c * 512, (c + 1) * 512)
                got = dot_nt(d_rows, wq[cc, :]) + dot(u_rows, ain_ref[:, cc])
                peer_0[:, cc] = got[: here // 2].astype(BF16)
                peer_1[:, cc] = got[here // 2 :].astype(BF16)

    shape = jax.ShapeDtypeStruct
    head_block = lambda: pl.BlockSpec((length, HD), lambda h: (0, h))
    return pl.pallas_call(
        body,
        grid=(heads,),
        in_specs=[pl.BlockSpec(memory_space=pltpu.SMEM)]
        + [const_spec(piece.shape) for piece in pieces]
        + [
            pl.BlockSpec((width, HD), lambda h: (0, wo_column + h)),
            any_spec(),
            const_spec(bo.shape),
            pl.BlockSpec((RANK, HD), lambda h: (0, h)),
            head_block(),
            const_spec(k.shape),
            const_spec(v.shape),
            pl.BlockSpec((1, length, length), lambda h: (h, 0, 0)),
            head_block(),
            pl.BlockSpec((length, HD), lambda h: (0, heads), pipeline_mode=pl.Buffered(1)),
            const_spec(gains.shape),
            const_spec(cos.shape),
            const_spec(sin.shape),
            head_block(),
            const_spec(u_t.shape),
            const_spec(b_qkv.shape),
            const_spec(a_in_t.shape),
            const_spec(u_attn_t.shape),
        ],
        out_specs=[
            const_spec((here // 2, width)),
            const_spec((here // 2, width)),
            const_spec((length, total)),
            const_spec((length, 3 * RANK)),
            const_spec((RANK, total + q_width)),
            const_spec((RANK, width)),
        ],
        out_shape=[
            shape((here // 2, width), BF16),
            shape((here // 2, width), BF16),
            shape((length, total), BF16),
            shape((length, 3 * RANK), BF16),
            shape((RANK, total + q_width), BF16),
            shape((RANK, width), BF16),
        ],
        scratch_shapes=[
            pltpu.VMEM((length, width), BF16),
            pltpu.VMEM((length, RANK), BF16),
            pltpu.VMEM((length, HD), F32),
            pltpu.VMEM((length, HD), F32),
            pltpu.VMEM((width, total), BF16),
            pltpu.SemaphoreType.DMA,
        ],
        compiler_params=params(),
        cost_estimate=pl.CostEstimate(flops=1024 * 1024, bytes_accessed=1024 * 1024, transcendentals=0),
        name="attention_bwd",
    )(turn, *pieces, packed, packed, bo, ao_t, q, k, v, probs, raw, raw, gains, cos, sin, context, u_t, b_qkv,
      a_in_t, u_attn_t)


def final_bwd(x, d_norm, d_branch, dh_own, dh_recv, gains, prev, rb):
    rows, width = x.shape
    half = rows // 2
    tile = half // 2

    def body(x_ref, dn_ref, db_ref, ho_ref, hr_ref, gain_ref, *refs):
        out_ref = refs[-1]
        total = dn_ref[...] + ho_ref[...] + hr_ref[...].astype(F32)
        out_ref[...] = db_ref[...] + norm_back(x_ref[...].astype(F32), gain_ref[0:1, :], total)

    n = half // tile
    here = pl.BlockSpec((tile, width), lambda i: (i, 0))
    there = pl.BlockSpec((tile, width), lambda i: (rb * n + i, 0))
    return pl.pallas_call(
        body,
        grid=(n,),
        in_specs=[there] * 4 + [here, const_spec(gains.shape)] + [any_spec() for _ in prev],
        out_specs=there,
        out_shape=jax.ShapeDtypeStruct((rows, width), F32),
        input_output_aliases={6: 0} if prev else {},
        compiler_params=params(),
        cost_estimate=pl.CostEstimate(
            flops=20 * half * width, bytes_accessed=20 * half * width, transcendentals=0
        ),
        name="final_bwd",
    )(x, d_norm, d_branch, dh_own, dh_recv, gains, *prev)


def add_by_adapter(ids_ref, got_ref, total, seqs, share):
    total[...] = jnp.zeros_like(total)

    def step(i, carry):
        where = ids_ref[i // share]
        total[where] += got_ref[i].astype(F32)
        return carry

    lax.fori_loop(0, seqs, step, 0)


def ffn_adapter_sums(got, ids, adapters, units):
    seqs = got.shape[0]
    tile = 1024

    def body(ids_ref, got_ref, out_ref, down_ref, total):
        add_by_adapter(ids_ref, got_ref, total, seqs, 1)
        out_ref[:, :, 0, :] = total[:, :RANK, :]
        out_ref[:, :, 1, :] = total[:, RANK : 2 * RANK, :]
        down_ref[...] = total[:, 2 * RANK :, :]

    return pl.pallas_call(
        body,
        grid=(units // tile,),
        in_specs=[
            pl.BlockSpec(memory_space=pltpu.SMEM),
            pl.BlockSpec((seqs, 3 * RANK, tile), lambda i: (0, 0, i)),
        ],
        out_specs=[
            pl.BlockSpec((adapters, RANK, 2, tile), lambda i: (0, 0, 0, i)),
            pl.BlockSpec((adapters, RANK, tile), lambda i: (0, 0, i)),
        ],
        out_shape=[
            jax.ShapeDtypeStruct((adapters, RANK, 2, units), F32),
            jax.ShapeDtypeStruct((adapters, RANK, units), F32),
        ],
        scratch_shapes=[pltpu.VMEM((adapters, 3 * RANK, tile), F32)],
        compiler_params=params(),
        cost_estimate=pl.CostEstimate(
            flops=6 * seqs * RANK * units, bytes_accessed=6 * seqs * RANK * units, transcendentals=0
        ),
        name="adapter_sums",
    )(ids, got)


def shared_sums(got, ids, adapters):
    seqs, rows, columns = got.shape
    cuts = (2 * RANK, RANK, RANK, 3 * RANK)

    def body(ids_ref, got_ref, *refs):
        total = refs[-1]
        add_by_adapter(ids_ref, got_ref, total, seqs, 2)
        for n in range(adapters):
            flipped = total[n].T
            at = 0
            for ref, cut in zip(refs, cuts):
                ref[n] = flipped[at : at + cut, :]
                at += cut

    return pl.pallas_call(
        body,
        grid=(1,),
        in_specs=[pl.BlockSpec(memory_space=pltpu.SMEM), const_spec(got.shape)],
        out_specs=[const_spec((adapters, cut, rows)) for cut in cuts],
        out_shape=[jax.ShapeDtypeStruct((adapters, cut, rows), F32) for cut in cuts],
        scratch_shapes=[pltpu.VMEM((adapters, rows, columns), F32)],
        compiler_params=params(),
        name="shared_sums",
    )(ids, got)


def head_sums(got, ids, adapters, qkv_width):
    seqs, rank, columns = got.shape
    rest = columns - qkv_width

    def body(ids_ref, got_ref, qkv_ref, attn_ref, total):
        add_by_adapter(ids_ref, got_ref, total, seqs, 1)
        qkv_ref[:, :, 0, :] = total[:, :, :qkv_width]
        attn_ref[...] = total[:, :, qkv_width:]

    return pl.pallas_call(
        body,
        grid=(1,),
        in_specs=[pl.BlockSpec(memory_space=pltpu.SMEM), const_spec(got.shape)],
        out_specs=[const_spec((adapters, rank, 1, qkv_width)), const_spec((adapters, rank, rest))],
        out_shape=[
            jax.ShapeDtypeStruct((adapters, rank, 1, qkv_width), F32),
            jax.ShapeDtypeStruct((adapters, rank, rest), F32),
        ],
        scratch_shapes=[pltpu.VMEM((adapters, rank, columns), F32)],
        compiler_params=params(),
        name="head_sums",
    )(ids, got)


def rope_tables(length):
    half_dim = HD // 2
    inverse = ROPE_BASE ** (-jnp.arange(half_dim, dtype=F32) / half_dim)
    angles = jnp.arange(length, dtype=F32)[:, None] * inverse[None, :]
    return jnp.cos(angles), jnp.sin(angles)


def rotate(values, cos, sin):
    half_dim = HD // 2
    a, b = values[..., :half_dim], values[..., half_dim:]
    return jnp.concatenate([a * cos - b * sin, b * cos + a * sin], axis=-1)


def on_device(
    hidden_in,
    per_layer_input,
    out_grad,
    adapter_ids,
    weight_qkv,
    weight_attn_out,
    weight_gate_up,
    weight_down,
    laurel_left,
    laurel_right,
    per_layer_gate,
    per_layer_proj,
    norm_gains,
    head_gains,
    adapter_qkv_in,
    adapter_qkv_out,
    adapter_attn_in,
    adapter_attn_out,
    adapter_ffn_in,
    adapter_ffn_out,
    adapter_down_in,
    adapter_down_out,
):
    rows_here, width = hidden_in.shape
    dp = lax.axis_size("dp")
    length = rows_here * 2
    part = rows_here // STREAMS
    per_group = HEADS // KV
    q_width = per_group * HD
    qkv_width = q_width + 2 * HD
    units = weight_down.shape[0]
    blocks = units // UB
    adapters = adapter_qkv_in.shape[0]
    a = adapter_ids[0]
    t = lax.axis_index("tensor")

    def swap(v):
        return lax.ppermute(v, "tensor", [(0, 1), (1, 0)])

    def in_order(own, other):
        first = jnp.where(t == 0, own, other)
        second = jnp.where(t == 0, other, own)
        return jnp.concatenate([first, second], axis=0)

    def mine(v):
        return lax.dynamic_slice_in_dim(v, t * rows_here, rows_here, axis=0)

    def theirs(v):
        return lax.dynamic_slice_in_dim(v, (1 - t) * rows_here, rows_here, axis=0)

    split = blocks // 4
    rows_packed = laurel_left.shape[0]
    lr = laurel_left.shape[1]
    pd = per_layer_gate.shape[1]
    pack_1 = pack_shards(
        weight_gate_up, 0, split,
        [(weight_qkv[:, 0, :], qkv_width), (weight_attn_out, q_width), (laurel_left.T, lr), (laurel_right, lr)],
        rows_packed, "pack_1",
    )
    gather = lambda v: lax.all_gather(v, "dp", axis=0, tiled=True)
    full_1 = gather(pack_1)
    x_peer = swap(hidden_in)
    pack_2 = pack_shards(weight_gate_up, split, blocks - split, [], rows_packed, "pack_2")
    pack_3 = pack_shards(
        None, 0, 0, [(weight_down, units), (per_layer_gate, pd), (per_layer_proj, pd)],
        rows_packed, "pack_3",
    )
    qkv_at = split * GB
    w_qkv = full_1[:, qkv_at : qkv_at + qkv_width]
    wo_at = qkv_at + qkv_width
    w_o_t = full_1[:, wo_at : wo_at + q_width]
    lau_at = wo_at + q_width
    left = full_1[:, lau_at : lau_at + lr]
    right_t = full_1[:, lau_at + lr : lau_at + 2 * lr]
    ple_column = units // (2 * pd)

    two = jnp.asarray(2.0, BF16)
    qkv_in = adapter_qkv_in[a]
    raw_out = adapter_qkv_out[a].reshape(RANK, qkv_width) * two
    column = jnp.arange(qkv_width)
    member = (column >= q_width).astype(jnp.int32) + (column >= q_width + HD).astype(jnp.int32)
    pick = (jnp.arange(3)[:, None] == member[None, :]).astype(BF16)
    b_qkv = (pick[:, None, :] * raw_out[None]).reshape(3 * RANK, qkv_width)
    a_o = adapter_attn_in[a]
    b_o = adapter_attn_out[a] * two
    a_ffn = adapter_ffn_in[a]
    b_ffn = adapter_ffn_out[a] * two
    b_unit = jnp.swapaxes(b_ffn.reshape(RANK, 2, blocks, UB), 1, 2)
    side = (jnp.arange(2)[:, None] == jnp.arange(2)[None, :]).astype(BF16)
    bgu = (side[:, None, None, :, None] * b_unit[None]).reshape(2 * RANK, 2 * units)
    ad_t = adapter_down_in[a].T
    b_d = adapter_down_out[a] * two

    cos, sin = rope_tables(length)
    x_float = hidden_in.astype(F32)
    x_norm = normed(x_float, norm_gains[0])
    h_own = x_norm.astype(BF16)
    x_all = in_order(hidden_in, x_peer)
    h_all = normed(x_all.astype(F32), norm_gains[0]).astype(BF16)
    u_qkv = dot(h_all, qkv_in).astype(BF16)
    ids = lax.all_gather(jnp.full((16, 128), a, BF16), "dp", axis=0, tiled=False)[:, 0, 0]
    ids = ids.astype(jnp.int32)
    pack_2, _, h_all, u_qkv, bgu, ids = lax.optimization_barrier(
        (pack_2, full_1, h_all, u_qkv, bgu, ids)
    )
    full_2 = gather(pack_2)
    raw = dot(h_all, w_qkv) + dot(u_qkv, b_qkv)
    q_raw = raw[:, :q_width].reshape(length, per_group, HD)
    k_raw = raw[:, q_width : q_width + HD]
    queries = rotate(normed(q_raw, head_gains[0]), cos[:, None], sin[:, None]).astype(BF16)
    keys = rotate(normed(k_raw, head_gains[1]), cos, sin).astype(BF16)
    values = raw[:, q_width + HD :].astype(BF16)
    index = jnp.arange(length) // BLK
    distance = index[:, None] - index[None, :]
    allowed = ((distance >= 0) & (distance < WIN // BLK))[None]
    scores = jnp.einsum("lqd,md->qlm", queries, keys, preferred_element_type=F32) * HD ** (-0.5)
    scores = jnp.where(allowed, scores, NEG_BIG)
    shifted = jnp.exp(scores - jnp.max(scores, axis=-1, keepdims=True))
    probs = (shifted / jnp.sum(shifted, axis=-1, keepdims=True)).astype(BF16)
    context = (
        jnp.einsum("qlm,md->lqd", probs, values, preferred_element_type=F32)
        .reshape(length, q_width)
        .astype(BF16)
    )
    queries = queries.reshape(length, q_width)
    u_attn_f = dot(context, a_o)
    u_attn = u_attn_f.astype(BF16)
    attn_part = dot_nt(context, w_o_t) + dot(u_attn, b_o)
    attn_recv = swap(theirs(attn_part).astype(BF16))
    attn_proj = mine(attn_part) + attn_recv.astype(F32)
    laurel_low = dot(h_own, left).astype(BF16)
    laurel_wide = dot_nt(laurel_low, right_t)
    combined = (
        x_float + normed(attn_proj, norm_gains[1]) + x_norm + normed(laurel_wide, norm_gains[2])
    ) * RSQRT_TWO
    h2_own = normed(combined, norm_gains[3]).astype(BF16)

    h2_peer = swap(h2_own)
    h2 = jnp.concatenate(
        [v[s * part : (s + 1) * part] for s in range(STREAMS) for v in (h2_own, h2_peer)], axis=0
    )
    u_ffn = dot(h2, a_ffn).astype(BF16)
    u_qkv_t, qkv_in_t, a_o_t, a_ffn_t, u_ffn_t = u_qkv.T, qkv_in.T, a_o.T, a_ffn.T, u_ffn.T
    u_attn_t = u_attn.T
    pack_3, _, _ = lax.optimization_barrier((pack_3, full_2, h2_own))
    full_3 = gather(pack_3)
    partial = ffn_up(h2, full_1, split, 0, u_ffn, bgu, ad_t, None)
    ud, g_pre, u_pre, hidden = ffn_up(
        h2, full_2, blocks - split, split, u_ffn, bgu, ad_t, partial
    )
    ud_t = ud.astype(BF16).T
    (queries, keys, values, raw, context, u_qkv_t, qkv_in_t, a_o_t, a_ffn_t, u_ffn_t, b_qkv, b_o, cos, sin, u_attn_t, ud_t, hidden) = (
        lax.optimization_barrier(
            (queries, keys, values, raw, context, u_qkv_t, qkv_in_t, a_o_t, a_ffn_t, u_ffn_t, b_qkv, b_o, cos, sin, u_attn_t, ud_t, hidden)
        )
    )
    ple_parts, layer_out = [], []
    own_0, peer_0, own_1, peer_1 = ffn_down(hidden, full_3, ud, b_d, 0, 2)
    hidden, peer_0, peer_1 = lax.optimization_barrier((hidden, peer_0, peer_1))
    own_2, peer_2 = ffn_down(hidden, full_3, ud, b_d, 2, 1)
    recv_0 = swap(peer_0)
    recv_1 = swap(peer_1)
    for s, (own, recv) in enumerate(((own_0, recv_0), (own_1, recv_1), (own_2, None))):
        if s == 0:
            recv, own_2 = lax.optimization_barrier((recv, own_2))
        if s == 2:
            peer_2, _ = lax.optimization_barrier((peer_2, ple_parts[0][1]))
            recv = swap(peer_2)
        whole, d_ffn_s, d_first_s = ple_both(
            combined, own, recv, out_grad, per_layer_input, full_3, ple_column, norm_gains,
            layer_out, s,
        )
        layer_out = [whole]
        ple_parts.append([d_ffn_s, swap(d_ffn_s), d_first_s])
    packs = (full_1, full_2, full_3)
    common = (g_pre, u_pre, bgu, ad_t, b_d, u_ffn_t, a_ffn_t, h2, ud_t)
    lau_column = lau_at // (2 * lr)
    d_attn_own, d_attn_recv, branch, waiting, sums = [], [], [], [], None

    def between(branch):
        d_first_s, d_h2_own, d_h2_recv, s = waiting.pop(0)
        d_attn_s, *branch = between_bwd(
            d_first_s, combined, d_h2_own, d_h2_recv, attn_proj, laurel_low, full_1, lau_column,
            norm_gains, branch, s,
        )
        d_attn_own.append(d_attn_s)
        d_attn_recv.append(swap(d_attn_s))
        return branch

    for s in range(STREAMS):
        own, recv, first = ple_parts[s]
        if s >= 2:
            own, _ = lax.optimization_barrier((own, d_attn_own[s - 2]))
        elif s == 1:
            own, _ = lax.optimization_barrier((own, d_h2_peer))
        *sums, d_h2_own, d_h2_peer = ffn_bwd(
            own, recv, packs, split, *common, s, sums, BF16 if s == STREAMS - 1 else F32
        )
        send_ffn = sums[0]
        if waiting:
            first_w, own_w, recv_w, s_w = waiting[0]
            if s == STREAMS - 1:
                send_ffn, recv_w = lax.optimization_barrier((send_ffn, recv_w))
            else:
                recv_w, _ = lax.optimization_barrier((recv_w, d_h2_peer))
            waiting[0] = (first_w, own_w, recv_w, s_w)
            waiting.append((first, d_h2_own, swap(d_h2_peer), s))
            branch = between(branch)
        else:
            waiting.append((first, d_h2_own, swap(d_h2_peer), s))
    send_ffn, d_attn_recv[0] = lax.optimization_barrier((send_ffn, d_attn_recv[0]))
    got_ffn = lax.all_gather(send_ffn, "dp", axis=0, tiled=False)
    d_branch, d_norm = between(branch)

    pieces = d_attn_own + d_attn_recv
    d_h_peer_0, d_h_peer_1, d_raw, d_u, send_heads, grad_attn_out = attention_bwd(
        pieces, t.astype(jnp.int32).reshape(1), full_1, qkv_at, wo_at // HD, b_o, a_o_t, queries, keys,
        values, probs, raw, head_gains, cos, sin, context, u_qkv_t, b_qkv, qkv_in_t,
        u_attn_t,
    )
    d_h_recv_0 = swap(d_h_peer_0)
    d_raw, d_u, got_ffn = lax.optimization_barrier((d_raw, d_u, got_ffn))
    got_heads = lax.all_gather(send_heads, "dp", axis=0, tiled=False)
    send = jnp.concatenate(
        [sums[1].astype(BF16), grad_attn_out, dot_tn(d_u, h_all).astype(BF16)], axis=0
    ).T
    send, d_h_peer_1 = lax.optimization_barrier((send, d_h_peer_1))
    d_h_recv_1 = swap(d_h_peer_1)
    got = lax.all_to_all(send, ("dp", "tensor"), 0, 0, tiled=True).reshape(2 * dp, -1, send.shape[1])
    out_ffn_out, out_down_in = ffn_adapter_sums(got_ffn, ids, adapters, units)
    d_h_own = dot_nt(mine(d_raw), w_qkv) + dot_nt(mine(d_u), qkv_in)
    got, out_ffn_out, out_down_in, d_h_own = lax.optimization_barrier(
        (got, out_ffn_out, out_down_in, d_h_own)
    )
    out_ffn_in, out_down_out, out_attn_out, out_qkv_in = shared_sums(got, ids, adapters)
    d_h_own, out_qkv_in = lax.optimization_barrier((d_h_own, out_qkv_in))
    final_args = (hidden_in, d_norm, d_branch, d_h_own)
    input_grad = final_bwd(*final_args, d_h_recv_0, norm_gains, [], 0)
    input_grad = final_bwd(*final_args, d_h_recv_1, norm_gains, [input_grad], 1)
    got_heads, input_grad = lax.optimization_barrier((got_heads, input_grad))
    out_qkv_out, out_attn_in = head_sums(got_heads, ids, adapters, qkv_width)
    return (
        layer_out[0],
        input_grad,
        jnp.swapaxes(out_qkv_in, 1, 2),
        out_qkv_out,
        jnp.swapaxes(out_attn_in, 1, 2),
        out_attn_out,
        jnp.swapaxes(out_ffn_in, 1, 2),
        out_ffn_out,
        jnp.swapaxes(out_down_in, 1, 2),
        out_down_out,
    )


def solution(mesh):
    in_specs = (
        P(("dp", "tensor"), None),
        P(("dp", "tensor"), None),
        P(("dp", "tensor"), None),
        P("dp"),
        P("dp", "tensor", None),
        P("tensor", "dp"),
        P("dp", None, "tensor"),
        P("tensor", "dp"),
        P("dp", None),
        P(None, "dp"),
        P("dp", None),
        P(None, "dp"),
        P(),
        P(),
        P(),
        P(None, None, "tensor", None),
        P(None, "tensor", None),
        P(),
        P(),
        P(None, None, None, "tensor"),
        P(None, "tensor", None),
        P(),
    )
    out_specs = (
        P(("dp", "tensor"), None),
        P(("dp", "tensor"), None),
        P(None, ("dp", "tensor"), None),
        P(None, None, "tensor", None),
        P(None, "tensor", None),
        P(None, None, ("dp", "tensor")),
        P(None, ("dp", "tensor"), None),
        P(None, None, None, "tensor"),
        P(None, "tensor", None),
        P(None, None, ("dp", "tensor")),
    )
    return jax.shard_map(
        on_device, mesh=mesh, in_specs=in_specs, out_specs=out_specs, check_vma=False
    )
```

```python
import functools

import jax
import jax.numpy as jnp
from jax import lax
from jax.experimental import pallas as pl
from jax.experimental.pallas import tpu as pltpu
from jax.sharding import PartitionSpec as P

HEADS = 8
KV = 2
HD = 256
WIN = 512
BLK = 256
RANK = 16
UB = 512
GB = 2 * UB

NORM_EPSILON = 1e-06
RSQRT_TWO = 0.7071067811865476
ROPE_BASE = 10000.0
NEG_BIG = -1e30
GELU_A = 0.7978845608028654
GELU_B = 0.044715

F32 = jnp.float32
BF16 = jnp.bfloat16
VMEM_LIMIT = 63 * 1024 * 1024
DOWN_CHUNK = 512
STREAMS = 3


def dot(a, b):
    return lax.dot_general(a, b, (((1,), (0,)), ((), ())), preferred_element_type=F32)


def dot_nt(a, b):
    return lax.dot_general(a, b, (((1,), (1,)), ((), ())), preferred_element_type=F32)


def dot_tn(a, b):
    return lax.dot_general(a, b, (((0,), (0,)), ((), ())), preferred_element_type=F32)


def inv_rms(v):
    return lax.rsqrt(jnp.mean(v * v, axis=-1, keepdims=True) + NORM_EPSILON)


def normed(v, gains):
    return v * inv_rms(v) * gains


def norm_back(v, gains, cotangent):
    r = inv_rms(v)
    gc = gains * cotangent
    return r * gc - v * (r * r * r * jnp.mean(v * gc, axis=-1, keepdims=True))


def gelu_tanh(v):
    return 0.5 * v * (1.0 + jnp.tanh(GELU_A * (v + GELU_B * v * v * v)))


def gelu_both(v):
    v2 = v * v
    th = jnp.tanh(GELU_A * v * (1.0 + GELU_B * v2))
    half = 0.5 * (1.0 + th)
    slope = half + 0.5 * v * (1.0 - th * th) * (GELU_A * (1.0 + 3.0 * GELU_B * v2))
    return v * half, slope


def const_spec(shape):
    return pl.BlockSpec(shape, lambda *_: (0,) * len(shape), pipeline_mode=pl.Buffered(1))


def any_spec():
    return pl.BlockSpec(memory_space=pl.ANY)


def params():
    return pltpu.CompilerParams(vmem_limit_bytes=VMEM_LIMIT)


def pack_shards(gate_up, first, count, rest, rows, name):
    width = count * GB + sum(n for _, n in rest)

    def body(*refs):
        out = refs[-1]
        for b in range(count):
            cs = slice(b * UB, (b + 1) * UB)
            out[:, b * GB : b * GB + UB] = refs[0][:, 0, cs]
            out[:, b * GB + UB : (b + 1) * GB] = refs[0][:, 1, cs]
        at = count * GB
        for ref, (value, n) in zip(refs[1 if count else 0 : -1], rest):
            out[:, at : at + n] = ref[...] if value.shape == (rows, n) else ref[...].T
            at += n

    block = (pl.Element(rows), pl.Element(2), pl.Element(count * UB))
    gate_spec = [pl.BlockSpec(block, lambda i: (0, 0, first * UB))] if count else []
    return pl.pallas_call(
        body,
        grid=(1,),
        in_specs=gate_spec + [const_spec(v.shape) for v, _ in rest],
        out_specs=const_spec((rows, width)),
        out_shape=jax.ShapeDtypeStruct((rows, width), BF16),
        compiler_params=params(),
        name=name,
    )(*([gate_up] if count else []), *[v for v, _ in rest])


def ffn_up(h2, packed, blocks, first, u_low, bgu, ad_t, prev):
    rows, width = h2.shape
    units = ad_t.shape[1]
    tile = rows // 2
    sub = 256

    def body(*refs):
        h_ref, w_ref, ul_ref, bgu_ref, ad_ref = refs[:5]
        g_out, u_out, hid_out, ud_out = refs[-4:]
        j = pl.program_id(0)

        @pl.when(j == 0)
        def _():
            if prev is None:
                ud_out[...] = jnp.zeros_like(ud_out)
            else:
                ud_out[...] = refs[5][...]

        for k in range(rows // tile):
            at_rows = slice(k * tile, (k + 1) * tile)
            h = h_ref[at_rows, :]
            ul = ul_ref[at_rows, :]
            for n in range(UB // sub):
                cs = slice(n * sub, (n + 1) * sub)
                us = slice(UB + n * sub, UB + (n + 1) * sub)
                g = dot(h, w_ref[:, cs]) + dot(ul, bgu_ref[:, cs])
                u = dot(h, w_ref[:, us]) + dot(ul, bgu_ref[:, us])
                g_out[at_rows, cs] = g.astype(BF16)
                u_out[at_rows, cs] = u.astype(BF16)
                hid_out[at_rows, cs] = (gelu_tanh(g) * u).astype(BF16)
            ud_out[at_rows, :] += dot_nt(hid_out[at_rows, :], ad_ref[...])

    in_specs = [
        const_spec((rows, width)),
        pl.BlockSpec((width, GB), lambda j: (0, j)),
        const_spec((rows, 2 * RANK)),
        pl.BlockSpec((2 * RANK, GB), lambda j: (0, first + j)),
        pl.BlockSpec((RANK, UB), lambda j: (0, first + j)),
    ]
    args = [h2, packed, u_low, bgu, ad_t]
    aliases = {}
    if prev is not None:
        in_specs += [const_spec((rows, RANK)), any_spec(), any_spec(), any_spec()]
        args += list(prev)
        aliases = {6: 0, 7: 1, 8: 2}
    unit_block = pl.BlockSpec((rows, UB), lambda j: (0, first + j))
    shape = jax.ShapeDtypeStruct
    g, u, hidden, ud = pl.pallas_call(
        body,
        grid=(blocks,),
        in_specs=in_specs,
        out_specs=[unit_block] * 3 + [const_spec((rows, RANK))],
        out_shape=[shape((rows, units), BF16)] * 3 + [shape((rows, RANK), F32)],
        input_output_aliases=aliases,
        compiler_params=params(),
        cost_estimate=pl.CostEstimate(
            flops=4 * rows * width * UB * blocks,
            bytes_accessed=2 * width * GB * blocks,
            transcendentals=rows * UB * blocks,
        ),
        name="ffn_up",
    )(*args)
    return ud, g, u, hidden


def ffn_down(hidden, packed, ud, bd, rb, streams):
    rows, units = hidden.shape
    width = packed.shape[0]
    part = rows // (2 * STREAMS)
    r = 2 * part * streams
    chunk = DOWN_CHUNK

    def body(h_ref, w_ref, ud_ref, bd_ref, *outs):
        total = dot_nt(h_ref[...], w_ref[...]) + dot(ud_ref[...].astype(BF16), bd_ref[...])
        for n, out in enumerate(outs):
            out[...] = total[n * part : (n + 1) * part].astype(out.dtype)

    row_const = lambda n: pl.BlockSpec((r, n), lambda j: (rb, 0), pipeline_mode=pl.Buffered(1))
    column = pl.BlockSpec((part, chunk), lambda j: (0, j))
    shape = jax.ShapeDtypeStruct
    return pl.pallas_call(
        body,
        grid=(width // chunk,),
        in_specs=[
            row_const(units),
            pl.BlockSpec((chunk, units), lambda j: (j, 0)),
            row_const(RANK),
            pl.BlockSpec((RANK, chunk), lambda j: (0, j)),
        ],
        out_specs=[column] * (2 * streams),
        out_shape=[shape((part, width), F32), shape((part, width), BF16)] * streams,
        compiler_params=params(),
        cost_estimate=pl.CostEstimate(
            flops=2 * r * width * units, bytes_accessed=2 * width * units, transcendentals=0
        ),
        name="ffn_down",
    )(hidden, packed, ud, bd)


def ffn_bwd(own, peer, packs, split, g_pre, u_pre, bgu, ad_t, bd, u_t, a_in_t, h2, ud_t, rb, base, grad_type):
    half, width = own.shape
    r = 2 * half
    units = ad_t.shape[1]
    first, blocks = 0, units // UB
    sub = 256

    def body(*refs):
        own_ref, peer_ref, g_ref, u_ref, bgu_ref, ad_ref, bd_ref, ut_ref, ain_ref = refs[:9]
        pack_refs = refs[9 : 9 + len(packs)]
        at = 9 + len(packs)
        h2_any, udt_ref = refs[at : at + 2]
        at += 2
        if base is not None:
            base_ref, base_in = refs[at : at + 2]
            at += 2
        grad_out, in_out, own_out, peer_out = refs[at : at + 4]
        at += 4
        df, acc, wbuf, dd, du, dgu, hs, sem, h2_sem = refs[at:]
        j = pl.program_id(0)
        slot = lax.rem(j, 2)

        def copy(ref, column, where, part):
            lo, n = ((2 * UB, UB), (0, 2 * UB))[part]
            return pltpu.make_async_copy(
                ref.at[:, pl.ds(column, n)], wbuf.at[where, :, pl.ds(lo, n)], sem.at[where, part]
            )

        def fetch(step, where):
            block = first + step
            copy(pack_refs[2], pl.multiple_of(block * UB, UB), where, 0).start()

            @pl.when(block < split)
            def _():
                copy(pack_refs[0], pl.multiple_of(block * GB, GB), where, 1).start()

            @pl.when(block >= split)
            def _():
                copy(pack_refs[1], pl.multiple_of((block - split) * GB, GB), where, 1).start()

        @pl.when(j == 0)
        def _():
            fetch(j, 0)
            df[0:half, :] = own_ref[...]
            df[half:r, :] = peer_ref[...]
            acc[...] = jnp.zeros_like(acc)
            du[...] = jnp.zeros_like(du)
            dd[...] = dot_nt(df[...], bd_ref[...]).astype(BF16)

        @pl.when(j + 1 < blocks)
        def _():
            fetch(j + 1, 1 - slot)

        copy(pack_refs[2], 0, slot, 0).wait()
        for n in range(UB // sub):
            cs = slice(n * sub, (n + 1) * sub)
            dh = dot(df[...], wbuf[slot, :, 2 * UB + n * sub : 2 * UB + (n + 1) * sub])
            dh += dot(dd[...], ad_ref[:, cs])
            g = g_ref[:, cs].astype(F32)
            u = u_ref[:, cs].astype(F32)
            act, slope = gelu_both(g)
            dgu[:, cs] = (dh * u * slope).astype(BF16)
            dgu[:, UB + n * sub : UB + (n + 1) * sub] = (dh * act).astype(BF16)
            hs[:, cs] = (act * u).astype(BF16)
        copy(pack_refs[0], 0, slot, 1).wait()
        d_both = dgu[...]
        for c in range(width // 512):
            cc = slice(c * 512, (c + 1) * 512)
            acc[:, cc] += dot_nt(d_both, wbuf[slot, cc, 0 : 2 * UB])
        du[...] += dot_nt(d_both, bgu_ref[...])
        both = dot(ut_ref[...], d_both)
        rows = (2.0 * both[:RANK, :UB], 2.0 * both[RANK:, UB:], dot_tn(dd[...], hs[...]))
        for m, row in enumerate(rows):
            ms = slice(m * RANK, (m + 1) * RANK)
            if base is not None:
                row = row + base_ref[ms, :]
            grad_out[ms, :] = row.astype(grad_out.dtype)

        @pl.when(j == blocks - 1)
        def _():
            down = dot(udt_ref[...], df[...])
            rows_copy = pltpu.make_async_copy(h2_any.at[pl.ds(rb * r, r), :], df, h2_sem)
            rows_copy.start()
            du_low = du[...].astype(BF16)
            total = acc[...] + dot(du_low, ain_ref[...])
            own_out[...] = total[:half]
            peer_out[...] = total[half:].astype(BF16)
            rows_copy.wait()
            up = dot_tn(du_low, df[...])
            down = 2.0 * down
            if base is not None:
                up = up + base_in[0 : 2 * RANK, :]
                down = down + base_in[2 * RANK : 3 * RANK, :]
            in_out[0 : 2 * RANK, :] = up.astype(grad_type)
            in_out[2 * RANK : 3 * RANK, :] = down.astype(grad_type)

    rows_block = lambda: pl.BlockSpec((r, UB), lambda j: (rb, first + j))
    unit_block = lambda: pl.BlockSpec((RANK, UB), lambda j: (0, first + j))
    shape = jax.ShapeDtypeStruct
    in_specs = [
        const_spec((half, width)),
        const_spec((half, width)),
        rows_block(),
        rows_block(),
        pl.BlockSpec((2 * RANK, 2 * UB), lambda j: (0, first + j)),
        unit_block(),
        const_spec((RANK, width)),
        pl.BlockSpec((2 * RANK, r), lambda j: (0, rb), pipeline_mode=pl.Buffered(1)),
        const_spec((2 * RANK, width)),
    ] + [any_spec() for _ in packs]
    args = [own, peer, g_pre, u_pre, bgu, ad_t, bd, u_t, a_in_t, *packs]
    grad_block = lambda: pl.BlockSpec((3 * RANK, UB), lambda j: (0, first + j))
    in_specs += [
        any_spec(),
        pl.BlockSpec((RANK, r), lambda j: (0, rb), pipeline_mode=pl.Buffered(1)),
    ]
    args += [h2, ud_t]
    if base is not None:
        in_specs += [grad_block(), const_spec((3 * RANK, width))]
        args += list(base)
    out_specs = [
        grad_block(),
        const_spec((3 * RANK, width)),
        const_spec((half, width)),
        const_spec((half, width)),
    ]
    out_shape = [
        shape((3 * RANK, units), grad_type),
        shape((3 * RANK, width), grad_type),
        shape((half, width), F32),
        shape((half, width), BF16),
    ]
    return pl.pallas_call(
        body,
        grid=(blocks,),
        in_specs=in_specs,
        out_specs=out_specs,
        out_shape=out_shape,
        scratch_shapes=[
            pltpu.VMEM((r, width), BF16),
            pltpu.VMEM((r, width), F32),
            pltpu.VMEM((2, width, 3 * UB), BF16),
            pltpu.VMEM((r, RANK), BF16),
            pltpu.VMEM((r, 2 * RANK), F32),
            pltpu.VMEM((r, 2 * UB), BF16),
            pltpu.VMEM((r, UB), BF16),
            pltpu.SemaphoreType.DMA((2, 2)),
            pltpu.SemaphoreType.DMA,
        ],
        compiler_params=params(),
        cost_estimate=pl.CostEstimate(
            flops=6 * r * width * UB * blocks,
            bytes_accessed=6 * width * UB * blocks,
            transcendentals=r * UB * blocks,
        ),
        name="ffn_bwd",
    )(*args)


def ple_both(combined, ffn_own, ffn_recv, out_grad, ple_in, packed, column, gains, prev, rb):
    half, width = ffn_own.shape
    rows = combined.shape[0]
    pd = ple_in.shape[1]
    tile = half

    def body(c_ref, fo_ref, fr_ref, og_ref, pi_ref, w_ref, gain_ref, *refs):
        out_ref, dffn_ref, dfirst_ref = refs[-3:]
        ffn = fo_ref[...] + fr_ref[...].astype(F32)
        y = c_ref[...] + normed(ffn, gain_ref[4:5, :])
        pre = dot(y.astype(BF16), w_ref[:, 0:pd])
        side = pi_ref[...].astype(F32)
        act, slope = gelu_both(pre)
        wide = dot_nt((act * side).astype(BF16), w_ref[:, pd : 2 * pd])
        out_ref[...] = (y + normed(wide, gain_ref[5:6, :])).astype(BF16)
        cot = og_ref[...].astype(F32)
        d_wide = norm_back(wide, gain_ref[5:6, :], cot).astype(BF16)
        d_pre = (dot(d_wide, w_ref[:, pd : 2 * pd]) * side * slope).astype(BF16)
        d_first = cot + dot_nt(d_pre, w_ref[:, 0:pd])
        dfirst_ref[...] = d_first
        dffn_ref[...] = norm_back(ffn, gain_ref[4:5, :], d_first).astype(BF16)

    n = half // tile
    here = lambda w: pl.BlockSpec((tile, w), lambda i: (i, 0))
    there = lambda w: pl.BlockSpec((tile, w), lambda i: (rb * n + i, 0))
    shape = jax.ShapeDtypeStruct
    return pl.pallas_call(
        body,
        grid=(n,),
        in_specs=[
            there(width),
            here(width),
            here(width),
            there(width),
            there(pd),
            pl.BlockSpec((width, 2 * pd), lambda i: (0, column), pipeline_mode=pl.Buffered(1)),
            const_spec(gains.shape),
        ]
        + [any_spec() for _ in prev],
        out_specs=[there(width), here(width), here(width)],
        out_shape=[
            shape((rows, width), BF16),
            shape((half, width), BF16),
            shape((half, width), F32),
        ],
        input_output_aliases={7: 0} if prev else {},
        compiler_params=params(),
        cost_estimate=pl.CostEstimate(
            flops=8 * half * width * pd, bytes_accessed=20 * half * width, transcendentals=0
        ),
        name="ple_both",
    )(combined, ffn_own, ffn_recv, out_grad, ple_in, packed, gains, *prev)


def between_bwd(d_first, combined, dh_own, dh_recv, attn_proj, low, packed, column, gains, prev, rb):
    half, width = d_first.shape
    rows = combined.shape[0]
    lr = low.shape[1]
    tile = half

    def body(df_ref, c_ref, ho_ref, hr_ref, ap_ref, low_ref, w_ref, gain_ref, *refs):
        da_ref, db_ref, dn_ref = refs[-3:]
        d_h2 = ho_ref[...] + hr_ref[...].astype(F32)
        d_comb = df_ref[...] + norm_back(c_ref[...], gain_ref[3:4, :], d_h2)
        d_branch = d_comb * RSQRT_TWO
        db_ref[...] = d_branch
        da_ref[...] = norm_back(ap_ref[...], gain_ref[1:2, :], d_branch).astype(BF16)
        wide = dot_nt(low_ref[...], w_ref[:, lr : 2 * lr])
        d_wide = norm_back(wide, gain_ref[2:3, :], d_branch).astype(BF16)
        d_low = dot(d_wide, w_ref[:, lr : 2 * lr]).astype(BF16)
        dn_ref[...] = d_branch + dot_nt(d_low, w_ref[:, 0:lr])

    n = half // tile
    here = lambda w: pl.BlockSpec((tile, w), lambda i: (i, 0))
    there = lambda w: pl.BlockSpec((tile, w), lambda i: (rb * n + i, 0))
    shape = jax.ShapeDtypeStruct
    return pl.pallas_call(
        body,
        grid=(n,),
        in_specs=[
            here(width),
            there(width),
            here(width),
            here(width),
            there(width),
            there(lr),
            pl.BlockSpec((width, 2 * lr), lambda i: (0, column), pipeline_mode=pl.Buffered(1)),
            const_spec(gains.shape),
        ]
        + [any_spec() for _ in prev],
        out_specs=[here(width), there(width), there(width)],
        out_shape=[
            shape((half, width), BF16),
            shape((rows, width), F32),
            shape((rows, width), F32),
        ],
        input_output_aliases={8: 1, 9: 2} if prev else {},
        compiler_params=params(),
        cost_estimate=pl.CostEstimate(
            flops=6 * half * width * lr, bytes_accessed=26 * half * width, transcendentals=0
        ),
        name="between_bwd",
    )(d_first, combined, dh_own, dh_recv, attn_proj, low, packed, gains, *prev)


def attention_bwd(pieces, turn, packed, qkv_column, wo_column, bo, ao_t, q, k, v, probs, raw, gains, cos, sin,
                  context, u_t, b_qkv, a_in_t, u_attn_t):
    length, q_width = q.shape
    width = packed.shape[0]
    heads = q_width // HD
    half_hd = HD // 2
    scale = HD ** (-0.5)
    n_blocks = length // BLK
    span = WIN // BLK
    quarter = pieces[0].shape[0]
    count = len(pieces)
    total = q_width + 2 * HD
    here = length // 2

    def unrotate(d, cos_v, sin_v):
        d1, d2 = d[:, :half_hd], d[:, half_hd:]
        return jnp.concatenate([d1 * cos_v + d2 * sin_v, d2 * cos_v - d1 * sin_v], axis=1)

    def body(turn_ref, *refs):
        piece_refs = refs[:count]
        (wo_ref, w_any, bo_ref, ao_ref, q_ref, k_ref, v_ref, p_ref, rq_ref, rk_ref, gain_ref, cos_ref,
         sin_ref, ctx_ref, ut_ref, b_ref, ain_ref, uat_ref, peer_0, peer_1, draw, du_out, heads_out, out_rows,
         da, du, dk, dv, wq, sem) = refs[count:]
        hh = pl.program_id(0)
        weights = pltpu.make_async_copy(w_any.at[:, pl.ds(qkv_column, total)], wq, sem)

        @pl.when(hh == 0)
        def _():
            weights.start()
            shift = turn_ref[0] * here
            for i, ref in enumerate(piece_refs):
                place = lax.rem(shift + i * quarter, length)
                da[pl.ds(pl.multiple_of(place, quarter), quarter), :] = ref[...]
            du[...] = dot_nt(da[...], bo_ref[...]).astype(BF16)
            dk[...] = jnp.zeros_like(dk)
            dv[...] = jnp.zeros_like(dv)

        dctx = (dot(da[...], wo_ref[...]) + dot(du[...], ao_ref[...])).astype(BF16)
        cos_v, sin_v = cos_ref[...], sin_ref[...]
        column = pl.multiple_of(hh * HD, HD)
        for i in range(n_blocks):
            low, high = max(0, i - span + 1) * BLK, (i + 1) * BLK
            rows = slice(i * BLK, (i + 1) * BLK)
            d_i = dctx[rows]
            p_i = p_ref[0, rows, low:high]
            p_f = p_i.astype(F32)
            dp = dot_nt(d_i, v_ref[low:high, :])
            ds = p_f * (dp - jnp.sum(p_f * dp, axis=-1, keepdims=True))
            ds = ds.astype(BF16)
            dq = dot(ds, k_ref[low:high, :]) * scale
            dk[low:high, :] += dot_tn(ds, q_ref[rows, :])
            dv[low:high, :] += dot_tn(p_i, d_i)
            back = norm_back(rq_ref[rows, :], gain_ref[0:1, :], unrotate(dq, cos_v[rows], sin_v[rows]))
            draw[rows, pl.ds(column, HD)] = back.astype(BF16)
        heads_out[:, pl.ds(column, HD)] = (
            2.0 * dot(ut_ref[0:RANK, :], draw[:, pl.ds(column, HD)])
        ).astype(BF16)
        heads_out[:, pl.ds(pl.multiple_of(total + hh * HD, HD), HD)] = dot_tn(
            du[...], ctx_ref[...]
        ).astype(BF16)

        @pl.when(hh == heads - 1)
        def _():
            back = norm_back(rk_ref[...], gain_ref[1:2, :], unrotate(dk[...] * scale, cos_v, sin_v))
            at_k, at_v = slice(q_width, q_width + HD), slice(q_width + HD, total)
            draw[:, at_k] = back.astype(BF16)
            draw[:, at_v] = dv[...].astype(BF16)
            for m, where in ((1, at_k), (2, at_v)):
                got = dot(ut_ref[m * RANK : (m + 1) * RANK, :], draw[:, where])
                heads_out[:, where] = (2.0 * got).astype(BF16)
            du_out[...] = dot_nt(draw[...], b_ref[...]).astype(BF16)
            out_rows[...] = (2.0 * dot(uat_ref[...], da[...])).astype(BF16)
            weights.wait()
            theirs = pl.multiple_of((1 - turn_ref[0]) * here, here)
            d_rows = draw[pl.ds(theirs, here), :]
            u_rows = du_out[pl.ds(theirs, here), :]
            for c in range(width // 512):
                cc = slice(c * 512, (c + 1) * 512)
                got = dot_nt(d_rows, wq[cc, :]) + dot(u_rows, ain_ref[:, cc])
                peer_0[:, cc] = got[: here // 2].astype(BF16)
                peer_1[:, cc] = got[here // 2 :].astype(BF16)

    shape = jax.ShapeDtypeStruct
    head_block = lambda: pl.BlockSpec((length, HD), lambda h: (0, h))
    return pl.pallas_call(
        body,
        grid=(heads,),
        in_specs=[pl.BlockSpec(memory_space=pltpu.SMEM)]
        + [const_spec(piece.shape) for piece in pieces]
        + [
            pl.BlockSpec((width, HD), lambda h: (0, wo_column + h)),
            any_spec(),
            const_spec(bo.shape),
            pl.BlockSpec((RANK, HD), lambda h: (0, h)),
            head_block(),
            const_spec(k.shape),
            const_spec(v.shape),
            pl.BlockSpec((1, length, length), lambda h: (h, 0, 0)),
            head_block(),
            pl.BlockSpec((length, HD), lambda h: (0, heads), pipeline_mode=pl.Buffered(1)),
            const_spec(gains.shape),
            const_spec(cos.shape),
            const_spec(sin.shape),
            head_block(),
            const_spec(u_t.shape),
            const_spec(b_qkv.shape),
            const_spec(a_in_t.shape),
            const_spec(u_attn_t.shape),
        ],
        out_specs=[
            const_spec((here // 2, width)),
            const_spec((here // 2, width)),
            const_spec((length, total)),
            const_spec((length, 3 * RANK)),
            const_spec((RANK, total + q_width)),
            const_spec((RANK, width)),
        ],
        out_shape=[
            shape((here // 2, width), BF16),
            shape((here // 2, width), BF16),
            shape((length, total), BF16),
            shape((length, 3 * RANK), BF16),
            shape((RANK, total + q_width), BF16),
            shape((RANK, width), BF16),
        ],
        scratch_shapes=[
            pltpu.VMEM((length, width), BF16),
            pltpu.VMEM((length, RANK), BF16),
            pltpu.VMEM((length, HD), F32),
            pltpu.VMEM((length, HD), F32),
            pltpu.VMEM((width, total), BF16),
            pltpu.SemaphoreType.DMA,
        ],
        compiler_params=params(),
        cost_estimate=pl.CostEstimate(flops=1024 * 1024, bytes_accessed=1024 * 1024, transcendentals=0),
        name="attention_bwd",
    )(turn, *pieces, packed, packed, bo, ao_t, q, k, v, probs, raw, raw, gains, cos, sin, context, u_t, b_qkv,
      a_in_t, u_attn_t)


def final_bwd(x, d_norm, d_branch, dh_own, dh_recv, gains, prev, rb):
    rows, width = x.shape
    half = rows // 2
    tile = half // 2

    def body(x_ref, dn_ref, db_ref, ho_ref, hr_ref, gain_ref, *refs):
        out_ref = refs[-1]
        total = dn_ref[...] + ho_ref[...] + hr_ref[...].astype(F32)
        out_ref[...] = db_ref[...] + norm_back(x_ref[...].astype(F32), gain_ref[0:1, :], total)

    n = half // tile
    here = pl.BlockSpec((tile, width), lambda i: (i, 0))
    there = pl.BlockSpec((tile, width), lambda i: (rb * n + i, 0))
    return pl.pallas_call(
        body,
        grid=(n,),
        in_specs=[there] * 4 + [here, const_spec(gains.shape)] + [any_spec() for _ in prev],
        out_specs=there,
        out_shape=jax.ShapeDtypeStruct((rows, width), F32),
        input_output_aliases={6: 0} if prev else {},
        compiler_params=params(),
        cost_estimate=pl.CostEstimate(
            flops=20 * half * width, bytes_accessed=20 * half * width, transcendentals=0
        ),
        name="final_bwd",
    )(x, d_norm, d_branch, dh_own, dh_recv, gains, *prev)


def add_by_adapter(ids_ref, got_ref, total, seqs, share):
    total[...] = jnp.zeros_like(total)

    def step(i, carry):
        where = ids_ref[i // share]
        total[where] += got_ref[i].astype(F32)
        return carry

    lax.fori_loop(0, seqs, step, 0)


def ffn_adapter_sums(got, ids, adapters, units):
    seqs = got.shape[0]
    tile = 1024

    def body(ids_ref, got_ref, out_ref, down_ref, total):
        add_by_adapter(ids_ref, got_ref, total, seqs, 1)
        out_ref[:, :, 0, :] = total[:, :RANK, :]
        out_ref[:, :, 1, :] = total[:, RANK : 2 * RANK, :]
        down_ref[...] = total[:, 2 * RANK :, :]

    return pl.pallas_call(
        body,
        grid=(units // tile,),
        in_specs=[
            pl.BlockSpec(memory_space=pltpu.SMEM),
            pl.BlockSpec((seqs, 3 * RANK, tile), lambda i: (0, 0, i)),
        ],
        out_specs=[
            pl.BlockSpec((adapters, RANK, 2, tile), lambda i: (0, 0, 0, i)),
            pl.BlockSpec((adapters, RANK, tile), lambda i: (0, 0, i)),
        ],
        out_shape=[
            jax.ShapeDtypeStruct((adapters, RANK, 2, units), F32),
            jax.ShapeDtypeStruct((adapters, RANK, units), F32),
        ],
        scratch_shapes=[pltpu.VMEM((adapters, 3 * RANK, tile), F32)],
        compiler_params=params(),
        cost_estimate=pl.CostEstimate(
            flops=6 * seqs * RANK * units, bytes_accessed=6 * seqs * RANK * units, transcendentals=0
        ),
        name="adapter_sums",
    )(ids, got)


def shared_sums(got, ids, adapters):
    seqs, rows, columns = got.shape
    cuts = (2 * RANK, RANK, RANK, 3 * RANK)

    def body(ids_ref, got_ref, *refs):
        total = refs[-1]
        add_by_adapter(ids_ref, got_ref, total, seqs, 2)
        for n in range(adapters):
            flipped = total[n].T
            at = 0
            for ref, cut in zip(refs, cuts):
                ref[n] = flipped[at : at + cut, :]
                at += cut

    return pl.pallas_call(
        body,
        grid=(1,),
        in_specs=[pl.BlockSpec(memory_space=pltpu.SMEM), const_spec(got.shape)],
        out_specs=[const_spec((adapters, cut, rows)) for cut in cuts],
        out_shape=[jax.ShapeDtypeStruct((adapters, cut, rows), F32) for cut in cuts],
        scratch_shapes=[pltpu.VMEM((adapters, rows, columns), F32)],
        compiler_params=params(),
        name="shared_sums",
    )(ids, got)


def head_sums(got, ids, adapters, qkv_width):
    seqs, rank, columns = got.shape
    rest = columns - qkv_width

    def body(ids_ref, got_ref, qkv_ref, attn_ref, total):
        add_by_adapter(ids_ref, got_ref, total, seqs, 1)
        qkv_ref[:, :, 0, :] = total[:, :, :qkv_width]
        attn_ref[...] = total[:, :, qkv_width:]

    return pl.pallas_call(
        body,
        grid=(1,),
        in_specs=[pl.BlockSpec(memory_space=pltpu.SMEM), const_spec(got.shape)],
        out_specs=[const_spec((adapters, rank, 1, qkv_width)), const_spec((adapters, rank, rest))],
        out_shape=[
            jax.ShapeDtypeStruct((adapters, rank, 1, qkv_width), F32),
            jax.ShapeDtypeStruct((adapters, rank, rest), F32),
        ],
        scratch_shapes=[pltpu.VMEM((adapters, rank, columns), F32)],
        compiler_params=params(),
        name="head_sums",
    )(ids, got)


def rope_tables(length):
    half_dim = HD // 2
    inverse = ROPE_BASE ** (-jnp.arange(half_dim, dtype=F32) / half_dim)
    angles = jnp.arange(length, dtype=F32)[:, None] * inverse[None, :]
    return jnp.cos(angles), jnp.sin(angles)


def rotate(values, cos, sin):
    half_dim = HD // 2
    a, b = values[..., :half_dim], values[..., half_dim:]
    return jnp.concatenate([a * cos - b * sin, b * cos + a * sin], axis=-1)


def on_device(
    hidden_in,
    per_layer_input,
    out_grad,
    adapter_ids,
    weight_qkv,
    weight_attn_out,
    weight_gate_up,
    weight_down,
    laurel_left,
    laurel_right,
    per_layer_gate,
    per_layer_proj,
    norm_gains,
    head_gains,
    adapter_qkv_in,
    adapter_qkv_out,
    adapter_attn_in,
    adapter_attn_out,
    adapter_ffn_in,
    adapter_ffn_out,
    adapter_down_in,
    adapter_down_out,
):
    rows_here, width = hidden_in.shape
    dp = lax.axis_size("dp")
    length = rows_here * 2
    part = rows_here // STREAMS
    per_group = HEADS // KV
    q_width = per_group * HD
    qkv_width = q_width + 2 * HD
    units = weight_down.shape[0]
    blocks = units // UB
    adapters = adapter_qkv_in.shape[0]
    a = adapter_ids[0]
    t = lax.axis_index("tensor")

    def swap(v):
        return lax.ppermute(v, "tensor", [(0, 1), (1, 0)])

    def in_order(own, other):
        first = jnp.where(t == 0, own, other)
        second = jnp.where(t == 0, other, own)
        return jnp.concatenate([first, second], axis=0)

    def mine(v):
        return lax.dynamic_slice_in_dim(v, t * rows_here, rows_here, axis=0)

    def theirs(v):
        return lax.dynamic_slice_in_dim(v, (1 - t) * rows_here, rows_here, axis=0)

    split = blocks // 4
    rows_packed = laurel_left.shape[0]
    lr = laurel_left.shape[1]
    pd = per_layer_gate.shape[1]
    pack_1 = pack_shards(
        weight_gate_up, 0, split,
        [(weight_qkv[:, 0, :], qkv_width), (weight_attn_out, q_width), (laurel_left.T, lr), (laurel_right, lr)],
        rows_packed, "pack_1",
    )
    gather = lambda v: lax.all_gather(v, "dp", axis=0, tiled=True)
    full_1 = gather(pack_1)
    x_peer = swap(hidden_in)
    pack_2 = pack_shards(weight_gate_up, split, blocks - split, [], rows_packed, "pack_2")
    pack_3 = pack_shards(
        None, 0, 0, [(weight_down, units), (per_layer_gate, pd), (per_layer_proj, pd)],
        rows_packed, "pack_3",
    )
    qkv_at = split * GB
    w_qkv = full_1[:, qkv_at : qkv_at + qkv_width]
    wo_at = qkv_at + qkv_width
    w_o_t = full_1[:, wo_at : wo_at + q_width]
    lau_at = wo_at + q_width
    left = full_1[:, lau_at : lau_at + lr]
    right_t = full_1[:, lau_at + lr : lau_at + 2 * lr]
    ple_column = units // (2 * pd)

    two = jnp.asarray(2.0, BF16)
    qkv_in = adapter_qkv_in[a]
    raw_out = adapter_qkv_out[a].reshape(RANK, qkv_width) * two
    column = jnp.arange(qkv_width)
    member = (column >= q_width).astype(jnp.int32) + (column >= q_width + HD).astype(jnp.int32)
    pick = (jnp.arange(3)[:, None] == member[None, :]).astype(BF16)
    b_qkv = (pick[:, None, :] * raw_out[None]).reshape(3 * RANK, qkv_width)
    a_o = adapter_attn_in[a]
    b_o = adapter_attn_out[a] * two
    a_ffn = adapter_ffn_in[a]
    b_ffn = adapter_ffn_out[a] * two
    b_unit = jnp.swapaxes(b_ffn.reshape(RANK, 2, blocks, UB), 1, 2)
    side = (jnp.arange(2)[:, None] == jnp.arange(2)[None, :]).astype(BF16)
    bgu = (side[:, None, None, :, None] * b_unit[None]).reshape(2 * RANK, 2 * units)
    ad_t = adapter_down_in[a].T
    b_d = adapter_down_out[a] * two

    cos, sin = rope_tables(length)
    x_float = hidden_in.astype(F32)
    x_norm = normed(x_float, norm_gains[0])
    h_own = x_norm.astype(BF16)
    x_all = in_order(hidden_in, x_peer)
    h_all = normed(x_all.astype(F32), norm_gains[0]).astype(BF16)
    u_qkv = dot(h_all, qkv_in).astype(BF16)
    ids = lax.all_gather(jnp.full((16, 128), a, BF16), "dp", axis=0, tiled=False)[:, 0, 0]
    ids = ids.astype(jnp.int32)
    pack_2, _, h_all, u_qkv, bgu, ids = lax.optimization_barrier(
        (pack_2, full_1, h_all, u_qkv, bgu, ids)
    )
    full_2 = gather(pack_2)
    raw = dot(h_all, w_qkv) + dot(u_qkv, b_qkv)
    q_raw = raw[:, :q_width].reshape(length, per_group, HD)
    k_raw = raw[:, q_width : q_width + HD]
    queries = rotate(normed(q_raw, head_gains[0]), cos[:, None], sin[:, None]).astype(BF16)
    keys = rotate(normed(k_raw, head_gains[1]), cos, sin).astype(BF16)
    values = raw[:, q_width + HD :].astype(BF16)
    index = jnp.arange(length) // BLK
    distance = index[:, None] - index[None, :]
    allowed = ((distance >= 0) & (distance < WIN // BLK))[None]
    scores = jnp.einsum("lqd,md->qlm", queries, keys, preferred_element_type=F32) * HD ** (-0.5)
    scores = jnp.where(allowed, scores, NEG_BIG)
    shifted = jnp.exp(scores - jnp.max(scores, axis=-1, keepdims=True))
    probs = (shifted / jnp.sum(shifted, axis=-1, keepdims=True)).astype(BF16)
    context = (
        jnp.einsum("qlm,md->lqd", probs, values, preferred_element_type=F32)
        .reshape(length, q_width)
        .astype(BF16)
    )
    queries = queries.reshape(length, q_width)
    u_attn_f = dot(context, a_o)
    u_attn = u_attn_f.astype(BF16)
    attn_part = dot_nt(context, w_o_t) + dot(u_attn, b_o)
    attn_recv = swap(theirs(attn_part).astype(BF16))
    attn_proj = mine(attn_part) + attn_recv.astype(F32)
    laurel_low = dot(h_own, left).astype(BF16)
    laurel_wide = dot_nt(laurel_low, right_t)
    combined = (
        x_float + normed(attn_proj, norm_gains[1]) + x_norm + normed(laurel_wide, norm_gains[2])
    ) * RSQRT_TWO
    h2_own = normed(combined, norm_gains[3]).astype(BF16)

    h2_peer = swap(h2_own)
    h2 = jnp.concatenate(
        [v[s * part : (s + 1) * part] for s in range(STREAMS) for v in (h2_own, h2_peer)], axis=0
    )
    u_ffn = dot(h2, a_ffn).astype(BF16)
    u_qkv_t, qkv_in_t, a_o_t, a_ffn_t, u_ffn_t = u_qkv.T, qkv_in.T, a_o.T, a_ffn.T, u_ffn.T
    u_attn_t = u_attn.T
    pack_3, _, _ = lax.optimization_barrier((pack_3, full_2, h2_own))
    full_3 = gather(pack_3)
    partial = ffn_up(h2, full_1, split, 0, u_ffn, bgu, ad_t, None)
    ud, g_pre, u_pre, hidden = ffn_up(
        h2, full_2, blocks - split, split, u_ffn, bgu, ad_t, partial
    )
    ud_t = ud.astype(BF16).T
    (queries, keys, values, raw, context, u_qkv_t, qkv_in_t, a_o_t, a_ffn_t, u_ffn_t, b_qkv, b_o, cos, sin, u_attn_t, ud_t, hidden) = (
        lax.optimization_barrier(
            (queries, keys, values, raw, context, u_qkv_t, qkv_in_t, a_o_t, a_ffn_t, u_ffn_t, b_qkv, b_o, cos, sin, u_attn_t, ud_t, hidden)
        )
    )
    ple_parts, layer_out = [], []
    own_0, peer_0, own_1, peer_1 = ffn_down(hidden, full_3, ud, b_d, 0, 2)
    hidden, peer_0, peer_1 = lax.optimization_barrier((hidden, peer_0, peer_1))
    own_2, peer_2 = ffn_down(hidden, full_3, ud, b_d, 2, 1)
    recv_0 = swap(peer_0)
    recv_1 = swap(peer_1)
    for s, (own, recv) in enumerate(((own_0, recv_0), (own_1, recv_1), (own_2, None))):
        if s == 0:
            recv, own_2 = lax.optimization_barrier((recv, own_2))
        if s == 2:
            peer_2, _ = lax.optimization_barrier((peer_2, ple_parts[0][1]))
            recv = swap(peer_2)
        whole, d_ffn_s, d_first_s = ple_both(
            combined, own, recv, out_grad, per_layer_input, full_3, ple_column, norm_gains,
            layer_out, s,
        )
        layer_out = [whole]
        ple_parts.append([d_ffn_s, swap(d_ffn_s), d_first_s])
    packs = (full_1, full_2, full_3)
    common = (g_pre, u_pre, bgu, ad_t, b_d, u_ffn_t, a_ffn_t, h2, ud_t)
    lau_column = lau_at // (2 * lr)
    d_attn_own, d_attn_recv, branch, waiting, sums = [], [], [], [], None

    def between(branch):
        d_first_s, d_h2_own, d_h2_recv, s = waiting.pop(0)
        d_attn_s, *branch = between_bwd(
            d_first_s, combined, d_h2_own, d_h2_recv, attn_proj, laurel_low, full_1, lau_column,
            norm_gains, branch, s,
        )
        d_attn_own.append(d_attn_s)
        d_attn_recv.append(swap(d_attn_s))
        return branch

    for s in range(STREAMS):
        own, recv, first = ple_parts[s]
        if s >= 2:
            own, _ = lax.optimization_barrier((own, d_attn_own[s - 2]))
        elif s == 1:
            own, _ = lax.optimization_barrier((own, d_h2_peer))
        *sums, d_h2_own, d_h2_peer = ffn_bwd(
            own, recv, packs, split, *common, s, sums, BF16 if s == STREAMS - 1 else F32
        )
        send_ffn = sums[0]
        if waiting:
            first_w, own_w, recv_w, s_w = waiting[0]
            if s == STREAMS - 1:
                send_ffn, recv_w = lax.optimization_barrier((send_ffn, recv_w))
            else:
                recv_w, _ = lax.optimization_barrier((recv_w, d_h2_peer))
            waiting[0] = (first_w, own_w, recv_w, s_w)
            waiting.append((first, d_h2_own, swap(d_h2_peer), s))
            branch = between(branch)
        else:
            waiting.append((first, d_h2_own, swap(d_h2_peer), s))
    send_ffn, d_attn_recv[0] = lax.optimization_barrier((send_ffn, d_attn_recv[0]))
    got_ffn = lax.all_gather(send_ffn, "dp", axis=0, tiled=False)
    d_branch, d_norm = between(branch)

    pieces = d_attn_own + d_attn_recv
    d_h_peer_0, d_h_peer_1, d_raw, d_u, send_heads, grad_attn_out = attention_bwd(
        pieces, t.astype(jnp.int32).reshape(1), full_1, qkv_at, wo_at // HD, b_o, a_o_t, queries, keys,
        values, probs, raw, head_gains, cos, sin, context, u_qkv_t, b_qkv, qkv_in_t,
        u_attn_t,
    )
    d_h_recv_0 = swap(d_h_peer_0)
    d_raw, d_u, got_ffn = lax.optimization_barrier((d_raw, d_u, got_ffn))
    got_heads = lax.all_gather(send_heads, "dp", axis=0, tiled=False)
    send = jnp.concatenate(
        [sums[1], grad_attn_out, dot_tn(d_u, h_all).astype(BF16)], axis=0
    ).T
    send, d_h_peer_1 = lax.optimization_barrier((send, d_h_peer_1))
    d_h_recv_1 = swap(d_h_peer_1)
    got = lax.all_to_all(send, ("dp", "tensor"), 0, 0, tiled=True).reshape(2 * dp, -1, send.shape[1])
    out_ffn_out, out_down_in = ffn_adapter_sums(got_ffn, ids, adapters, units)
    d_h_own = dot_nt(mine(d_raw), w_qkv) + dot_nt(mine(d_u), qkv_in)
    got, out_ffn_out, out_down_in, d_h_own = lax.optimization_barrier(
        (got, out_ffn_out, out_down_in, d_h_own)
    )
    out_ffn_in, out_down_out, out_attn_out, out_qkv_in = shared_sums(got, ids, adapters)
    d_h_own, out_qkv_in = lax.optimization_barrier((d_h_own, out_qkv_in))
    final_args = (hidden_in, d_norm, d_branch, d_h_own)
    input_grad = final_bwd(*final_args, d_h_recv_0, norm_gains, [], 0)
    input_grad = final_bwd(*final_args, d_h_recv_1, norm_gains, [input_grad], 1)
    got_heads, input_grad = lax.optimization_barrier((got_heads, input_grad))
    out_qkv_out, out_attn_in = head_sums(got_heads, ids, adapters, qkv_width)
    return (
        layer_out[0],
        input_grad,
        jnp.swapaxes(out_qkv_in, 1, 2),
        out_qkv_out,
        jnp.swapaxes(out_attn_in, 1, 2),
        out_attn_out,
        jnp.swapaxes(out_ffn_in, 1, 2),
        out_ffn_out,
        jnp.swapaxes(out_down_in, 1, 2),
        out_down_out,
    )


def solution(mesh):
    in_specs = (
        P(("dp", "tensor"), None),
        P(("dp", "tensor"), None),
        P(("dp", "tensor"), None),
        P("dp"),
        P("dp", "tensor", None),
        P("tensor", "dp"),
        P("dp", None, "tensor"),
        P("tensor", "dp"),
        P("dp", None),
        P(None, "dp"),
        P("dp", None),
        P(None, "dp"),
        P(),
        P(),
        P(),
        P(None, None, "tensor", None),
        P(None, "tensor", None),
        P(),
        P(),
        P(None, None, None, "tensor"),
        P(None, "tensor", None),
        P(),
    )
    out_specs = (
        P(("dp", "tensor"), None),
        P(("dp", "tensor"), None),
        P(None, ("dp", "tensor"), None),
        P(None, None, "tensor", None),
        P(None, "tensor", None),
        P(None, None, ("dp", "tensor")),
        P(None, ("dp", "tensor"), None),
        P(None, None, None, "tensor"),
        P(None, "tensor", None),
        P(None, None, ("dp", "tensor")),
    )
    return jax.shard_map(
        on_device, mesh=mesh, in_specs=in_specs, out_specs=out_specs, check_vma=False
    )
```
